32 devices in a mesh: seq: 8 (over z, x), chan: 4 (over y, core).
Axes of the slice: x: 2, y: 2, z: 4, core: 2. Of those that a mesh axis runs over, the one named last changes fastest.
Arguments:
- query: bfloat16 [2048, 4096], P('seq', 'chan'), may hold values from -6 to 6
- key_gate: bfloat16 [2048, 4096], P('seq', 'chan'), may hold values from -6 to 6
- value: bfloat16 [2048, 4096], P('seq', 'chan'), may hold values from -6 to 6
- group_order: int32 [16], replicated, may hold values from 0 to 15, each once
- emb_weight: float32 [33, 64], replicated, may hold values from -32 to 32
- emb_bias: float32 [64], replicated, may hold values from -1 to 1
- mid_weight: float32 [64, 64], replicated, may hold values from -0.75 to 0.75
- mid_bias: float32 [64], replicated, may hold values from -1 to 1
- out_filter: float32 [64, 4096], P(None, 'chan'), may hold values from -0.75 to 0.75
- decay_rate: float32 [4096], P('chan'), may hold values from 0.00014648438 to 0.0014648438
- skip_gain: float32 [4096], P('chan'), may hold values from 0.5 to 1.5
- out_weight: bfloat16 [4096, 4096], P('chan'), may hold values from -0.125 to 0.125
Outputs:
- projected: float32 [4096, 2048], P('chan', 'seq')
The draws below stay inside these ranges and needn't reach their ends.
Inputs may be any that keep to these rules, and one draw needn't show every extreme that they name: `group_order`: a permutation of the group numbers.
All inputs are finite; a program needn't handle non-finite values.
Results may differ from the reference program's by a relative error of at most 0.011.
Values may be sent and summed in bfloat16 or wider, within the bound.
No kernel may reach another device: no remote copies, remote signals or barrier semaphores. Data moves between devices by JAX's collectives and lax.ppermute only.
A program may use at most 128 MiB of HBM per device.

```python
import math
import jax
import jax.numpy as jnp
from jax import lax

C = 4096
ORDER = 64
EMB = 33
BLOCK = 128
LEN = 2048
NCHUNK = 16


def raised(drawn, own_key, source, target, shards_of, factor):
    owner, partner = [(jnp.arange(drawn.shape[position]) // (drawn.shape[position] // shards_of)).reshape([-1 if axis == position else 1 for axis in range(drawn.ndim)]) for position in (source, target)]
    chosen = jax.random.permutation(own_key, shards_of)[partner]
    strong = (owner == chosen) | (owner == (partner + shards_of // 2) % shards_of)
    return jnp.where(strong, factor * drawn, drawn)


def shard_levels(own_key, shape, shards, least, top_value):
    gain, own = 1.0, jax.random.fold_in(own_key, 6)
    for dim, blocks in shards:
        heights = jnp.exp(jax.random.uniform(jax.random.fold_in(own, dim), (blocks,), jnp.float32, least / len(shards), top_value / len(shards)))
        gain = gain * jnp.repeat(heights, shape[dim] // blocks).reshape([-1 if axis == dim else 1 for axis in range(len(shape))])
    return gain


def bell_draw(key, dims, scale, bound, pieces=(), held_as=jnp.bfloat16):
    level = shard_levels(key, dims, pieces, -0.22, 0.18) if pieces else 1.0
    entries = jax.random.normal(key, dims, jnp.float32) * scale * level
    return jnp.minimum(jnp.maximum(entries, -bound), bound).astype(held_as)


def noise_with(key, shape, spread, reach, pieces, heavy, kind=jnp.bfloat16):
    drawn = spread * jax.random.normal(key, shape, jnp.float32)
    if pieces:
        drawn = drawn * shard_levels(key, shape, pieces, -0.22, 0.18)
    return jnp.clip(raised(drawn, jax.random.fold_in(key, 3), *heavy), -reach, reach).astype(kind)


def setup_inputs(seed: int = 0) -> dict:
    key_of = jax.random.split(jax.random.key(seed), 13)
    query = bell_draw(key_of[0], (LEN, C), 1.0, 6.0, ((0, 8), (1, 4)))
    key_gate = bell_draw(key_of[1], (LEN, C), 1.0, 6.0, ((0, 8), (1, 4)))
    value = bell_draw(key_of[2], (LEN, C), 1.0, 6.0, ((0, 8), (1, 4)))
    group_order = jax.random.permutation(key_of[3], NCHUNK).astype(jnp.int32)
    emb_weight = jnp.clip(jax.random.uniform(key_of[4], (EMB, ORDER), jnp.float32, -32.0, 32.0), -32.0, 32.0)
    emb_bias = jnp.clip(jax.random.uniform(key_of[5], (ORDER,), jnp.float32, -1.0, 1.0), -1.0, 1.0)
    mid_weight = bell_draw(key_of[6], (ORDER, ORDER), ORDER ** -0.5, 0.75, (), jnp.float32)
    mid_bias = jnp.clip(jax.random.uniform(key_of[7], (ORDER,), jnp.float32, -1.0, 1.0), -1.0, 1.0)
    out_filter = bell_draw(key_of[8], (ORDER, C), ORDER ** -0.5, 0.75, ((1, 4),), jnp.float32)
    decay_rate = jnp.clip(jnp.exp(math.log(0.0014648438) - 2.3025851 * jax.random.uniform(key_of[9], (C,), jnp.float32) ** shard_levels(key_of[9], (C,), ((0, 4),), -0.2, 0.2)), 0.00014648438, 0.0014648438)
    skip_gain = jnp.clip(0.5 + 1.0 * jax.random.uniform(key_of[10], (C,), jnp.float32) ** shard_levels(key_of[10], (C,), ((0, 4),), -0.2, 0.2), 0.5, 1.5)
    out_weight = noise_with(key_of[11], (C, C), C ** -0.5, 0.125, ((0, 4),), (0, 1, 4, 2.0))
    return dict(query=query, key_gate=key_gate, value=value, group_order=group_order, emb_weight=emb_weight, emb_bias=emb_bias, mid_weight=mid_weight, mid_bias=mid_bias, out_filter=out_filter, decay_rate=decay_rate, skip_gain=skip_gain, out_weight=out_weight)


sine_freq = 2.0

def transform_tables(block):
    period = 2 * block
    row_index = jnp.arange(block, dtype=jnp.int32)
    freq_index = jnp.arange(block + 1, dtype=jnp.int32)
    scale = math.pi / block
    angle_head = (freq_index[:, None] * row_index[None, :] % period).astype(jnp.float32) * scale
    fwd_head = jnp.concatenate([jnp.cos(angle_head), -jnp.sin(angle_head)], 0).astype(jnp.bfloat16)
    angle_tail = (freq_index[:, None] * (row_index[None, :] + block) % period).astype(jnp.float32) * scale
    keep_cols = (row_index > 0).astype(jnp.float32)[None, :]
    fwd_tail = (jnp.concatenate([jnp.cos(angle_tail), -jnp.sin(angle_tail)], 0) * keep_cols).astype(jnp.bfloat16)
    weights = jnp.where((freq_index == 0) | (freq_index == block), 1.0, 2.0).astype(jnp.float32) / period
    angle_back = (row_index[:, None] * freq_index[None, :] % period).astype(jnp.float32) * scale
    inverse = jnp.concatenate([jnp.cos(angle_back) * weights[None, :], -jnp.sin(angle_back) * weights[None, :]], 1).astype(jnp.bfloat16)
    return (fwd_head, fwd_tail, inverse)

def filter_rows(positions, length, emb_weight, emb_bias, mid_weight, mid_bias, out_filter, decay_rate):
    high = lax.Precision.HIGHEST
    time_float = positions.astype(jnp.float32)
    band_count = (emb_weight.shape[0] - 1) // 2
    band_index = jnp.arange(1, band_count + 1, dtype=jnp.int32)
    angles = (positions[:, None] * band_index[None, :] % length).astype(jnp.float32) * (2.0 * math.pi / length)
    embedded = jnp.concatenate([time_float[:, None] / length, jnp.cos(angles), jnp.sin(angles)], 1)
    hidden = jnp.sin(sine_freq * (jnp.dot(embedded, emb_weight, precision=high) + emb_bias[None, :]))
    hidden = jnp.sin(sine_freq * (jnp.dot(hidden, mid_weight, precision=high) + mid_bias[None, :]))
    filter_raw = jnp.dot(hidden, out_filter, precision=high)
    norm_scale = jnp.sqrt(-jnp.expm1(-2.0 * decay_rate))
    decayed = jnp.exp(-decay_rate[None, :] * time_float[:, None])
    return (filter_raw * decayed * norm_scale[None, :]).astype(jnp.bfloat16)

def reference(query, key_gate, value, group_order, emb_weight, emb_bias, mid_weight, mid_bias, out_filter, decay_rate, skip_gain, out_weight):
    fwd_head, fwd_tail, inverse = transform_tables(BLOCK)
    signal = (key_gate.astype(jnp.float32) * value.astype(jnp.float32)).astype(jnp.bfloat16)
    positions = jnp.arange(LEN, dtype=jnp.int32)
    filt = filter_rows(positions, LEN, emb_weight, emb_bias, mid_weight, mid_bias, out_filter, decay_rate)
    blocks = filt.reshape(NCHUNK, BLOCK, C).astype(jnp.float32)
    previous = jnp.concatenate([jnp.zeros((1, BLOCK, C), jnp.float32), blocks[:-1]], 0)
    head_part = jnp.einsum('kr,mrc->mkc', fwd_head.astype(jnp.float32), blocks)
    tail_part = jnp.einsum('kr,mrc->mkc', fwd_tail.astype(jnp.float32), previous)
    filter_spectrum = (head_part + tail_part).astype(jnp.bfloat16)
    sig_blocks = signal.reshape(NCHUNK, BLOCK, C).astype(jnp.float32)
    signal_spectrum = jnp.einsum('kr,mrc->mkc', fwd_head.astype(jnp.float32), sig_blocks).astype(jnp.bfloat16)
    half_rows = BLOCK + 1
    sig_real = signal_spectrum[:, :half_rows].astype(jnp.float32)
    sig_imag = signal_spectrum[:, half_rows:].astype(jnp.float32)

    def output_group(global_id):
        lag_index = global_id - group_order
        causal = (lag_index >= 0).astype(jnp.float32)[:, None, None]
        picked = filter_spectrum[jnp.maximum(lag_index, 0)]
        filt_real = picked[:, :half_rows].astype(jnp.float32)
        filt_imag = picked[:, half_rows:].astype(jnp.float32)
        real_part = lax.optimization_barrier(jnp.sum(causal * (filt_real * sig_real - filt_imag * sig_imag), 0))
        imag_part = lax.optimization_barrier(jnp.sum(causal * (filt_real * sig_imag + filt_imag * sig_real), 0))
        spectrum = jnp.concatenate([real_part, imag_part], 0).astype(jnp.bfloat16)
        return jnp.dot(inverse, spectrum, preferred_element_type=jnp.float32)
    convolved = lax.map(output_group, group_order).reshape(LEN, C)
    mixed = (query.astype(jnp.float32) * (convolved + skip_gain[None, :] * signal.astype(jnp.float32))).astype(jnp.bfloat16)
    result = jnp.dot(mixed.astype(jnp.float32), out_weight.astype(jnp.float32))
    return result.T
```

```python
import functools
import math

import jax
import jax.numpy as jnp
import numpy as np
from jax import lax
from jax.experimental import pallas as pl
from jax.experimental.pallas import tpu as pltpu
from jax.sharding import PartitionSpec as P

GROUP = 128
LANES = 128
SINE_FREQ = 2.0
F32 = jnp.float32
BF16 = jnp.bfloat16


def packed_tables(block):
    period = 2 * block
    row = np.arange(block)
    freq = np.arange(block)

    def forward(shift):
        angle = 2.0 * np.pi * (freq[:, None] * (row[None, :] + shift) % period) / period
        real, imag = np.cos(angle), -np.sin(angle)
        imag[0] = np.where((row + shift) % 2 == 0, 1.0, -1.0)
        return np.concatenate([real, imag], 0)

    head, tail = forward(0), forward(block)
    tail[:, 0] = 0.0
    weight = np.where(freq == 0, 1.0, 2.0) / period
    angle = 2.0 * np.pi * (row[:, None] * freq[None, :] % period) / period
    real, imag = np.cos(angle) * weight, -np.sin(angle) * weight
    imag[:, 0] = np.where(row % 2 == 0, 1.0, -1.0) / period
    inverse = np.concatenate([real, imag], 1)
    to_bf16 = lambda table: jnp.asarray(table.astype(np.float32)).astype(BF16)
    return to_bf16(head), to_bf16(np.concatenate([head, tail], 1)), to_bf16(inverse)


def feature_table(length, bands, rows):
    lag = np.arange(length)
    angle = 2.0 * np.pi * (np.arange(1, bands + 1)[:, None] * lag[None, :] % length) / length
    table = np.zeros((rows, length), np.float32)
    table[0] = lag / length
    table[1 : bands + 1] = np.cos(angle)
    table[bands + 1 : 2 * bands + 1] = np.sin(angle)
    table[2 * bands + 1] = 1.0
    return jnp.asarray(table)


def gated_kernel(key_ref, value_ref, out_ref):
    width = out_ref.shape[2]
    for j in range(out_ref.shape[0]):
        cols = slice(j * width, (j + 1) * width)
        out_ref[j] = (key_ref[:, cols].astype(F32) * value_ref[:, cols].astype(F32)).astype(BF16)


def contract_first(lhs, rhs):
    return lax.dot_general(
        lhs, rhs, (((0,), (0,)), ((), ())), precision=lax.Precision.HIGHEST, preferred_element_type=F32
    )


def filter_kernel(
    block, index_ref, feat_ref, emb_w_ref, emb_b_ref, mid_w_ref, mid_b_ref, out_w_ref, decay_ref, norm_ref, table_ref,
    real_ref, imag_ref, edge_ref, w1, w2, hid, filt,
):
    emb, order = emb_w_ref.shape
    length = feat_ref.shape[1]
    blocks = length // block
    w1[...] = jnp.zeros_like(w1)
    w1[0:emb, :] = emb_w_ref[...]
    w1[emb : emb + 1, :] = emb_b_ref[...]
    w2[...] = jnp.zeros_like(w2)
    w2[0:order, :] = mid_w_ref[...]
    w2[order : order + 1, :] = mid_b_ref[...]
    hid[order:, :] = jnp.ones_like(hid[order:, :])
    hid[0:order, :] = jnp.sin(SINE_FREQ * contract_first(w1[...], feat_ref[...]))
    hidden = jnp.sin(SINE_FREQ * contract_first(w2[...], hid[...]))
    raw = contract_first(hidden, out_w_ref[...])
    decay = decay_ref[...]
    within = jnp.exp(-decay * lax.broadcasted_iota(jnp.int32, (block, LANES), 0).astype(F32))
    within = within * norm_ref[...]
    filt[0:block, :] = jnp.zeros((block, LANES), BF16)
    for m in range(blocks):
        start = jnp.exp(-decay * float(m * block))
        filt[(m + 1) * block : (m + 2) * block, :] = (raw[m * block : (m + 1) * block] * (within * start)).astype(BF16)
    first_row = lax.broadcasted_iota(jnp.int32, (16, LANES), 0) == 0
    group = 2
    for m0 in range(0, blocks, group):
        stacked = jnp.concatenate(
            [
                jnp.concatenate(
                    [filt[(m + 1) * block : (m + 2) * block, :], filt[m * block : (m + 1) * block, :]], 0
                )
                for m in range(m0, m0 + group)
            ],
            1,
        )
        spectrum = jnp.dot(table_ref[...], stacked, preferred_element_type=F32)
        for i in range(group):
            m = m0 + i
            real = spectrum[:block, i * LANES : (i + 1) * LANES]
            imag = spectrum[block:, i * LANES : (i + 1) * LANES]
            real_ref[m] = real
            imag_ref[m] = imag
            edge_ref[m] = jnp.where(first_row, imag[:16], real[:16])
            imag_ref[m, 0:16, :] = jnp.where(first_row, 0.0, imag[:16])


def conv_kernel(
    block, order_ref, x_ref, real_ref, imag_ref, edge_ref, head_ref, inverse_ref, out_ref, sig, sre, sim, spec, conv
):
    slots = x_ref.shape[0]
    length = slots * GROUP
    blocks = length // block
    for p in range(slots):
        start = pl.multiple_of(order_ref[p] * GROUP, GROUP)
        sig[pl.ds(start, GROUP), :] = x_ref[p]
    group = 2
    for b0 in range(0, blocks, group):
        stacked = jnp.concatenate([sig[b * block : (b + 1) * block, :] for b in range(b0, b0 + group)], 1)
        spectrum = jnp.dot(head_ref[...], stacked, preferred_element_type=F32)
        for i in range(group):
            sre[b0 + i] = spectrum[:block, i * LANES : (i + 1) * LANES]
            sim[b0 + i] = spectrum[block:, i * LANES : (i + 1) * LANES]

    def tile(start, first):
        rows = pl.ds(start, 16)
        mirror = pl.ds(block + start, 16)
        s_real = [sre[q, rows, :] for q in range(blocks)]
        s_imag = [sim[q, rows, :] for q in range(blocks)]
        for g in range(blocks):
            acc_real = acc_imag = None
            for q in range(g + 1):
                fr, fi = real_ref[g - q, rows, :], imag_ref[g - q, rows, :]
                fe = edge_ref[g - q] if first else fr
                re = fr * s_real[q] - fi * s_imag[q]
                im = fe * s_imag[q] + fi * s_real[q]
                acc_real = re if q == 0 else acc_real + re
                acc_imag = im if q == 0 else acc_imag + im
            spec[rows, g * LANES : (g + 1) * LANES] = acc_real.astype(BF16)
            spec[mirror, g * LANES : (g + 1) * LANES] = acc_imag.astype(BF16)

    tile(0, True)

    @pl.loop(1, block // 16)
    def _(t):
        tile(pl.multiple_of(t * 16, 16), False)

    result = jnp.dot(inverse_ref[...], spec[...], preferred_element_type=F32)
    for g in range(blocks):
        conv[g * block : (g + 1) * block, :] = result[:, g * LANES : (g + 1) * LANES].astype(BF16)
    for p in range(slots):
        start = pl.multiple_of(order_ref[p] * GROUP, GROUP)
        out_ref[p] = conv[pl.ds(start, GROUP), :]


def mixed_kernel(query_ref, conv_ref, sig_ref, gain_ref, out_ref):
    width = conv_ref.shape[2]
    for j in range(conv_ref.shape[0]):
        cols = slice(j * width, (j + 1) * width)
        inner = conv_ref[j].astype(F32) + gain_ref[:, cols] * sig_ref[j].astype(F32)
        out_ref[:, cols] = (query_ref[:, cols].astype(F32) * inner).astype(BF16)


def project_kernel(index_ref, mixed_ref, weight_ref, out_ref):
    out_ref[0] = jnp.dot(mixed_ref[...], weight_ref[...], preferred_element_type=F32).astype(BF16)


def project(owners, mixed, out_weight, width):
    rows, depth = mixed.shape
    tile = min(width, 512)
    count = owners.shape[0]
    return pl.pallas_call(
        project_kernel,
        out_shape=jax.ShapeDtypeStruct((count, rows, width), BF16),
        grid_spec=pltpu.PrefetchScalarGridSpec(
            num_scalar_prefetch=1,
            grid=(count, width // tile),
            in_specs=[
                pl.BlockSpec((rows, depth), lambda j, t, o: (0, 0)),
                pl.BlockSpec((depth, tile), lambda j, t, o: (0, o[j] * (width // tile) + t)),
            ],
            out_specs=pl.BlockSpec((1, rows, tile), lambda j, t, o: (j, 0, t)),
        ),
    )(owners, mixed, out_weight)


def local(
    query, key_gate, value, group_order, emb_weight, emb_bias, mid_weight, mid_bias, out_filter, decay_rate, skip_gain,
    out_weight,
):
    rows, chan_width = query.shape
    seq_count, chan_count = lax.axis_size("seq"), lax.axis_size("chan")
    seq_index, chan_index = lax.axis_index("seq"), lax.axis_index("chan")
    length = rows * seq_count
    slots = length // GROUP
    width = chan_width // seq_count
    block = max(GROUP, length // 16)
    blocks = length // block
    emb, order = emb_weight.shape
    head, head_tail, inverse = packed_tables(block)
    feat_rows = -(-(emb + 1) // 8) * 8
    features = feature_table(length, (emb - 1) // 2, feat_rows)
    vmem = pltpu.CompilerParams(vmem_limit_bytes=48 << 20)

    signal = pl.pallas_call(
        gated_kernel,
        out_shape=jax.ShapeDtypeStruct((seq_count, rows, width), BF16),
    )(key_gate, value)
    spread = lax.all_to_all(signal, "seq", 0, 0, tiled=True).reshape(slots, GROUP, width)

    my_filter = lax.dynamic_slice_in_dim(out_filter, seq_index * width, width, 1)
    my_decay = lax.dynamic_slice_in_dim(decay_rate, seq_index * width, width)[None, :]
    norm = jnp.sqrt(-jnp.expm1(-2.0 * my_decay))
    pad = [(0, 0), (0, LANES - width)]
    if width < LANES:
        my_filter, my_decay, norm = jnp.pad(my_filter, pad), jnp.pad(my_decay, pad), jnp.pad(norm, pad)
        spread = jnp.pad(spread, [(0, 0)] + pad)
    real, imag, edge = pl.pallas_call(
        functools.partial(filter_kernel, block, None),
        out_shape=(
            jax.ShapeDtypeStruct((blocks, block, LANES), F32),
            jax.ShapeDtypeStruct((blocks, block, LANES), F32),
            jax.ShapeDtypeStruct((blocks, 16, LANES), F32),
        ),
        scratch_shapes=[
            pltpu.VMEM((feat_rows, order), F32),
            pltpu.VMEM((order + 8, order), F32),
            pltpu.VMEM((order + 8, length), F32),
            pltpu.VMEM((length + block, LANES), BF16),
        ],
        compiler_params=vmem,
    )(features, emb_weight, emb_bias[None, :], mid_weight, mid_bias[None, :], my_filter, my_decay, norm, head_tail)

    convolved = pl.pallas_call(
        functools.partial(conv_kernel, block),
        out_shape=jax.ShapeDtypeStruct((slots, GROUP, LANES), BF16),
        in_specs=[pl.BlockSpec(memory_space=pltpu.SMEM)] + [pl.BlockSpec(memory_space=pltpu.VMEM)] * 6,
        scratch_shapes=[
            pltpu.VMEM((length, LANES), BF16),
            pltpu.VMEM((blocks, block, LANES), F32),
            pltpu.VMEM((blocks, block, LANES), F32),
            pltpu.VMEM((2 * block, blocks * LANES), BF16),
            pltpu.VMEM((length, LANES), BF16),
        ],
        compiler_params=vmem,
    )(group_order, spread, real, imag, edge, head, inverse)
    if width < LANES:
        convolved = convolved[:, :, :width]
    back = lax.all_to_all(convolved.reshape(seq_count, rows, width), "seq", 0, 0, tiled=True)

    mixed = pl.pallas_call(
        mixed_kernel,
        out_shape=jax.ShapeDtypeStruct((rows, chan_width), BF16),
        compiler_params=vmem,
    )(query, back, signal, skip_gain[None, :])

    out_width = out_weight.shape[1] // chan_count
    half = chan_count // 2
    odd = chan_index ^ jnp.arange(1, chan_count, 2, dtype=jnp.int32)
    even = chan_index ^ jnp.arange(0, chan_count, 2, dtype=jnp.int32)
    away = project(odd, mixed, out_weight, out_width)
    terms = lax.ppermute(away, "chan", [(i, i ^ 1) for i in range(chan_count)])
    kept = project(even, mixed, out_weight, out_width)
    bit = 2
    total = kept.astype(F32) + terms.astype(F32)
    while bit < chan_count:
        send, keep = total[1::2].astype(BF16), total[0::2]
        total = keep + lax.ppermute(send, "chan", [(i, i ^ bit) for i in range(chan_count)]).astype(F32)
        bit *= 2
    return total[0].T


def solution(mesh):
    return jax.shard_map(
        local,
        mesh=mesh,
        in_specs=(
            P("seq", "chan"), P("seq", "chan"), P("seq", "chan"), P(), P(), P(), P(), P(), P(None, "chan"), P("chan"),
            P("chan"), P("chan", None),
        ),
        out_specs=P("chan", "seq"),
        check_vma=False,
    )
```

```python
import functools
import math

import jax
import jax.numpy as jnp
import numpy as np
from jax import lax
from jax.experimental import pallas as pl
from jax.experimental.pallas import tpu as pltpu
from jax.sharding import PartitionSpec as P

GROUP = 128
LANES = 128
SINE_FREQ = 2.0
F32 = jnp.float32
BF16 = jnp.bfloat16


def packed_tables(block):
    period = 2 * block
    row = np.arange(block)
    freq = np.arange(block)

    def forward(shift):
        angle = 2.0 * np.pi * (freq[:, None] * (row[None, :] + shift) % period) / period
        real, imag = np.cos(angle), -np.sin(angle)
        imag[0] = np.where((row + shift) % 2 == 0, 1.0, -1.0)
        return np.concatenate([real, imag], 0)

    head, tail = forward(0), forward(block)
    tail[:, 0] = 0.0
    weight = np.where(freq == 0, 1.0, 2.0) / period
    angle = 2.0 * np.pi * (row[:, None] * freq[None, :] % period) / period
    real, imag = np.cos(angle) * weight, -np.sin(angle) * weight
    imag[:, 0] = np.where(row % 2 == 0, 1.0, -1.0) / period
    inverse = np.concatenate([real, imag], 1)
    to_bf16 = lambda table: jnp.asarray(table.astype(np.float32)).astype(BF16)
    return to_bf16(head), to_bf16(np.concatenate([head, tail], 1)), to_bf16(inverse)


def feature_table(length, bands, rows):
    lag = np.arange(length)
    angle = 2.0 * np.pi * (np.arange(1, bands + 1)[:, None] * lag[None, :] % length) / length
    table = np.zeros((rows, length), np.float32)
    table[0] = lag / length
    table[1 : bands + 1] = np.cos(angle)
    table[bands + 1 : 2 * bands + 1] = np.sin(angle)
    table[2 * bands + 1] = 1.0
    return jnp.asarray(table)


def contract_first(lhs, rhs):
    return lax.dot_general(
        lhs, rhs, (((0,), (0,)), ((), ())), precision=lax.Precision.HIGHEST, preferred_element_type=F32
    )


def filter_kernel(
    block, out_w_ref, decay_ref, norm_ref, feat_hbm, emb_w_hbm, emb_b_hbm, mid_w_hbm, mid_b_hbm, table_hbm,
    head_hbm, inverse_hbm, real_ref, imag_ref, edge_ref, head_ref, inverse_ref, feat_ref, emb_w_ref, emb_b_ref, mid_w_ref, mid_b_ref, table_ref, w1, w2, hid, filt, sem,
):
    sources = (feat_hbm, emb_w_hbm, emb_b_hbm, mid_w_hbm, mid_b_hbm, table_hbm, head_hbm, inverse_hbm)
    targets = (feat_ref, emb_w_ref, emb_b_ref, mid_w_ref, mid_b_ref, table_ref, head_ref, inverse_ref)
    copies = [pltpu.make_async_copy(s, t, sem.at[i]) for i, (s, t) in enumerate(zip(sources, targets))]
    for copy in copies:
        copy.start()
    for copy in copies:
        copy.wait()
    emb, order = emb_w_ref.shape
    length = feat_ref.shape[1]
    blocks = length // block
    w1[...] = jnp.zeros_like(w1)
    w1[0:emb, :] = emb_w_ref[...]
    w1[emb : emb + 1, :] = emb_b_ref[...]
    w2[...] = jnp.zeros_like(w2)
    w2[0:order, :] = mid_w_ref[...]
    w2[order : order + 1, :] = mid_b_ref[...]
    hid[order:, :] = jnp.ones_like(hid[order:, :])
    hid[0:order, :] = jnp.sin(SINE_FREQ * contract_first(w1[...], feat_ref[...]))
    hidden = jnp.sin(SINE_FREQ * contract_first(w2[...], hid[...]))
    raw = contract_first(hidden, out_w_ref[...])
    decay = decay_ref[...]
    within = jnp.exp(-decay * lax.broadcasted_iota(jnp.int32, (block, LANES), 0).astype(F32))
    within = within * norm_ref[...]
    filt[0:block, :] = jnp.zeros((block, LANES), BF16)
    for m in range(blocks):
        start = jnp.exp(-decay * float(m * block))
        filt[(m + 1) * block : (m + 2) * block, :] = (raw[m * block : (m + 1) * block] * (within * start)).astype(BF16)
    first_row = lax.broadcasted_iota(jnp.int32, (16, LANES), 0) == 0
    group = 2
    for m0 in range(0, blocks, group):
        stacked = jnp.concatenate(
            [
                jnp.concatenate(
                    [filt[(m + 1) * block : (m + 2) * block, :], filt[m * block : (m + 1) * block, :]], 0
                )
                for m in range(m0, m0 + group)
            ],
            1,
        )
        spectrum = jnp.dot(table_ref[...], stacked, preferred_element_type=F32)
        for i in range(group):
            m = m0 + i
            real = spectrum[:block, i * LANES : (i + 1) * LANES]
            imag = spectrum[block:, i * LANES : (i + 1) * LANES]
            real_ref[m] = real
            imag_ref[m] = imag
            edge_ref[m] = jnp.where(first_row, imag[:16], real[:16])
            imag_ref[m, 0:16, :] = jnp.where(first_row, 0.0, imag[:16])


def conv_kernel(
    block, order_ref, index_ref, x_ref, real_ref, imag_ref, edge_ref, table_ref, inverse_ref, weight_hbm, query_hbm,
    signal_hbm, out_ref, weight_out, query_out, signal_out, sig, sre, sim, spec, conv, weight_sem, sem,
):
    owners, _, width = weight_out.shape
    copies = [
        pltpu.make_async_copy(query_hbm, query_out, sem.at[0]),
        pltpu.make_async_copy(signal_hbm, signal_out, sem.at[1]),
    ]
    for j in range(owners):
        cols = pl.ds(pl.multiple_of((index_ref[0] ^ j) * width, LANES), width)
        copies.append(pltpu.make_async_copy(weight_hbm.at[:, cols], weight_out.at[j], weight_sem.at[j]))
    for copy in copies:
        copy.start()
    slots = x_ref.shape[0]
    length = slots * GROUP
    blocks = length // block
    for p in range(slots):
        start = pl.multiple_of(order_ref[p] * GROUP, GROUP)
        sig[pl.ds(start, GROUP), :] = x_ref[p]
    group = 2
    for b0 in range(0, blocks, group):
        stacked = jnp.concatenate([sig[b * block : (b + 1) * block, :] for b in range(b0, b0 + group)], 1)
        spectrum = jnp.dot(table_ref[...], stacked, preferred_element_type=F32)
        for i in range(group):
            sre[b0 + i] = spectrum[:block, i * LANES : (i + 1) * LANES]
            sim[b0 + i] = spectrum[block:, i * LANES : (i + 1) * LANES]

    def tile(start, first):
        rows = pl.ds(start, 16)
        mirror = pl.ds(block + start, 16)
        s_real = [sre[q, rows, :] for q in range(blocks)]
        s_imag = [sim[q, rows, :] for q in range(blocks)]
        for g in range(blocks):
            acc_real = acc_imag = None
            for q in range(g + 1):
                fr, fi = real_ref[g - q, rows, :], imag_ref[g - q, rows, :]
                fe = edge_ref[g - q] if first else fr
                re = fr * s_real[q] - fi * s_imag[q]
                im = fe * s_imag[q] + fi * s_real[q]
                acc_real = re if q == 0 else acc_real + re
                acc_imag = im if q == 0 else acc_imag + im
            spec[rows, g * LANES : (g + 1) * LANES] = acc_real.astype(BF16)
            spec[mirror, g * LANES : (g + 1) * LANES] = acc_imag.astype(BF16)

    tile(0, True)

    @pl.loop(1, block // 16)
    def _(t):
        tile(pl.multiple_of(t * 16, 16), False)

    result = jnp.dot(inverse_ref[...], spec[...], preferred_element_type=F32)
    for g in range(blocks):
        conv[g * block : (g + 1) * block, :] = result[:, g * LANES : (g + 1) * LANES].astype(BF16)
    for p in range(slots):
        start = pl.multiple_of(order_ref[p] * GROUP, GROUP)
        out_ref[p] = conv[pl.ds(start, GROUP), :]
    for copy in copies:
        copy.wait()


def mix_kernel(first, step, back_ref, sig_ref, query_ref, gain_ref, weight_ref, out_ref, mixed_ref):
    count, _, width = back_ref.shape
    for j in range(count):
        cols = slice(j * width, (j + 1) * width)
        inner = back_ref[j].astype(F32) + gain_ref[:, cols] * sig_ref[j].astype(F32)
        mixed_ref[:, cols] = (query_ref[:, cols].astype(F32) * inner).astype(BF16)
    project_kernel(first, step, mixed_ref, weight_ref, out_ref)


def project_kernel(first, step, mixed_ref, weight_ref, out_ref):
    mixed = mixed_ref[...]
    for i in range(out_ref.shape[0]):
        terms = jnp.dot(mixed, weight_ref[first + step * i], preferred_element_type=F32)
        out_ref[i] = terms.astype(out_ref.dtype)


def finish_kernel(*refs):
    *terms, out_ref = refs
    total = terms[0][...].astype(F32)
    for term in terms[1:]:
        total = total + term[...].astype(F32)
    out_ref[...] = total.T


def gated_kernel(key_ref, value_ref, out_ref):
    width = out_ref.shape[2]
    for j in range(out_ref.shape[0]):
        cols = slice(j * width, (j + 1) * width)
        out_ref[j] = (key_ref[:, cols].astype(F32) * value_ref[:, cols].astype(F32)).astype(BF16)


def local(
    query, key_gate, value, group_order, emb_weight, emb_bias, mid_weight, mid_bias, out_filter, decay_rate, skip_gain,
    out_weight,
):
    rows, chan_width = query.shape
    seq_count, chan_count = lax.axis_size("seq"), lax.axis_size("chan")
    seq_index, chan_index = lax.axis_index("seq"), lax.axis_index("chan")
    length = rows * seq_count
    slots = length // GROUP
    width = chan_width // seq_count
    block = max(2 * GROUP, length // 16)
    blocks = length // block
    emb, order = emb_weight.shape
    head, head_tail, inverse = packed_tables(block)
    feat_rows = -(-(emb + 1) // 8) * 8
    features = feature_table(length, (emb - 1) // 2, feat_rows)

    tile = GROUP // 2
    signal = pl.pallas_call(
        gated_kernel,
        out_shape=jax.ShapeDtypeStruct((seq_count, rows, width), BF16),
        grid=(rows // tile,),
        in_specs=[pl.BlockSpec((tile, chan_width), lambda i: (i, 0))] * 2,
        out_specs=pl.BlockSpec((seq_count, tile, width), lambda i: (0, i, 0)),
    )(key_gate, value)
    spread = lax.all_to_all(signal, "seq", 0, 0, tiled=True).reshape(slots, GROUP, width)

    my_filter = lax.dynamic_slice_in_dim(out_filter, seq_index * width, width, 1)
    my_decay = lax.dynamic_slice_in_dim(decay_rate, seq_index * width, width)[None, :]
    norm = jnp.sqrt(-jnp.expm1(-2.0 * my_decay))
    pad = [(0, 0), (0, LANES - width)]
    if width < LANES:
        my_filter, my_decay, norm = jnp.pad(my_filter, pad), jnp.pad(my_decay, pad), jnp.pad(norm, pad)
        spread = jnp.pad(spread, [(0, 0)] + pad)
    limit = pltpu.CompilerParams(vmem_limit_bytes=20 << 20)
    in_vmem = pl.BlockSpec(memory_space=pltpu.VMEM)
    in_smem = pl.BlockSpec(memory_space=pltpu.SMEM)
    in_hbm = pl.BlockSpec(memory_space=pltpu.HBM)
    far = lambda operand: pltpu.with_memory_space_constraint(operand, pltpu.HBM)
    out_width = out_weight.shape[1] // chan_count
    real, imag, edge, head, inverse = pl.pallas_call(
        functools.partial(filter_kernel, block),
        out_shape=(
            jax.ShapeDtypeStruct((blocks, block, LANES), F32),
            jax.ShapeDtypeStruct((blocks, block, LANES), F32),
            jax.ShapeDtypeStruct((blocks, 16, LANES), F32),
            jax.ShapeDtypeStruct(head.shape, BF16),
            jax.ShapeDtypeStruct(inverse.shape, BF16),
        ),
        in_specs=[in_vmem] * 3 + [in_hbm] * 8,
        out_specs=[in_vmem] * 5,
        scratch_shapes=[
            pltpu.VMEM(features.shape, F32),
            pltpu.VMEM((emb, order), F32),
            pltpu.VMEM((1, order), F32),
            pltpu.VMEM((order, order), F32),
            pltpu.VMEM((1, order), F32),
            pltpu.VMEM(head_tail.shape, BF16),
            pltpu.VMEM((feat_rows, order), F32),
            pltpu.VMEM((order + 8, order), F32),
            pltpu.VMEM((order + 8, length), F32),
            pltpu.VMEM((length + block, LANES), BF16),
            pltpu.SemaphoreType.DMA((8,)),
        ],
        compiler_params=limit,
    )(
        my_filter, my_decay, norm,
        *map(far, (features, emb_weight, emb_bias[None, :], mid_weight, mid_bias[None, :], head_tail, head, inverse)),
    )

    convolved, weights, query_near, signal_near = pl.pallas_call(
        functools.partial(conv_kernel, block),
        out_shape=(
            jax.ShapeDtypeStruct((slots, GROUP, LANES), BF16),
            jax.ShapeDtypeStruct((chan_count, chan_width, out_width), BF16),
            jax.ShapeDtypeStruct(query.shape, BF16),
            jax.ShapeDtypeStruct(signal.shape, BF16),
        ),
        in_specs=[in_smem] * 2 + [in_vmem] * 6 + [in_hbm] * 3,
        out_specs=[in_vmem] * 4,
        scratch_shapes=[
            pltpu.VMEM((length, LANES), BF16),
            pltpu.VMEM((blocks, block, LANES), F32),
            pltpu.VMEM((blocks, block, LANES), F32),
            pltpu.VMEM((2 * block, blocks * LANES), BF16),
            pltpu.VMEM((length, LANES), BF16),
            pltpu.SemaphoreType.DMA((chan_count,)),
            pltpu.SemaphoreType.DMA((2,)),
        ],
        compiler_params=limit,
    )(group_order, chan_index[None], spread, real, imag, edge, head, inverse, *map(far, (out_weight, query, signal)))
    back = lax.all_to_all(convolved[:, :, :width].reshape(seq_count, rows, width), "seq", 0, 0, tiled=True)

    def exchange(terms, bit):
        return lax.ppermute(terms, "chan", [(d, d ^ bit) for d in range(chan_count)])

    def products(first, step, count, dtype):
        return pl.pallas_call(
            functools.partial(project_kernel, first, step),
            out_shape=jax.ShapeDtypeStruct((count, rows, out_width), dtype),
            in_specs=[in_vmem] * 2,
            out_specs=in_vmem,
            compiler_params=limit,
        )(mixed, weights)

    quarter = chan_count // 4
    far_away, mixed = pl.pallas_call(
        functools.partial(mix_kernel, 3, 4),
        out_shape=(
            jax.ShapeDtypeStruct((quarter, rows, out_width), BF16),
            jax.ShapeDtypeStruct((rows, chan_width), BF16),
        ),
        in_specs=[in_vmem] * 5,
        out_specs=[in_vmem] * 2,
        compiler_params=limit,
    )(back, signal_near, query_near, skip_gain[None, :], weights)
    far_terms = exchange(far_away, 1)
    far_kept = products(2, 4, quarter, F32)
    terms = [exchange((far_kept + far_terms.astype(F32)).astype(BF16), 2)]
    near_terms = exchange(products(1, 4, quarter, BF16), 1)
    terms += [products(0, 4, quarter, F32), near_terms]
    bit = 4
    while bit < chan_count:
        total = sum(term.astype(F32) for term in terms)
        terms = [total[0::2], exchange(total[1::2].astype(BF16), bit)]
        bit *= 2
    return pl.pallas_call(
        finish_kernel,
        out_shape=jax.ShapeDtypeStruct((out_width, rows), F32),
        compiler_params=limit,
    )(*[term[0] for term in terms])


def solution(mesh):
    return jax.shard_map(
        local,
        mesh=mesh,
        in_specs=(
            P("seq", "chan"), P("seq", "chan"), P("seq", "chan"), P(), P(), P(), P(), P(), P(None, "chan"), P("chan"),
            P("chan"), P("chan", None),
        ),
        out_specs=P("chan", "seq"),
        check_vma=False,
    )
```

```python
import functools
import math

import jax
import jax.numpy as jnp
import numpy as np
from jax import lax
from jax.experimental import pallas as pl
from jax.experimental.pallas import tpu as pltpu
from jax.sharding import PartitionSpec as P

GROUP = 128
LANES = 128
SINE_FREQ = 2.0
F32 = jnp.float32
BF16 = jnp.bfloat16


def packed_tables(block):
    period = 2 * block
    row = np.arange(block)
    freq = np.arange(block)

    def forward(shift):
        angle = 2.0 * np.pi * (freq[:, None] * (row[None, :] + shift) % period) / period
        real, imag = np.cos(angle), -np.sin(angle)
        imag[0] = np.where((row + shift) % 2 == 0, 1.0, -1.0)
        return np.concatenate([real, imag], 0)

    head, tail = forward(0), forward(block)
    tail[:, 0] = 0.0
    weight = np.where(freq == 0, 1.0, 2.0) / period
    angle = 2.0 * np.pi * (row[:, None] * freq[None, :] % period) / period
    real, imag = np.cos(angle) * weight, -np.sin(angle) * weight
    imag[:, 0] = np.where(row % 2 == 0, 1.0, -1.0) / period
    inverse = np.concatenate([real, imag], 1)
    to_bf16 = lambda table: jnp.asarray(table.astype(np.float32)).astype(BF16)
    return to_bf16(head), to_bf16(np.concatenate([head, tail], 1)), to_bf16(inverse)


def feature_table(length, bands, rows):
    lag = np.arange(length)
    angle = 2.0 * np.pi * (np.arange(1, bands + 1)[:, None] * lag[None, :] % length) / length
    table = np.zeros((rows, length), np.float32)
    table[0] = lag / length
    table[1 : bands + 1] = np.cos(angle)
    table[bands + 1 : 2 * bands + 1] = np.sin(angle)
    table[2 * bands + 1] = 1.0
    return jnp.asarray(table)


def contract_first(lhs, rhs):
    return lax.dot_general(
        lhs, rhs, (((0,), (0,)), ((), ())), precision=lax.Precision.HIGHEST, preferred_element_type=F32
    )


def filter_kernel(
    block, out_w_ref, decay_ref, norm_ref, feat_hbm, emb_w_hbm, emb_b_hbm, mid_w_hbm, mid_b_hbm, table_hbm,
    head_hbm, inverse_hbm, real_ref, imag_ref, edge_ref, head_ref, inverse_ref, feat_ref, emb_w_ref, emb_b_ref, mid_w_ref, mid_b_ref, table_ref, w1, w2, hid, filt, sem,
):
    sources = (feat_hbm, emb_w_hbm, emb_b_hbm, mid_w_hbm, mid_b_hbm, table_hbm, head_hbm, inverse_hbm)
    targets = (feat_ref, emb_w_ref, emb_b_ref, mid_w_ref, mid_b_ref, table_ref, head_ref, inverse_ref)
    copies = [pltpu.make_async_copy(s, t, sem.at[i]) for i, (s, t) in enumerate(zip(sources, targets))]
    for copy in copies:
        copy.start()
    for copy in copies:
        copy.wait()
    emb, order = emb_w_ref.shape
    length = feat_ref.shape[1]
    blocks = length // block
    w1[...] = jnp.zeros_like(w1)
    w1[0:emb, :] = emb_w_ref[...]
    w1[emb : emb + 1, :] = emb_b_ref[...]
    w2[...] = jnp.zeros_like(w2)
    w2[0:order, :] = mid_w_ref[...]
    w2[order : order + 1, :] = mid_b_ref[...]
    hid[order:, :] = jnp.ones_like(hid[order:, :])
    hid[0:order, :] = jnp.sin(SINE_FREQ * contract_first(w1[...], feat_ref[...]))
    hidden = jnp.sin(SINE_FREQ * contract_first(w2[...], hid[...]))
    raw = contract_first(hidden, out_w_ref[...])
    decay = decay_ref[...]
    within = jnp.exp(-decay * lax.broadcasted_iota(jnp.int32, (block, LANES), 0).astype(F32))
    within = within * norm_ref[...]
    filt[0:block, :] = jnp.zeros((block, LANES), BF16)
    for m in range(blocks):
        start = jnp.exp(-decay * float(m * block))
        filt[(m + 1) * block : (m + 2) * block, :] = (raw[m * block : (m + 1) * block] * (within * start)).astype(BF16)
    first_row = lax.broadcasted_iota(jnp.int32, (16, LANES), 0) == 0
    group = 2
    for m0 in range(0, blocks, group):
        stacked = jnp.concatenate(
            [
                jnp.concatenate(
                    [filt[(m + 1) * block : (m + 2) * block, :], filt[m * block : (m + 1) * block, :]], 0
                )
                for m in range(m0, m0 + group)
            ],
            1,
        )
        spectrum = jnp.dot(table_ref[...], stacked, preferred_element_type=F32)
        for i in range(group):
            m = m0 + i
            real = spectrum[:block, i * LANES : (i + 1) * LANES]
            imag = spectrum[block:, i * LANES : (i + 1) * LANES]
            real_ref[m] = real
            imag_ref[m] = imag
            edge_ref[m] = jnp.where(first_row, imag[:16], real[:16])
            imag_ref[m, 0:16, :] = jnp.where(first_row, 0.0, imag[:16])


def weight_copies(index_ref, blocks, weight_hbm, weight_out, sem):
    _, depth, width = weight_out.shape
    pieces = sem.shape[1]
    unit = depth // pieces
    copies = []
    for i, j in enumerate(blocks):
        cols = pl.ds(pl.multiple_of((index_ref[0] ^ j) * width, LANES), width)
        for k in range(pieces):
            rows = pl.ds(pl.multiple_of((index_ref[1] ^ k) * unit, LANES), unit)
            target = weight_out.at[i, k * unit : (k + 1) * unit]
            copies.append(pltpu.make_async_copy(weight_hbm.at[rows, cols], target, sem.at[i, k]))
    return copies


def conv_kernel(
    block, far_blocks, index_ref, x_ref, real_ref, imag_ref, edge_ref, table_ref, inverse_ref, weight_hbm,
    query_hbm, signal_hbm, *refs,
):
    *out_refs, weight_out, query_out, signal_out, sig, sre, sim, spec, conv, weight_sem, query_sem, signal_sem = refs
    pieces, _, unit = query_out.shape
    copies = []
    for k in range(pieces):
        piece = index_ref[1] ^ k
        cols = pl.ds(pl.multiple_of(piece * unit, LANES), unit)
        copies.append(pltpu.make_async_copy(query_hbm.at[:, cols], query_out.at[k], query_sem.at[k]))
        copies.append(pltpu.make_async_copy(signal_hbm.at[piece], signal_out.at[k], signal_sem.at[k]))
    copies += weight_copies(index_ref, far_blocks, weight_hbm, weight_out, weight_sem)
    for copy in copies:
        copy.start()
    slots = x_ref.shape[0]
    length = slots * GROUP
    blocks = length // block
    for p in range(slots):
        start = pl.multiple_of(index_ref[2 + p] * GROUP, GROUP)
        sig[pl.ds(start, GROUP), :] = x_ref[p]
    group = 2
    for b0 in range(0, blocks, group):
        stacked = jnp.concatenate([sig[b * block : (b + 1) * block, :] for b in range(b0, b0 + group)], 1)
        spectrum = jnp.dot(table_ref[...], stacked, preferred_element_type=F32)
        for i in range(group):
            sre[b0 + i] = spectrum[:block, i * LANES : (i + 1) * LANES]
            sim[b0 + i] = spectrum[block:, i * LANES : (i + 1) * LANES]

    def tile(start, first):
        rows = pl.ds(start, 16)
        mirror = pl.ds(block + start, 16)
        s_real = [sre[q, rows, :] for q in range(blocks)]
        s_imag = [sim[q, rows, :] for q in range(blocks)]
        for g in range(blocks):
            acc_real = acc_imag = None
            for q in range(g + 1):
                fr, fi = real_ref[g - q, rows, :], imag_ref[g - q, rows, :]
                fe = edge_ref[g - q] if first else fr
                re = fr * s_real[q] - fi * s_imag[q]
                im = fe * s_imag[q] + fi * s_real[q]
                acc_real = re if q == 0 else acc_real + re
                acc_imag = im if q == 0 else acc_imag + im
            spec[rows, g * LANES : (g + 1) * LANES] = acc_real.astype(BF16)
            spec[mirror, g * LANES : (g + 1) * LANES] = acc_imag.astype(BF16)

    tile(0, True)

    @pl.loop(1, block // 16)
    def _(t):
        tile(pl.multiple_of(t * 16, 16), False)

    result = jnp.dot(inverse_ref[...], spec[...], preferred_element_type=F32)
    for g in range(blocks):
        conv[g * block : (g + 1) * block, :] = result[:, g * LANES : (g + 1) * LANES].astype(BF16)
    groups = slots // len(out_refs)
    for k, out_ref in enumerate(out_refs):
        for i in range(groups):
            slot = (index_ref[1] ^ k) * groups + i
            start = pl.multiple_of(index_ref[2 + slot] * GROUP, GROUP)
            out_ref[i * GROUP : (i + 1) * GROUP, :] = conv[pl.ds(start, GROUP), :]
    for copy in copies:
        copy.wait()


def mix_kernel(index_ref, sig_ref, query_ref, gain_ref, weight_ref, *refs):
    *back_refs, out_ref, mixed_ref = refs
    unit = sig_ref.shape[2]
    for k, back_ref in enumerate(back_refs):
        gain = gain_ref[pl.ds(index_ref[1] ^ k, 1), :]
        inner = back_ref[...].astype(F32) + gain * sig_ref[k].astype(F32)
        mixed_ref[:, k * unit : (k + 1) * unit] = (query_ref[k].astype(F32) * inner).astype(BF16)
    project_kernel(0, mixed_ref, weight_ref, out_ref)


def project_kernel(first, mixed_ref, weight_ref, out_ref):
    mixed = mixed_ref[...]
    for i in range(out_ref.shape[0]):
        out_ref[i] = jnp.dot(mixed, weight_ref[first + i], preferred_element_type=F32).astype(out_ref.dtype)


def near_kernel(near_blocks, index_ref, mixed_ref, weight_hbm, away_ref, kept_ref, weight_near, sem):
    copies = weight_copies(index_ref, near_blocks, weight_hbm, weight_near, sem)
    for copy in copies:
        copy.start()
    count = away_ref.shape[0]
    for copy in copies[: len(copies) // 2]:
        copy.wait()
    project_kernel(0, mixed_ref, weight_near, away_ref)
    for copy in copies[len(copies) // 2 :]:
        copy.wait()
    project_kernel(count, mixed_ref, weight_near, kept_ref)


def finish_kernel(part, count, *refs):
    *operands, out_hbm, turned, sem = refs
    rows = turned.shape[1]
    total = operands[0][...].astype(F32)
    for term in operands[1:count]:
        total = total + term[...].astype(F32)
    turned[...] = total.T
    copy = pltpu.make_async_copy(turned, out_hbm.at[:, part * rows : (part + 1) * rows], sem.at[0])
    copy.start()
    copy.wait()


def gated_kernel(key_hbm, value_hbm, out_hbm, key_ref, value_ref, out_ref, in_sem, out_sem):
    parts, rows, _ = key_ref.shape
    count, _, width = out_hbm.shape
    loads, stores = [], []
    for i in range(parts):
        part = slice(i * rows, (i + 1) * rows)
        loads.append(pltpu.make_async_copy(key_hbm.at[part], key_ref.at[i], in_sem.at[0, i]))
        loads.append(pltpu.make_async_copy(value_hbm.at[part], value_ref.at[i], in_sem.at[1, i]))
        stores.append(pltpu.make_async_copy(out_ref.at[i], out_hbm.at[:, part], out_sem.at[i]))
    for load in loads:
        load.start()
    for i in range(parts):
        loads[2 * i].wait()
        loads[2 * i + 1].wait()
        for j in range(count):
            cols = slice(j * width, (j + 1) * width)
            out_ref[i, j] = (key_ref[i, :, cols].astype(F32) * value_ref[i, :, cols].astype(F32)).astype(BF16)
        stores[i].start()
    for store in stores:
        store.wait()


def local(
    query, key_gate, value, group_order, emb_weight, emb_bias, mid_weight, mid_bias, out_filter, decay_rate, skip_gain,
    out_weight,
):
    rows, chan_width = query.shape
    seq_count, chan_count = lax.axis_size("seq"), lax.axis_size("chan")
    seq_index, chan_index = lax.axis_index("seq"), lax.axis_index("chan")
    length = rows * seq_count
    slots = length // GROUP
    width = chan_width // seq_count
    block = max(2 * GROUP, length // 16)
    blocks = length // block
    emb, order = emb_weight.shape
    head, head_tail, inverse = packed_tables(block)
    feat_rows = -(-(emb + 1) // 8) * 8
    features = feature_table(length, (emb - 1) // 2, feat_rows)

    limit = pltpu.CompilerParams(vmem_limit_bytes=20 << 20)
    in_vmem = pl.BlockSpec(memory_space=pltpu.VMEM)
    in_smem = pl.BlockSpec(memory_space=pltpu.SMEM)
    in_hbm = pl.BlockSpec(memory_space=pltpu.HBM)
    far = lambda operand: pltpu.with_memory_space_constraint(operand, pltpu.HBM)
    parts = 4
    signal = pl.pallas_call(
        gated_kernel,
        out_shape=jax.ShapeDtypeStruct((seq_count, rows, width), BF16),
        in_specs=[in_hbm] * 2,
        out_specs=in_hbm,
        scratch_shapes=[
            pltpu.VMEM((parts, rows // parts, chan_width), BF16),
            pltpu.VMEM((parts, rows // parts, chan_width), BF16),
            pltpu.VMEM((parts, seq_count, rows // parts, width), BF16),
            pltpu.SemaphoreType.DMA((2, parts)),
            pltpu.SemaphoreType.DMA((parts,)),
        ],
        compiler_params=limit,
    )(far(key_gate), far(value))
    spread = lax.all_to_all(signal, "seq", 0, 0, tiled=True).reshape(slots, GROUP, width)

    my_filter = lax.dynamic_slice_in_dim(out_filter, seq_index * width, width, 1)
    my_decay = lax.dynamic_slice_in_dim(decay_rate, seq_index * width, width)[None, :]
    norm = jnp.sqrt(-jnp.expm1(-2.0 * my_decay))
    pad = [(0, 0), (0, LANES - width)]
    if width < LANES:
        my_filter, my_decay, norm = jnp.pad(my_filter, pad), jnp.pad(my_decay, pad), jnp.pad(norm, pad)
        spread = jnp.pad(spread, [(0, 0)] + pad)
    out_width = out_weight.shape[1] // chan_count
    real, imag, edge, head, inverse = pl.pallas_call(
        functools.partial(filter_kernel, block),
        out_shape=(
            jax.ShapeDtypeStruct((blocks, block, LANES), F32),
            jax.ShapeDtypeStruct((blocks, block, LANES), F32),
            jax.ShapeDtypeStruct((blocks, 16, LANES), F32),
            jax.ShapeDtypeStruct(head.shape, BF16),
            jax.ShapeDtypeStruct(inverse.shape, BF16),
        ),
        in_specs=[in_vmem] * 3 + [in_hbm] * 8,
        out_specs=[in_vmem] * 5,
        scratch_shapes=[
            pltpu.VMEM(features.shape, F32),
            pltpu.VMEM((emb, order), F32),
            pltpu.VMEM((1, order), F32),
            pltpu.VMEM((order, order), F32),
            pltpu.VMEM((1, order), F32),
            pltpu.VMEM(head_tail.shape, BF16),
            pltpu.VMEM((feat_rows, order), F32),
            pltpu.VMEM((order + 8, order), F32),
            pltpu.VMEM((order + 8, length), F32),
            pltpu.VMEM((length + block, LANES), BF16),
            pltpu.SemaphoreType.DMA((8,)),
        ],
        compiler_params=limit,
    )(
        my_filter, my_decay, norm,
        *map(far, (features, emb_weight, emb_bias[None, :], mid_weight, mid_bias[None, :], head_tail, head, inverse)),
    )

    unit = width if width % LANES == 0 else chan_width
    pieces = chan_width // unit
    if pieces == 1:
        signal = signal.transpose(1, 0, 2).reshape(1, rows, chan_width)
    base = seq_index if pieces > 1 else jnp.zeros_like(seq_index)
    index = jnp.concatenate([chan_index[None], base[None], group_order])
    quarter = chan_count // 4
    odd = range(1, chan_count, 2)
    far_blocks = [j for j in odd if j & 2] + [j ^ 1 for j in odd if j & 2]
    near_blocks = [j for j in odd if not j & 2] + [j ^ 1 for j in odd if not j & 2]
    *convolved, weights, query_near, signal_near = pl.pallas_call(
        functools.partial(conv_kernel, block, far_blocks),
        out_shape=(
            *[jax.ShapeDtypeStruct((rows, LANES), BF16)] * seq_count,
            jax.ShapeDtypeStruct((2 * quarter, chan_width, out_width), BF16),
            jax.ShapeDtypeStruct((pieces, rows, unit), BF16),
            jax.ShapeDtypeStruct((pieces, rows, unit), BF16),
        ),
        in_specs=[in_smem] + [in_vmem] * 6 + [in_hbm] * 3,
        out_specs=[in_vmem] * (seq_count + 3),
        scratch_shapes=[
            pltpu.VMEM((length, LANES), BF16),
            pltpu.VMEM((blocks, block, LANES), F32),
            pltpu.VMEM((blocks, block, LANES), F32),
            pltpu.VMEM((2 * block, blocks * LANES), BF16),
            pltpu.VMEM((length, LANES), BF16),
            pltpu.SemaphoreType.DMA((2 * quarter, pieces)),
            pltpu.SemaphoreType.DMA((pieces,)),
            pltpu.SemaphoreType.DMA((pieces,)),
        ],
        compiler_params=limit,
    )(index, spread, real, imag, edge, head, inverse, *map(far, (out_weight, query, signal)))
    if pieces == 1:
        ordered = lax.all_to_all(jnp.stack([piece[:, :width] for piece in convolved]), "seq", 0, 0, tiled=True)
        backs = [ordered.transpose(1, 0, 2).reshape(rows, chan_width)]
    else:
        backs = [convolved[0]]
        for k in range(1, seq_count):
            backs.append(lax.ppermute(convolved[k], "seq", [(d, d ^ k) for d in range(seq_count)]))

    def exchange(terms, bit):
        return lax.ppermute(terms, "chan", [(d, d ^ bit) for d in range(chan_count)])

    far_away, mixed = pl.pallas_call(
        mix_kernel,
        out_shape=(
            jax.ShapeDtypeStruct((quarter, rows, out_width), BF16),
            jax.ShapeDtypeStruct((rows, chan_width), BF16),
        ),
        in_specs=[in_smem] + [in_vmem] * (4 + pieces),
        out_specs=[in_vmem] * 2,
        compiler_params=limit,
    )(index, signal_near, query_near, skip_gain.reshape(pieces, unit), weights, *backs)
    far_terms = exchange(far_away, 1)
    far_kept = pl.pallas_call(
        functools.partial(project_kernel, quarter),
        out_shape=jax.ShapeDtypeStruct((quarter, rows, out_width), F32),
        in_specs=[in_vmem] * 2,
        out_specs=in_vmem,
        compiler_params=limit,
    )(mixed, weights)
    send, mixed = lax.optimization_barrier(((far_kept + far_terms.astype(F32)).astype(BF16), mixed))
    half = rows // 2
    halves = [slice(0, half), slice(half, rows)]
    sent = [exchange(send[:, part], 2) for part in halves]
    near_away, near_kept = pl.pallas_call(
        functools.partial(near_kernel, near_blocks),
        out_shape=(
            jax.ShapeDtypeStruct((quarter, rows, out_width), BF16),
            jax.ShapeDtypeStruct((quarter, rows, out_width), F32),
        ),
        in_specs=[in_smem, in_vmem, in_hbm],
        out_specs=[in_vmem] * 2,
        scratch_shapes=[
            pltpu.VMEM((2 * quarter, chan_width, out_width), BF16),
            pltpu.SemaphoreType.DMA((2 * quarter, pieces)),
        ],
        compiler_params=limit,
    )(index, mixed, far(out_weight))
    near_terms = exchange(near_away, 1)
    result = None
    for i, part in enumerate(halves):
        terms = [near_kept[:, part], near_terms[:, part], sent[i]]
        bit = 4
        while bit < chan_count:
            total = sum(term.astype(F32) for term in terms)
            terms = [total[0::2], exchange(total[1::2].astype(BF16), bit)]
            bit *= 2
        operands = [term[0] for term in terms]
        extra = [] if result is None else [result]
        result = pl.pallas_call(
            functools.partial(finish_kernel, i, len(operands)),
            out_shape=jax.ShapeDtypeStruct((out_width, rows), F32),
            in_specs=[in_vmem] * len(operands) + [in_hbm] * len(extra),
            out_specs=in_hbm,
            scratch_shapes=[pltpu.VMEM((out_width, half), F32), pltpu.SemaphoreType.DMA((1,))],
            input_output_aliases={len(operands): 0} if extra else {},
            compiler_params=limit,
        )(*operands, *extra)
    return result


def solution(mesh):
    return jax.shard_map(
        local,
        mesh=mesh,
        in_specs=(
            P("seq", "chan"), P("seq", "chan"), P("seq", "chan"), P(), P(), P(), P(), P(), P(None, "chan"), P("chan"),
            P("chan"), P("chan", None),
        ),
        out_specs=P("chan", "seq"),
        check_vma=False,
    )
```

```python
import functools
import math

import jax
import jax.numpy as jnp
import numpy as np
from jax import lax
from jax.experimental import pallas as pl
from jax.experimental.pallas import tpu as pltpu
from jax.sharding import PartitionSpec as P

GROUP = 128
LANES = 128
SINE_FREQ = 2.0
F32 = jnp.float32
BF16 = jnp.bfloat16


def packed_tables(block):
    period = 2 * block
    row = np.arange(block)
    freq = np.arange(block)

    def forward(shift):
        angle = 2.0 * np.pi * (freq[:, None] * (row[None, :] + shift) % period) / period
        real, imag = np.cos(angle), -np.sin(angle)
        imag[0] = np.where((row + shift) % 2 == 0, 1.0, -1.0)
        return np.concatenate([real, imag], 0)

    head, tail = forward(0), forward(block)
    tail[:, 0] = 0.0
    weight = np.where(freq == 0, 1.0, 2.0) / period
    angle = 2.0 * np.pi * (row[:, None] * freq[None, :] % period) / period
    real, imag = np.cos(angle) * weight, -np.sin(angle) * weight
    imag[:, 0] = np.where(row % 2 == 0, 1.0, -1.0) / period
    inverse = np.concatenate([real, imag], 1)
    to_bf16 = lambda table: jnp.asarray(table.astype(np.float32)).astype(BF16)
    return to_bf16(head), to_bf16(np.concatenate([head, tail], 1)), to_bf16(inverse)


def feature_table(length, bands, rows):
    lag = np.arange(length)
    angle = 2.0 * np.pi * (np.arange(1, bands + 1)[:, None] * lag[None, :] % length) / length
    table = np.zeros((rows, length), np.float32)
    table[0] = lag / length
    table[1 : bands + 1] = np.cos(angle)
    table[bands + 1 : 2 * bands + 1] = np.sin(angle)
    table[2 * bands + 1] = 1.0
    return jnp.asarray(table)


def contract_first(lhs, rhs):
    return lax.dot_general(
        lhs, rhs, (((0,), (0,)), ((), ())), precision=lax.Precision.HIGHEST, preferred_element_type=F32
    )


def filter_kernel(
    block, out_w_ref, decay_ref, norm_ref, feat_hbm, emb_w_hbm, emb_b_hbm, mid_w_hbm, mid_b_hbm, table_hbm,
    head_hbm, inverse_hbm, real_ref, imag_ref, edge_ref, head_ref, inverse_ref, feat_ref, emb_w_ref, emb_b_ref, mid_w_ref, mid_b_ref, table_ref, w1, w2, hid, filt, sem,
):
    sources = (feat_hbm, emb_w_hbm, emb_b_hbm, mid_w_hbm, mid_b_hbm, table_hbm, head_hbm, inverse_hbm)
    targets = (feat_ref, emb_w_ref, emb_b_ref, mid_w_ref, mid_b_ref, table_ref, head_ref, inverse_ref)
    copies = [pltpu.make_async_copy(s, t, sem.at[i]) for i, (s, t) in enumerate(zip(sources, targets))]
    for copy in copies:
        copy.start()
    for copy in copies:
        copy.wait()
    emb, order = emb_w_ref.shape
    length = feat_ref.shape[1]
    blocks = length // block
    w1[...] = jnp.zeros_like(w1)
    w1[0:emb, :] = emb_w_ref[...]
    w1[emb : emb + 1, :] = emb_b_ref[...]
    w2[...] = jnp.zeros_like(w2)
    w2[0:order, :] = mid_w_ref[...]
    w2[order : order + 1, :] = mid_b_ref[...]
    hid[order:, :] = jnp.ones_like(hid[order:, :])
    hid[0:order, :] = jnp.sin(SINE_FREQ * contract_first(w1[...], feat_ref[...]))
    hidden = jnp.sin(SINE_FREQ * contract_first(w2[...], hid[...]))
    raw = contract_first(hidden, out_w_ref[...])
    decay = decay_ref[...]
    within = jnp.exp(-decay * lax.broadcasted_iota(jnp.int32, (block, LANES), 0).astype(F32))
    within = within * norm_ref[...]
    filt[0:block, :] = jnp.zeros((block, LANES), BF16)
    for m in range(blocks):
        start = jnp.exp(-decay * float(m * block))
        filt[(m + 1) * block : (m + 2) * block, :] = (raw[m * block : (m + 1) * block] * (within * start)).astype(BF16)
    first_row = lax.broadcasted_iota(jnp.int32, (16, LANES), 0) == 0
    group = 2
    for m0 in range(0, blocks, group):
        stacked = jnp.concatenate(
            [
                jnp.concatenate(
                    [filt[(m + 1) * block : (m + 2) * block, :], filt[m * block : (m + 1) * block, :]], 0
                )
                for m in range(m0, m0 + group)
            ],
            1,
        )
        spectrum = jnp.dot(table_ref[...], stacked, preferred_element_type=F32)
        for i in range(group):
            m = m0 + i
            real = spectrum[:block, i * LANES : (i + 1) * LANES]
            imag = spectrum[block:, i * LANES : (i + 1) * LANES]
            real_ref[m] = real
            imag_ref[m] = imag
            edge_ref[m] = jnp.where(first_row, imag[:16], real[:16])
            imag_ref[m, 0:16, :] = jnp.where(first_row, 0.0, imag[:16])


def weight_copies(index_ref, blocks, weight_hbm, weight_out, sem):
    _, depth, width = weight_out.shape
    pieces = sem.shape[1]
    unit = depth // pieces
    copies = []
    for i, j in enumerate(blocks):
        cols = pl.ds(pl.multiple_of((index_ref[0] ^ j) * width, LANES), width)
        for k in range(pieces):
            rows = pl.ds(pl.multiple_of((index_ref[1] ^ k) * unit, LANES), unit)
            target = weight_out.at[i, k * unit : (k + 1) * unit]
            copies.append(pltpu.make_async_copy(weight_hbm.at[rows, cols], target, sem.at[i, k]))
    return copies


def conv_kernel(
    block, first_blocks, index_ref, x_ref, real_ref, imag_ref, edge_ref, table_ref, inverse_ref, gain_ref,
    weight_hbm, query_hbm, signal_hbm, *refs,
):
    *out_refs, weight_out, query_out, signal_out, gain_out, sig, sre, sim, spec, conv, weight_sem, query_sem, signal_sem = refs
    pieces, _, unit = query_out.shape
    copies = []
    for k in range(pieces):
        piece = index_ref[1] ^ k
        cols = pl.ds(pl.multiple_of(piece * unit, LANES), unit)
        copies.append(pltpu.make_async_copy(query_hbm.at[:, cols], query_out.at[k], query_sem.at[k]))
        copies.append(pltpu.make_async_copy(signal_hbm.at[piece], signal_out.at[k], signal_sem.at[k]))
        gain_out[k : k + 1, :] = gain_ref[pl.ds(piece, 1), :]
    copies += weight_copies(index_ref, first_blocks, weight_hbm, weight_out, weight_sem)
    for copy in copies:
        copy.start()
    slots = x_ref.shape[0]
    length = slots * GROUP
    blocks = length // block
    for p in range(slots):
        start = pl.multiple_of(index_ref[2 + p] * GROUP, GROUP)
        sig[pl.ds(start, GROUP), :] = x_ref[p]
    group = 2
    for b0 in range(0, blocks, group):
        stacked = jnp.concatenate([sig[b * block : (b + 1) * block, :] for b in range(b0, b0 + group)], 1)
        spectrum = jnp.dot(table_ref[...], stacked, preferred_element_type=F32)
        for i in range(group):
            sre[b0 + i] = spectrum[:block, i * LANES : (i + 1) * LANES]
            sim[b0 + i] = spectrum[block:, i * LANES : (i + 1) * LANES]

    def tile(start, first):
        rows = pl.ds(start, 16)
        mirror = pl.ds(block + start, 16)
        s_real = [sre[q, rows, :] for q in range(blocks)]
        s_imag = [sim[q, rows, :] for q in range(blocks)]
        for g in range(blocks):
            acc_real = acc_imag = None
            for q in range(g + 1):
                fr, fi = real_ref[g - q, rows, :], imag_ref[g - q, rows, :]
                fe = edge_ref[g - q] if first else fr
                re = fr * s_real[q] - fi * s_imag[q]
                im = fe * s_imag[q] + fi * s_real[q]
                acc_real = re if q == 0 else acc_real + re
                acc_imag = im if q == 0 else acc_imag + im
            spec[rows, g * LANES : (g + 1) * LANES] = acc_real.astype(BF16)
            spec[mirror, g * LANES : (g + 1) * LANES] = acc_imag.astype(BF16)

    tile(0, True)

    @pl.loop(1, block // 16)
    def _(t):
        tile(pl.multiple_of(t * 16, 16), False)

    result = jnp.dot(inverse_ref[...], spec[...], preferred_element_type=F32)
    for g in range(blocks):
        conv[g * block : (g + 1) * block, :] = result[:, g * LANES : (g + 1) * LANES].astype(BF16)
    groups = slots // len(out_refs)
    for k, out_ref in enumerate(out_refs):
        for i in range(groups):
            slot = (index_ref[1] ^ k) * groups + i
            start = pl.multiple_of(index_ref[2 + slot] * GROUP, GROUP)
            out_ref[i * GROUP : (i + 1) * GROUP, :] = conv[pl.ds(start, GROUP), :]
    for copy in copies:
        copy.wait()


def mix_kernel(sig_ref, query_ref, gain_ref, weight_ref, *refs):
    *back_refs, out_ref, mixed_ref = refs
    unit = sig_ref.shape[2]
    for k, back_ref in enumerate(back_refs):
        inner = back_ref[...].astype(F32) + gain_ref[k : k + 1, :] * sig_ref[k].astype(F32)
        mixed_ref[:, k * unit : (k + 1) * unit] = (query_ref[k].astype(F32) * inner).astype(BF16)
    project_kernel(0, mixed_ref, weight_ref, out_ref)


def project_kernel(first, mixed_ref, weight_ref, out_ref):
    mixed = mixed_ref[...]
    for i in range(out_ref.shape[0]):
        out_ref[i] = jnp.dot(mixed, weight_ref[first + i], preferred_element_type=F32).astype(out_ref.dtype)


def last_kernel(last_blocks, index_ref, mixed_ref, weight_hbm, out_ref, weight_near, sem):
    copies = weight_copies(index_ref, last_blocks, weight_hbm, weight_near, sem)
    for copy in copies:
        copy.start()
    for copy in copies:
        copy.wait()
    project_kernel(0, mixed_ref, weight_near, out_ref)


def finish_kernel(part, spans, count, *refs):
    operands, (out_hbm, turned, sem) = refs[: count + len(spans)], refs[-3:]
    rows = turned.shape[1]
    first, last = part * rows, (part + 1) * rows
    total = jnp.concatenate(
        [
            ref[max(first, start) - start : min(last, stop) - start, :].astype(F32)
            for ref, (start, stop) in zip(operands[count:], spans)
        ],
        0,
    )
    for ref in operands[:count]:
        total = total + ref[first:last, :].astype(F32)
    turned[...] = total.T
    copy = pltpu.make_async_copy(turned, out_hbm.at[:, first:last], sem.at[0])
    copy.start()
    copy.wait()


def gated_kernel(key_hbm, value_hbm, out_hbm, key_ref, value_ref, out_ref, in_sem, out_sem):
    parts, rows, _ = key_ref.shape
    count, _, width = out_hbm.shape
    loads, stores = [], []
    for i in range(parts):
        part = slice(i * rows, (i + 1) * rows)
        loads.append(pltpu.make_async_copy(key_hbm.at[part], key_ref.at[i], in_sem.at[0, i]))
        loads.append(pltpu.make_async_copy(value_hbm.at[part], value_ref.at[i], in_sem.at[1, i]))
        stores.append(pltpu.make_async_copy(out_ref.at[i], out_hbm.at[:, part], out_sem.at[i]))
    for load in loads:
        load.start()
    for i in range(parts):
        loads[2 * i].wait()
        loads[2 * i + 1].wait()
        for j in range(count):
            cols = slice(j * width, (j + 1) * width)
            out_ref[i, j] = (key_ref[i, :, cols].astype(F32) * value_ref[i, :, cols].astype(F32)).astype(BF16)
        stores[i].start()
    for store in stores:
        store.wait()


def local(
    query, key_gate, value, group_order, emb_weight, emb_bias, mid_weight, mid_bias, out_filter, decay_rate, skip_gain,
    out_weight,
):
    rows, chan_width = query.shape
    seq_count, chan_count = lax.axis_size("seq"), lax.axis_size("chan")
    seq_index, chan_index = lax.axis_index("seq"), lax.axis_index("chan")
    length = rows * seq_count
    slots = length // GROUP
    width = chan_width // seq_count
    block = max(2 * GROUP, length // 16)
    blocks = length // block
    emb, order = emb_weight.shape
    head, head_tail, inverse = packed_tables(block)
    feat_rows = -(-(emb + 1) // 8) * 8
    features = feature_table(length, (emb - 1) // 2, feat_rows)

    limit = pltpu.CompilerParams(vmem_limit_bytes=20 << 20)
    in_vmem = pl.BlockSpec(memory_space=pltpu.VMEM)
    in_smem = pl.BlockSpec(memory_space=pltpu.SMEM)
    in_hbm = pl.BlockSpec(memory_space=pltpu.HBM)
    far = lambda operand: pltpu.with_memory_space_constraint(operand, pltpu.HBM)
    parts = 4
    signal = pl.pallas_call(
        gated_kernel,
        out_shape=jax.ShapeDtypeStruct((seq_count, rows, width), BF16),
        in_specs=[in_hbm] * 2,
        out_specs=in_hbm,
        scratch_shapes=[
            pltpu.VMEM((parts, rows // parts, chan_width), BF16),
            pltpu.VMEM((parts, rows // parts, chan_width), BF16),
            pltpu.VMEM((parts, seq_count, rows // parts, width), BF16),
            pltpu.SemaphoreType.DMA((2, parts)),
            pltpu.SemaphoreType.DMA((parts,)),
        ],
        compiler_params=limit,
    )(far(key_gate), far(value))
    spread = lax.all_to_all(signal, "seq", 0, 0, tiled=True).reshape(slots, GROUP, width)

    my_filter = lax.dynamic_slice_in_dim(out_filter, seq_index * width, width, 1)
    my_decay = lax.dynamic_slice_in_dim(decay_rate, seq_index * width, width)[None, :]
    norm = jnp.sqrt(-jnp.expm1(-2.0 * my_decay))
    pad = [(0, 0), (0, LANES - width)]
    if width < LANES:
        my_filter, my_decay, norm = jnp.pad(my_filter, pad), jnp.pad(my_decay, pad), jnp.pad(norm, pad)
        spread = jnp.pad(spread, [(0, 0)] + pad)
    out_width = out_weight.shape[1] // chan_count
    real, imag, edge, head, inverse = pl.pallas_call(
        functools.partial(filter_kernel, block),
        out_shape=(
            jax.ShapeDtypeStruct((blocks, block, LANES), F32),
            jax.ShapeDtypeStruct((blocks, block, LANES), F32),
            jax.ShapeDtypeStruct((blocks, 16, LANES), F32),
            jax.ShapeDtypeStruct(head.shape, BF16),
            jax.ShapeDtypeStruct(inverse.shape, BF16),
        ),
        in_specs=[in_vmem] * 3 + [in_hbm] * 8,
        out_specs=[in_vmem] * 5,
        scratch_shapes=[
            pltpu.VMEM(features.shape, F32),
            pltpu.VMEM((emb, order), F32),
            pltpu.VMEM((1, order), F32),
            pltpu.VMEM((order, order), F32),
            pltpu.VMEM((1, order), F32),
            pltpu.VMEM(head_tail.shape, BF16),
            pltpu.VMEM((feat_rows, order), F32),
            pltpu.VMEM((order + 8, order), F32),
            pltpu.VMEM((order + 8, length), F32),
            pltpu.VMEM((length + block, LANES), BF16),
            pltpu.SemaphoreType.DMA((8,)),
        ],
        compiler_params=limit,
    )(
        my_filter, my_decay, norm,
        *map(far, (features, emb_weight, emb_bias[None, :], mid_weight, mid_bias[None, :], head_tail, head, inverse)),
    )

    unit = width if width % LANES == 0 else chan_width
    pieces = chan_width // unit
    if pieces == 1:
        signal = signal.transpose(1, 0, 2).reshape(1, rows, chan_width)
    base = seq_index if pieces > 1 else jnp.zeros_like(seq_index)
    index = jnp.concatenate([chan_index[None], base[None], group_order])
    quarter = chan_count // 4
    odd = range(1, chan_count, 2)
    first_blocks = [j for j in odd if j & 2] + [j ^ 1 for j in odd if j & 2] + [j for j in odd if not j & 2]
    last_blocks = [j ^ 1 for j in odd if not j & 2]
    *convolved, weights, query_near, signal_near, gain_near = pl.pallas_call(
        functools.partial(conv_kernel, block, first_blocks),
        out_shape=(
            *[jax.ShapeDtypeStruct((rows, LANES), BF16)] * seq_count,
            jax.ShapeDtypeStruct((3 * quarter, chan_width, out_width), BF16),
            jax.ShapeDtypeStruct((pieces, rows, unit), BF16),
            jax.ShapeDtypeStruct((pieces, rows, unit), BF16),
            jax.ShapeDtypeStruct((pieces, unit), F32),
        ),
        in_specs=[in_smem] + [in_vmem] * 7 + [in_hbm] * 3,
        out_specs=[in_vmem] * (seq_count + 4),
        scratch_shapes=[
            pltpu.VMEM((length, LANES), BF16),
            pltpu.VMEM((blocks, block, LANES), F32),
            pltpu.VMEM((blocks, block, LANES), F32),
            pltpu.VMEM((2 * block, blocks * LANES), BF16),
            pltpu.VMEM((length, LANES), BF16),
            pltpu.SemaphoreType.DMA((3 * quarter, pieces)),
            pltpu.SemaphoreType.DMA((pieces,)),
            pltpu.SemaphoreType.DMA((pieces,)),
        ],
        compiler_params=limit,
    )(
        index, spread, real, imag, edge, head, inverse, skip_gain.reshape(pieces, unit),
        *map(far, (out_weight, query, signal)),
    )
    if pieces == 1:
        ordered = lax.all_to_all(jnp.stack([piece[:, :width] for piece in convolved]), "seq", 0, 0, tiled=True)
        backs = [ordered.transpose(1, 0, 2).reshape(rows, chan_width)]
    else:
        backs = [convolved[0]]
        for k in range(1, seq_count):
            backs.append(lax.ppermute(convolved[k], "seq", [(d, d ^ k) for d in range(seq_count)]))

    def exchange(terms, bit):
        return lax.ppermute(terms, "chan", [(d, d ^ bit) for d in range(chan_count)])

    far_away, mixed = pl.pallas_call(
        mix_kernel,
        out_shape=(
            jax.ShapeDtypeStruct((quarter, rows, out_width), BF16),
            jax.ShapeDtypeStruct((rows, chan_width), BF16),
        ),
        in_specs=[in_vmem] * (4 + pieces),
        out_specs=[in_vmem] * 2,
        compiler_params=limit,
    )(signal_near, query_near, gain_near, weights, *backs)
    far_terms = exchange(far_away, 1)

    def products(first, dtype):
        return pl.pallas_call(
            functools.partial(project_kernel, first),
            out_shape=jax.ShapeDtypeStruct((quarter, rows, out_width), dtype),
            in_specs=[in_vmem] * 2,
            out_specs=in_vmem,
            compiler_params=limit,
        )(mixed, weights)

    far_kept, near_away = products(quarter, F32), products(2 * quarter, BF16)
    cuts = [0, rows // 2, rows]
    spans = list(zip(cuts, cuts[1:]))
    send = [(far_kept[:, a:b] + far_terms[:, a:b].astype(F32)).astype(BF16) for a, b in spans]
    send, near_away, mixed = lax.optimization_barrier((send, near_away, mixed))
    sent = [exchange(piece, 2) for piece in send]
    near_terms = exchange(near_away, 1)
    near_kept = pl.pallas_call(
        functools.partial(last_kernel, last_blocks),
        out_shape=jax.ShapeDtypeStruct((quarter, rows, out_width), F32),
        in_specs=[in_smem, in_vmem, in_hbm],
        out_specs=in_vmem,
        scratch_shapes=[
            pltpu.VMEM((quarter, chan_width, out_width), BF16),
            pltpu.SemaphoreType.DMA((quarter, pieces)),
        ],
        compiler_params=limit,
    )(index, mixed, far(out_weight))
    terms = [near_kept, near_terms]
    bit = 4
    while bit < chan_count:
        total = terms[0] + terms[1].astype(F32) + jnp.concatenate(sent, 1).astype(F32)
        sent, spans = [exchange(total[1::2].astype(BF16), bit)], [(0, rows)]
        terms = [total[0::2], jnp.zeros_like(total[0::2])]
        bit *= 2
    result = None
    for i in range(rows // GROUP):
        held = [j for j, (a, b) in enumerate(spans) if a < (i + 1) * GROUP and b > i * GROUP]
        operands = [term[0] for term in terms] + [sent[j][0] for j in held]
        extra = [] if result is None else [result]
        result = pl.pallas_call(
            functools.partial(finish_kernel, i, [spans[j] for j in held], len(terms)),
            out_shape=jax.ShapeDtypeStruct((out_width, rows), F32),
            in_specs=[in_vmem] * len(operands) + [in_hbm] * len(extra),
            out_specs=in_hbm,
            scratch_shapes=[pltpu.VMEM((out_width, GROUP), F32), pltpu.SemaphoreType.DMA((1,))],
            input_output_aliases={len(operands): 0} if extra else {},
            compiler_params=limit,
        )(*operands, *extra)
    return result


def solution(mesh):
    return jax.shard_map(
        local,
        mesh=mesh,
        in_specs=(
            P("seq", "chan"), P("seq", "chan"), P("seq", "chan"), P(), P(), P(), P(), P(), P(None, "chan"), P("chan"),
            P("chan"), P("chan", None),
        ),
        out_specs=P("chan", "seq"),
        check_vma=False,
    )
```

```python
import functools
import math

import jax
import jax.numpy as jnp
import numpy as np
from jax import lax
from jax.experimental import pallas as pl
from jax.experimental.pallas import tpu as pltpu
from jax.sharding import PartitionSpec as P

GROUP = 128
LANES = 128
SINE_FREQ = 2.0
F32 = jnp.float32
BF16 = jnp.bfloat16


def packed_tables(block):
    period = 2 * block
    row = np.arange(block)
    freq = np.arange(block)

    def forward(shift):
        angle = 2.0 * np.pi * (freq[:, None] * (row[None, :] + shift) % period) / period
        real, imag = np.cos(angle), -np.sin(angle)
        imag[0] = np.where((row + shift) % 2 == 0, 1.0, -1.0)
        return np.concatenate([real, imag], 0)

    head, tail = forward(0), forward(block)
    tail[:, 0] = 0.0
    weight = np.where(freq == 0, 1.0, 2.0) / period
    angle = 2.0 * np.pi * (row[:, None] * freq[None, :] % period) / period
    real, imag = np.cos(angle) * weight, -np.sin(angle) * weight
    imag[:, 0] = np.where(row % 2 == 0, 1.0, -1.0) / period
    inverse = np.concatenate([real, imag], 1)
    to_bf16 = lambda table: jnp.asarray(table.astype(np.float32)).astype(BF16)
    return to_bf16(head), to_bf16(np.concatenate([head, tail], 1)), to_bf16(inverse)


def feature_table(length, bands, rows):
    lag = np.arange(length)
    angle = 2.0 * np.pi * (np.arange(1, bands + 1)[:, None] * lag[None, :] % length) / length
    table = np.zeros((rows, length), np.float32)
    table[0] = lag / length
    table[1 : bands + 1] = np.cos(angle)
    table[bands + 1 : 2 * bands + 1] = np.sin(angle)
    table[2 * bands + 1] = 1.0
    return jnp.asarray(table)


def sine(x):
    n = jnp.round(x * (1.0 / math.pi))
    r = x - n * 3.140625
    r = r - n * 9.67502593994140625e-4
    r = r - n * 1.509957990978376432e-7
    square = r * r
    series = jnp.full_like(r, -2.5052108e-8)
    for term in (2.7557319e-6, -1.9841270e-4, 8.3333333e-3, -1.6666667e-1):
        series = series * square + term
    odd = n * 0.5 - jnp.floor(n * 0.5)
    return (r + r * square * series) * (1.0 - 4.0 * odd)


def contract_first(lhs, rhs):
    return lax.dot_general(
        lhs, rhs, (((0,), (0,)), ((), ())), precision=lax.Precision.HIGHEST, preferred_element_type=F32
    )


def first_piece(pieces):
    return lax.axis_index("seq") if pieces > 1 else 0


def filter_kernel(
    block, order_of_blocks, out_w_ref, decay_ref, norm_ref, *refs,
):
    smalls, refs = refs[:7], refs[7:]
    weight_hbm, query_hbm, real_ref, imag_ref, edge_ref, weight_out, query_out, gain_out, *refs = refs
    near, (w1, w2, hid, filt, near_sem, weight_sem, query_sem) = refs[:7], refs[7:]
    feat_ref, emb_w_ref, emb_b_ref, mid_w_ref, mid_b_ref, gain_ref, table_ref = near
    fetches = [pltpu.make_async_copy(s, t, near_sem.at[i]) for i, (s, t) in enumerate(zip(smalls, near))]
    for fetch in fetches:
        fetch.start()
    pieces, _, unit = query_out.shape
    width = weight_out.shape[2]
    chan_index, first = lax.axis_index("chan"), first_piece(pieces)
    copies = []
    for k in range(pieces):
        rows = pl.ds(pl.multiple_of((first ^ k) * unit, LANES), unit)
        copies.append(pltpu.make_async_copy(query_hbm.at[:, rows], query_out.at[k], query_sem.at[k]))
        for i, j in enumerate(order_of_blocks):
            cols = pl.ds(pl.multiple_of((chan_index ^ j) * width, LANES), width)
            target = weight_out.at[i, k * unit : (k + 1) * unit]
            copies.append(pltpu.make_async_copy(weight_hbm.at[rows, cols], target, weight_sem.at[i, k]))
    for copy in copies:
        copy.start()
    for fetch in fetches[:-1]:
        fetch.wait()
    for k in range(pieces):
        gain_out[k : k + 1, :] = gain_ref[pl.ds(first ^ k, 1), :]
    emb, order = emb_w_ref.shape
    length = feat_ref.shape[1]
    blocks = length // block
    w1[...] = jnp.zeros_like(w1)
    w1[0:emb, :] = emb_w_ref[...]
    w1[emb : emb + 1, :] = emb_b_ref[...]
    w2[...] = jnp.zeros_like(w2)
    w2[0:order, :] = mid_w_ref[...]
    w2[order : order + 1, :] = mid_b_ref[...]
    hid[order:, :] = jnp.ones_like(hid[order:, :])
    hid[0:order, :] = sine(SINE_FREQ * contract_first(w1[...], feat_ref[...]))
    hidden = sine(SINE_FREQ * contract_first(w2[...], hid[...]))
    raw = contract_first(hidden, out_w_ref[...])
    decay = decay_ref[...]
    within = jnp.exp(-decay * lax.broadcasted_iota(jnp.int32, (block, LANES), 0).astype(F32))
    within = within * norm_ref[...]
    filt[0:block, :] = jnp.zeros((block, LANES), BF16)
    for m in range(blocks):
        start = jnp.exp(-decay * float(m * block))
        filt[(m + 1) * block : (m + 2) * block, :] = (raw[m * block : (m + 1) * block] * (within * start)).astype(BF16)
    fetches[-1].wait()
    first_row = lax.broadcasted_iota(jnp.int32, (16, LANES), 0) == 0
    group = 2
    for m0 in range(0, blocks, group):
        stacked = jnp.concatenate(
            [
                jnp.concatenate(
                    [filt[(m + 1) * block : (m + 2) * block, :], filt[m * block : (m + 1) * block, :]], 0
                )
                for m in range(m0, m0 + group)
            ],
            1,
        )
        spectrum = jnp.dot(table_ref[...], stacked, preferred_element_type=F32)
        for i in range(group):
            m = m0 + i
            real = spectrum[:block, i * LANES : (i + 1) * LANES]
            imag = spectrum[block:, i * LANES : (i + 1) * LANES]
            real_ref[m] = real
            imag_ref[m] = imag
            edge_ref[m] = jnp.where(first_row, imag[:16], real[:16])
            imag_ref[m, 0:16, :] = jnp.where(first_row, 0.0, imag[:16])
    for copy in copies:
        copy.wait()


def conv_kernel(block, relative, order_ref, real_ref, imag_ref, edge_ref, table_ref, inverse_ref, *refs):
    *refs, sig, sre, sim, spec, conv = refs
    count = len(refs) // 2
    x_refs, out_refs = refs[:count], refs[count:]
    first = first_piece(count if relative else 1)
    groups = x_refs[0].shape[0] // GROUP
    length = sig.shape[0]
    blocks = length // block

    def place(k, i):
        return pl.multiple_of(order_ref[(first ^ k) * groups + i] * GROUP, GROUP)

    for k, x_ref in enumerate(x_refs):
        for i in range(groups):
            sig[pl.ds(place(k, i), GROUP), :] = x_ref[i * GROUP : (i + 1) * GROUP, :]
    group = 2
    for b0 in range(0, blocks, group):
        stacked = jnp.concatenate([sig[b * block : (b + 1) * block, :] for b in range(b0, b0 + group)], 1)
        spectrum = jnp.dot(table_ref[...], stacked, preferred_element_type=F32)
        for i in range(group):
            sre[b0 + i] = spectrum[:block, i * LANES : (i + 1) * LANES]
            sim[b0 + i] = spectrum[block:, i * LANES : (i + 1) * LANES]

    def tile(start, first):
        rows = pl.ds(start, 16)
        mirror = pl.ds(block + start, 16)
        s_real = [sre[q, rows, :] for q in range(blocks)]
        s_imag = [sim[q, rows, :] for q in range(blocks)]
        for g in range(blocks):
            acc_real = acc_imag = None
            for q in range(g + 1):
                fr, fi = real_ref[g - q, rows, :], imag_ref[g - q, rows, :]
                fe = edge_ref[g - q] if first else fr
                re = fr * s_real[q] - fi * s_imag[q]
                im = fe * s_imag[q] + fi * s_real[q]
                acc_real = re if q == 0 else acc_real + re
                acc_imag = im if q == 0 else acc_imag + im
            spec[rows, g * LANES : (g + 1) * LANES] = acc_real.astype(BF16)
            spec[mirror, g * LANES : (g + 1) * LANES] = acc_imag.astype(BF16)

    tile(0, True)

    @pl.loop(1, block // 16)
    def _(t):
        tile(pl.multiple_of(t * 16, 16), False)

    result = jnp.dot(inverse_ref[...], spec[...], preferred_element_type=F32)
    for g in range(blocks):
        conv[g * block : (g + 1) * block, :] = result[:, g * LANES : (g + 1) * LANES].astype(BF16)
    for k, out_ref in enumerate(out_refs):
        for i in range(groups):
            out_ref[i * GROUP : (i + 1) * GROUP, :] = conv[pl.ds(place(k, i), GROUP), :]


def mix_kernel(query_ref, gain_ref, weight_ref, *refs):
    *refs, out_ref, mixed_ref = refs
    count = len(refs) // 2
    unit = query_ref.shape[2]
    for k, (back_ref, sig_ref) in enumerate(zip(refs[:count], refs[count:])):
        inner = back_ref[...].astype(F32) + gain_ref[k : k + 1, :] * sig_ref[...].astype(F32)
        mixed_ref[:, k * unit : (k + 1) * unit] = (query_ref[k].astype(F32) * inner).astype(BF16)
    project_kernel(0, mixed_ref, weight_ref, out_ref)


def project_kernel(first, mixed_ref, weight_ref, out_ref):
    mixed = mixed_ref[...]
    for i in range(out_ref.shape[0]):
        out_ref[i] = jnp.dot(mixed, weight_ref[first + i], preferred_element_type=F32).astype(out_ref.dtype)


def finish_kernel(part, spans, count, *refs):
    operands, (out_hbm, turned, sem) = refs[: count + len(spans)], refs[-3:]
    rows = turned.shape[1]
    first, last = part * rows, (part + 1) * rows
    total = jnp.concatenate(
        [
            ref[max(first, start) - start : min(last, stop) - start, :].astype(F32)
            for ref, (start, stop) in zip(operands[count:], spans)
        ],
        0,
    )
    for ref in operands[:count]:
        total = total + ref[first:last, :].astype(F32)
    turned[...] = total.T
    copy = pltpu.make_async_copy(turned, out_hbm.at[:, first:last], sem.at[0])
    copy.start()
    copy.wait()


def gated_kernel(key_hbm, value_hbm, *refs):
    *out_refs, key_ref, value_ref, sem = refs
    pieces = len(out_refs)
    unit = out_refs[0].shape[1]
    copies = []
    for k in range(pieces):
        cols = pl.ds(pl.multiple_of((first_piece(pieces) ^ k) * unit, LANES), unit)
        copies.append(pltpu.make_async_copy(key_hbm.at[:, cols], key_ref.at[k], sem.at[0, k]))
        copies.append(pltpu.make_async_copy(value_hbm.at[:, cols], value_ref.at[k], sem.at[1, k]))
    for copy in copies:
        copy.start()
    for k, out_ref in enumerate(out_refs):
        copies[2 * k].wait()
        copies[2 * k + 1].wait()
        out_ref[...] = (key_ref[k].astype(F32) * value_ref[k].astype(F32)).astype(BF16)


def local(
    query, key_gate, value, group_order, emb_weight, emb_bias, mid_weight, mid_bias, out_filter, decay_rate, skip_gain,
    out_weight,
):
    rows, chan_width = query.shape
    seq_count, chan_count = lax.axis_size("seq"), lax.axis_size("chan")
    seq_index, chan_index = lax.axis_index("seq"), lax.axis_index("chan")
    length = rows * seq_count
    slots = length // GROUP
    width = chan_width // seq_count
    block = max(2 * GROUP, length // 16)
    blocks = length // block
    emb, order = emb_weight.shape
    head, head_tail, inverse = packed_tables(block)
    feat_rows = -(-(emb + 1) // 8) * 8
    features = feature_table(length, (emb - 1) // 2, feat_rows)

    limit = pltpu.CompilerParams(vmem_limit_bytes=20 << 20)
    in_vmem = pl.BlockSpec(memory_space=pltpu.VMEM)
    in_smem = pl.BlockSpec(memory_space=pltpu.SMEM)
    in_hbm = pl.BlockSpec(memory_space=pltpu.HBM)
    far = lambda operand: pltpu.with_memory_space_constraint(operand, pltpu.HBM)
    unit = width if width % LANES == 0 else chan_width
    pieces = chan_width // unit

    def swap(arrays):
        return [arrays[0]] + [
            lax.ppermute(arrays[k], "seq", [(d, d ^ k) for d in range(seq_count)]) for k in range(1, seq_count)
        ]

    signal = pl.pallas_call(
        gated_kernel,
        out_shape=[jax.ShapeDtypeStruct((rows, unit), BF16)] * pieces,
        in_specs=[in_hbm] * 2,
        out_specs=[in_vmem] * pieces,
        scratch_shapes=[
            pltpu.VMEM((pieces, rows, unit), BF16),
            pltpu.VMEM((pieces, rows, unit), BF16),
            pltpu.SemaphoreType.DMA((2, pieces)),
        ],
        compiler_params=limit,
    )(far(key_gate), far(value))
    if pieces > 1:
        spread = swap(signal)
    else:
        in_order = signal[0].reshape(rows, seq_count, width).transpose(1, 0, 2)
        in_order = lax.all_to_all(in_order, "seq", 0, 0, tiled=True)
        spread = list(jnp.pad(in_order, [(0, 0), (0, 0), (0, LANES - width)]))

    my_filter = lax.dynamic_slice_in_dim(out_filter, seq_index * width, width, 1)
    my_decay = lax.dynamic_slice_in_dim(decay_rate, seq_index * width, width)[None, :]
    norm = jnp.sqrt(-jnp.expm1(-2.0 * my_decay))
    pad = [(0, 0), (0, LANES - width)]
    if width < LANES:
        my_filter, my_decay, norm = jnp.pad(my_filter, pad), jnp.pad(my_decay, pad), jnp.pad(norm, pad)
    out_width = out_weight.shape[1] // chan_count
    quarter = chan_count // 4
    odd = range(1, chan_count, 2)
    far_odd, near_odd = [j for j in odd if j & 2], [j for j in odd if not j & 2]
    order_of_blocks = far_odd + [j ^ 1 for j in far_odd] + near_odd + [j ^ 1 for j in near_odd]
    smalls = (
        features, emb_weight, emb_bias[None, :], mid_weight, mid_bias[None, :], skip_gain.reshape(pieces, unit), head_tail
    )
    real, imag, edge, weights, query_near, gain_near = pl.pallas_call(
        functools.partial(filter_kernel, block, order_of_blocks),
        out_shape=(
            jax.ShapeDtypeStruct((blocks, block, LANES), F32),
            jax.ShapeDtypeStruct((blocks, block, LANES), F32),
            jax.ShapeDtypeStruct((blocks, 16, LANES), F32),
            jax.ShapeDtypeStruct((chan_count, chan_width, out_width), BF16),
            jax.ShapeDtypeStruct((pieces, rows, unit), BF16),
            jax.ShapeDtypeStruct((pieces, unit), F32),
        ),
        in_specs=[in_vmem] * 3 + [in_hbm] * 9,
        out_specs=[in_vmem] * 6,
        scratch_shapes=[
            *[pltpu.VMEM(small.shape, small.dtype) for small in smalls],
            pltpu.VMEM((feat_rows, order), F32),
            pltpu.VMEM((order + 8, order), F32),
            pltpu.VMEM((order + 8, length), F32),
            pltpu.VMEM((length + block, LANES), BF16),
            pltpu.SemaphoreType.DMA((len(smalls),)),
            pltpu.SemaphoreType.DMA((chan_count, pieces)),
            pltpu.SemaphoreType.DMA((pieces,)),
        ],
        compiler_params=limit,
    )(my_filter, my_decay, norm, *map(far, (*smalls, out_weight, query)))

    convolved = pl.pallas_call(
        functools.partial(conv_kernel, block, pieces > 1),
        out_shape=[jax.ShapeDtypeStruct((rows, LANES), BF16)] * seq_count,
        in_specs=[in_smem] + [in_vmem] * (5 + seq_count),
        out_specs=[in_vmem] * seq_count,
        scratch_shapes=[
            pltpu.VMEM((length, LANES), BF16),
            pltpu.VMEM((blocks, block, LANES), F32),
            pltpu.VMEM((blocks, block, LANES), F32),
            pltpu.VMEM((2 * block, blocks * LANES), BF16),
            pltpu.VMEM((length, LANES), BF16),
        ],
        compiler_params=limit,
    )(group_order, real, imag, edge, head, inverse, *spread)
    if pieces > 1:
        backs = swap(convolved)
    else:
        in_order = lax.all_to_all(jnp.stack([piece[:, :width] for piece in convolved]), "seq", 0, 0, tiled=True)
        backs = [in_order.transpose(1, 0, 2).reshape(rows, chan_width)]

    def exchange(terms, bit):
        return lax.ppermute(terms, "chan", [(d, d ^ bit) for d in range(chan_count)])

    far_away, mixed = pl.pallas_call(
        mix_kernel,
        out_shape=(
            jax.ShapeDtypeStruct((quarter, rows, out_width), BF16),
            jax.ShapeDtypeStruct((rows, chan_width), BF16),
        ),
        in_specs=[in_vmem] * (3 + 2 * pieces),
        out_specs=[in_vmem] * 2,
        compiler_params=limit,
    )(query_near, gain_near, weights, *backs, *signal)
    far_terms = exchange(far_away, 1)

    def products(first, mixed, dtype):
        return pl.pallas_call(
            functools.partial(project_kernel, first),
            out_shape=jax.ShapeDtypeStruct((quarter, rows, out_width), dtype),
            in_specs=[in_vmem] * 2,
            out_specs=in_vmem,
            compiler_params=limit,
        )(mixed, weights)

    far_kept, near_away = products(quarter, mixed, F32), products(2 * quarter, mixed, BF16)
    cuts = [0, rows // 2, rows]
    spans = list(zip(cuts, cuts[1:]))
    send = [(far_kept[:, a:b] + far_terms[:, a:b].astype(F32)).astype(BF16) for a, b in spans]
    send, near_away, mixed = lax.optimization_barrier((send, near_away, mixed))
    sent = [exchange(piece, 2) for piece in send]
    near_terms = exchange(near_away, 1)
    near_kept = products(3 * quarter, mixed, F32)
    terms = [near_kept, near_terms]
    bit = 4
    while bit < chan_count:
        total = terms[0] + terms[1].astype(F32) + jnp.concatenate(sent, 1).astype(F32)
        sent, spans = [exchange(total[1::2].astype(BF16), bit)], [(0, rows)]
        terms = [total[0::2], jnp.zeros_like(total[0::2])]
        bit *= 2
    result = None
    for i in range(rows // GROUP):
        held = [j for j, (a, b) in enumerate(spans) if a < (i + 1) * GROUP and b > i * GROUP]
        operands = [term[0] for term in terms] + [sent[j][0] for j in held]
        extra = [] if result is None else [result]
        result = pl.pallas_call(
            functools.partial(finish_kernel, i, [spans[j] for j in held], len(terms)),
            out_shape=jax.ShapeDtypeStruct((out_width, rows), F32),
            in_specs=[in_vmem] * len(operands) + [in_hbm] * len(extra),
            out_specs=in_hbm,
            scratch_shapes=[pltpu.VMEM((out_width, GROUP), F32), pltpu.SemaphoreType.DMA((1,))],
            input_output_aliases={len(operands): 0} if extra else {},
            compiler_params=limit,
        )(*operands, *extra)
    return result


def solution(mesh):
    return jax.shard_map(
        local,
        mesh=mesh,
        in_specs=(
            P("seq", "chan"), P("seq", "chan"), P("seq", "chan"), P(), P(), P(), P(), P(), P(None, "chan"), P("chan"),
            P("chan"), P("chan", None),
        ),
        out_specs=P("chan", "seq"),
        check_vma=False,
    )
```

```python
import functools
import math

import jax
import jax.numpy as jnp
import numpy as np
from jax import lax
from jax.experimental import pallas as pl
from jax.experimental.pallas import tpu as pltpu
from jax.sharding import PartitionSpec as P

GROUP = 128
LANES = 128
SINE_FREQ = 2.0
F32 = jnp.float32
BF16 = jnp.bfloat16


def packed_tables(block):
    period = 2 * block
    row = np.arange(block)
    freq = np.arange(block)

    def forward(shift):
        angle = 2.0 * np.pi * (freq[:, None] * (row[None, :] + shift) % period) / period
        real, imag = np.cos(angle), -np.sin(angle)
        imag[0] = np.where((row + shift) % 2 == 0, 1.0, -1.0)
        return np.concatenate([real, imag], 0)

    head, tail = forward(0), forward(block)
    tail[:, 0] = 0.0
    weight = np.where(freq == 0, 1.0, 2.0) / period
    angle = 2.0 * np.pi * (row[:, None] * freq[None, :] % period) / period
    real, imag = np.cos(angle) * weight, -np.sin(angle) * weight
    imag[:, 0] = np.where(row % 2 == 0, 1.0, -1.0) / period
    inverse = np.concatenate([real, imag], 1)
    to_bf16 = lambda table: jnp.asarray(table.astype(np.float32)).astype(BF16)
    return to_bf16(head), to_bf16(np.concatenate([head, tail], 1)), to_bf16(inverse)


def feature_table(length, bands, rows):
    lag = np.arange(length)
    angle = 2.0 * np.pi * (np.arange(1, bands + 1)[:, None] * lag[None, :] % length) / length
    table = np.zeros((rows, length), np.float32)
    table[0] = lag / length
    table[1 : bands + 1] = np.cos(angle)
    table[bands + 1 : 2 * bands + 1] = np.sin(angle)
    table[2 * bands + 1] = 1.0
    return jnp.asarray(table)


def sine(x):
    n = jnp.round(x * (1.0 / math.pi))
    r = x - n * 3.140625
    r = r - n * 9.67502593994140625e-4
    r = r - n * 1.509957990978376432e-7
    square = r * r
    series = jnp.full_like(r, -2.5052108e-8)
    for term in (2.7557319e-6, -1.9841270e-4, 8.3333333e-3, -1.6666667e-1):
        series = series * square + term
    odd = n * 0.5 - jnp.floor(n * 0.5)
    return (r + r * square * series) * (1.0 - 4.0 * odd)


def contract_first(lhs, rhs):
    return lax.dot_general(
        lhs, rhs, (((0,), (0,)), ((), ())), precision=lax.Precision.HIGHEST, preferred_element_type=F32
    )


def first_piece(pieces):
    return lax.axis_index("seq") if pieces > 1 else 0


def weight_copies(blocks, pieces, weight_hbm, weight_out, sem):
    _, depth, width = weight_out.shape
    unit = depth // pieces
    copies = []
    for i, j in enumerate(blocks):
        cols = pl.ds(pl.multiple_of((lax.axis_index("chan") ^ j) * width, LANES), width)
        for k in range(pieces):
            rows = pl.ds(pl.multiple_of((first_piece(pieces) ^ k) * unit, LANES), unit)
            target = weight_out.at[i, k * unit : (k + 1) * unit]
            copies.append(pltpu.make_async_copy(weight_hbm.at[rows, cols], target, sem.at[i, k]))
    return copies


def one_minus_exp(y):
    series = jnp.full_like(y, -1.0 / 40320)
    for term in (5040, -720, 120, -24, 6, -2, 1):
        series = series * y + 1.0 / term
    return jnp.where(y < 0.5, y * series, 1.0 - jnp.exp(-y))


def filter_kernel(block, blocks_first, out_w_ref, *refs):
    smalls, (weight_hbm, query_hbm), refs = refs[:8], refs[8:10], refs[10:]
    (real_ref, imag_ref, edge_ref, weight_out, query_out, gain_out), refs = refs[:6], refs[6:]
    near, (w1, w2, hid, filt, near_sem, weight_sem, query_sem) = refs[:8], refs[8:]
    feat_ref, emb_w_ref, emb_b_ref, mid_w_ref, mid_b_ref, gain_ref, decay_all, table_ref = near
    fetches = [pltpu.make_async_copy(s, t, near_sem.at[i]) for i, (s, t) in enumerate(zip(smalls, near))]
    for fetch in fetches:
        fetch.start()
    pieces, _, unit = query_out.shape
    first = first_piece(pieces)
    copies = weight_copies(blocks_first, pieces, weight_hbm, weight_out, weight_sem)
    for k in range(pieces):
        cols = pl.ds(pl.multiple_of((first ^ k) * unit, LANES), unit)
        copies.append(pltpu.make_async_copy(query_hbm.at[:, cols], query_out.at[k], query_sem.at[k]))
    for fetch in fetches:
        fetch.wait()
    for copy in copies:
        copy.start()
    for k in range(pieces):
        gain_out[k : k + 1, :] = gain_ref[pl.ds(first ^ k, 1), :]
    emb, order = emb_w_ref.shape
    length = feat_ref.shape[1]
    blocks = length // block
    w1[...] = jnp.zeros_like(w1)
    w1[0:emb, :] = emb_w_ref[...]
    w1[emb : emb + 1, :] = emb_b_ref[...]
    w2[...] = jnp.zeros_like(w2)
    w2[0:order, :] = mid_w_ref[...]
    w2[order : order + 1, :] = mid_b_ref[...]
    hid[order:, :] = jnp.ones_like(hid[order:, :])
    hid[0:order, :] = sine(SINE_FREQ * contract_first(w1[...], feat_ref[...]))
    hidden = sine(SINE_FREQ * contract_first(w2[...], hid[...]))
    raw = contract_first(hidden, out_w_ref[...])
    decay = decay_all[pl.ds(first, 1), :]
    within = jnp.exp(-decay * lax.broadcasted_iota(jnp.int32, (block, LANES), 0).astype(F32))
    within = within * jnp.sqrt(one_minus_exp(2.0 * decay))
    filt[0:block, :] = jnp.zeros((block, LANES), BF16)
    for m in range(blocks):
        start = jnp.exp(-decay * float(m * block))
        filt[(m + 1) * block : (m + 2) * block, :] = (raw[m * block : (m + 1) * block] * (within * start)).astype(BF16)
    first_row = lax.broadcasted_iota(jnp.int32, (16, LANES), 0) == 0
    group = 2
    for m0 in range(0, blocks, group):
        stacked = jnp.concatenate(
            [
                jnp.concatenate(
                    [filt[(m + 1) * block : (m + 2) * block, :], filt[m * block : (m + 1) * block, :]], 0
                )
                for m in range(m0, m0 + group)
            ],
            1,
        )
        spectrum = jnp.dot(table_ref[...], stacked, preferred_element_type=F32)
        for i in range(group):
            m = m0 + i
            real = spectrum[:block, i * LANES : (i + 1) * LANES]
            imag = spectrum[block:, i * LANES : (i + 1) * LANES]
            real_ref[m] = real
            imag_ref[m] = imag
            edge_ref[m] = jnp.where(first_row, imag[:16], real[:16])
            imag_ref[m, 0:16, :] = jnp.where(first_row, 0.0, imag[:16])
    for copy in copies:
        copy.wait()


def conv_kernel(
    block, blocks_next, relative, order_ref, real_ref, imag_ref, edge_ref, table_ref, inverse_ref, weight_hbm, *refs
):
    *refs, weight_out, sig, sre, sim, spec, conv, weight_sem = refs
    count = len(refs) // 2
    x_refs, out_refs = refs[:count], refs[count:]
    pieces = count if relative else 1
    first = first_piece(pieces)
    copies = weight_copies(blocks_next, pieces, weight_hbm, weight_out, weight_sem)
    for copy in copies:
        copy.start()
    groups = x_refs[0].shape[0] // GROUP
    length = sig.shape[0]
    blocks = length // block

    def place(k, i):
        return pl.multiple_of(order_ref[(first ^ k) * groups + i] * GROUP, GROUP)

    for k, x_ref in enumerate(x_refs):
        for i in range(groups):
            sig[pl.ds(place(k, i), GROUP), :] = x_ref[i * GROUP : (i + 1) * GROUP, :]
    group = 2
    for b0 in range(0, blocks, group):
        stacked = jnp.concatenate([sig[b * block : (b + 1) * block, :] for b in range(b0, b0 + group)], 1)
        spectrum = jnp.dot(table_ref[...], stacked, preferred_element_type=F32)
        for i in range(group):
            sre[b0 + i] = spectrum[:block, i * LANES : (i + 1) * LANES]
            sim[b0 + i] = spectrum[block:, i * LANES : (i + 1) * LANES]

    def tile(start, first):
        rows = pl.ds(start, 16)
        mirror = pl.ds(block + start, 16)
        s_real = [sre[q, rows, :] for q in range(blocks)]
        s_imag = [sim[q, rows, :] for q in range(blocks)]
        for g in range(blocks):
            acc_real = acc_imag = None
            for q in range(g + 1):
                fr, fi = real_ref[g - q, rows, :], imag_ref[g - q, rows, :]
                fe = edge_ref[g - q] if first else fr
                re = fr * s_real[q] - fi * s_imag[q]
                im = fe * s_imag[q] + fi * s_real[q]
                acc_real = re if q == 0 else acc_real + re
                acc_imag = im if q == 0 else acc_imag + im
            spec[rows, g * LANES : (g + 1) * LANES] = acc_real.astype(BF16)
            spec[mirror, g * LANES : (g + 1) * LANES] = acc_imag.astype(BF16)

    tile(0, True)

    @pl.loop(1, block // 16)
    def _(t):
        tile(pl.multiple_of(t * 16, 16), False)

    result = jnp.dot(inverse_ref[...], spec[...], preferred_element_type=F32)
    for g in range(blocks):
        conv[g * block : (g + 1) * block, :] = result[:, g * LANES : (g + 1) * LANES].astype(BF16)
    for k, out_ref in enumerate(out_refs):
        for i in range(groups):
            out_ref[i * GROUP : (i + 1) * GROUP, :] = conv[pl.ds(place(k, i), GROUP), :]
    for copy in copies:
        copy.wait()


def mix_kernel(query_ref, gain_ref, weight_ref, *refs):
    *refs, out_ref, mixed_ref = refs
    count = len(refs) // 2
    unit = query_ref.shape[2]
    for k, (back_ref, sig_ref) in enumerate(zip(refs[:count], refs[count:])):
        inner = back_ref[...].astype(F32) + gain_ref[k : k + 1, :] * sig_ref[...].astype(F32)
        mixed_ref[:, k * unit : (k + 1) * unit] = (query_ref[k].astype(F32) * inner).astype(BF16)
    project_kernel(0, mixed_ref, weight_ref, out_ref)


def project_kernel(first, mixed_ref, weight_ref, out_ref):
    mixed = mixed_ref[...]
    for i in range(out_ref.shape[0]):
        out_ref[i] = jnp.dot(mixed, weight_ref[first + i], preferred_element_type=F32).astype(out_ref.dtype)


def last_kernel(blocks_last, pieces, mixed_ref, weight_hbm, out_ref, weight_near, sem):
    copies = weight_copies(blocks_last, pieces, weight_hbm, weight_near, sem)
    for copy in copies:
        copy.start()
    for copy in copies:
        copy.wait()
    project_kernel(0, mixed_ref, weight_near, out_ref)


def finish_kernel(part, spans, count, *refs):
    operands, (out_hbm, turned, sem) = refs[: count + len(spans)], refs[-3:]
    rows = turned.shape[1]
    first, last = part * rows, (part + 1) * rows
    total = jnp.concatenate(
        [
            ref[max(first, start) - start : min(last, stop) - start, :].astype(F32)
            for ref, (start, stop) in zip(operands[count:], spans)
        ],
        0,
    )
    for ref in operands[:count]:
        total = total + ref[first:last, :].astype(F32)
    turned[...] = total.T
    copy = pltpu.make_async_copy(turned, out_hbm.at[:, first:last], sem.at[0])
    copy.start()
    copy.wait()


def gated_kernel(key_hbm, value_hbm, *refs):
    *out_refs, key_ref, value_ref, sem = refs
    pieces = len(out_refs)
    unit = out_refs[0].shape[1]
    copies = []
    for k in range(pieces):
        cols = pl.ds(pl.multiple_of((first_piece(pieces) ^ k) * unit, LANES), unit)
        copies.append(pltpu.make_async_copy(key_hbm.at[:, cols], key_ref.at[k], sem.at[0, k]))
        copies.append(pltpu.make_async_copy(value_hbm.at[:, cols], value_ref.at[k], sem.at[1, k]))
    for copy in copies:
        copy.start()
    for k, out_ref in enumerate(out_refs):
        copies[2 * k].wait()
        copies[2 * k + 1].wait()
        out_ref[...] = (key_ref[k].astype(F32) * value_ref[k].astype(F32)).astype(BF16)


def local(
    query, key_gate, value, group_order, emb_weight, emb_bias, mid_weight, mid_bias, out_filter, decay_rate, skip_gain,
    out_weight,
):
    rows, chan_width = query.shape
    seq_count, chan_count = lax.axis_size("seq"), lax.axis_size("chan")
    seq_index, chan_index = lax.axis_index("seq"), lax.axis_index("chan")
    length = rows * seq_count
    slots = length // GROUP
    width = chan_width // seq_count
    block = max(2 * GROUP, length // 16)
    blocks = length // block
    emb, order = emb_weight.shape
    head, head_tail, inverse = packed_tables(block)
    feat_rows = -(-(emb + 1) // 8) * 8
    features = feature_table(length, (emb - 1) // 2, feat_rows)

    limit = pltpu.CompilerParams(vmem_limit_bytes=20 << 20)
    in_vmem = pl.BlockSpec(memory_space=pltpu.VMEM)
    in_smem = pl.BlockSpec(memory_space=pltpu.SMEM)
    in_hbm = pl.BlockSpec(memory_space=pltpu.HBM)
    far = lambda operand: pltpu.with_memory_space_constraint(operand, pltpu.HBM)
    unit = width if width % LANES == 0 else chan_width
    pieces = chan_width // unit

    def swap(arrays):
        return [arrays[0]] + [
            lax.ppermute(arrays[k], "seq", [(d, d ^ k) for d in range(seq_count)]) for k in range(1, seq_count)
        ]

    signal = pl.pallas_call(
        gated_kernel,
        out_shape=[jax.ShapeDtypeStruct((rows, unit), BF16)] * pieces,
        in_specs=[in_hbm] * 2,
        out_specs=[in_vmem] * pieces,
        scratch_shapes=[
            pltpu.VMEM((pieces, rows, unit), BF16),
            pltpu.VMEM((pieces, rows, unit), BF16),
            pltpu.SemaphoreType.DMA((2, pieces)),
        ],
        compiler_params=limit,
    )(far(key_gate), far(value))
    if pieces > 1:
        spread = swap(signal)
    else:
        in_order = signal[0].reshape(rows, seq_count, width).transpose(1, 0, 2)
        in_order = lax.all_to_all(in_order, "seq", 0, 0, tiled=True)
        spread = list(jnp.pad(in_order, [(0, 0), (0, 0), (0, LANES - width)]))

    my_filter = lax.dynamic_slice_in_dim(out_filter, seq_index * width, width, 1)
    decay = decay_rate.reshape(seq_count, width)
    if pieces == 1:
        pad = [(0, 0), (0, LANES - width)]
        my_filter = jnp.pad(my_filter, pad)
        decay = jnp.pad(lax.dynamic_slice_in_dim(decay, seq_index, 1), pad)
    out_width = out_weight.shape[1] // chan_count
    quarter = chan_count // 4
    odd = range(1, chan_count, 2)
    far_odd, near_odd = [j for j in odd if j & 2], [j for j in odd if not j & 2]
    blocks_first, blocks_next, blocks_last = far_odd + [j ^ 1 for j in far_odd], near_odd, [j ^ 1 for j in near_odd]
    smalls = (
        features, emb_weight, emb_bias[None, :], mid_weight, mid_bias[None, :], skip_gain.reshape(pieces, unit), decay,
        head_tail,
    )
    real, imag, edge, weights_first, query_near, gain_near = pl.pallas_call(
        functools.partial(filter_kernel, block, blocks_first),
        out_shape=(
            jax.ShapeDtypeStruct((blocks, block, LANES), F32),
            jax.ShapeDtypeStruct((blocks, block, LANES), F32),
            jax.ShapeDtypeStruct((blocks, 16, LANES), F32),
            jax.ShapeDtypeStruct((2 * quarter, chan_width, out_width), BF16),
            jax.ShapeDtypeStruct((pieces, rows, unit), BF16),
            jax.ShapeDtypeStruct((pieces, unit), F32),
        ),
        in_specs=[in_vmem] + [in_hbm] * 10,
        out_specs=[in_vmem] * 6,
        scratch_shapes=[
            *[pltpu.VMEM(small.shape, small.dtype) for small in smalls],
            pltpu.VMEM((feat_rows, order), F32),
            pltpu.VMEM((order + 8, order), F32),
            pltpu.VMEM((order + 8, length), F32),
            pltpu.VMEM((length + block, LANES), BF16),
            pltpu.SemaphoreType.DMA((len(smalls),)),
            pltpu.SemaphoreType.DMA((2 * quarter, pieces)),
            pltpu.SemaphoreType.DMA((pieces,)),
        ],
        compiler_params=limit,
    )(my_filter, *map(far, (*smalls, out_weight, query)))

    *convolved, weights_next = pl.pallas_call(
        functools.partial(conv_kernel, block, blocks_next, pieces > 1),
        out_shape=[
            *[jax.ShapeDtypeStruct((rows, LANES), BF16)] * seq_count,
            jax.ShapeDtypeStruct((quarter, chan_width, out_width), BF16),
        ],
        in_specs=[in_smem] + [in_vmem] * 5 + [in_hbm] + [in_vmem] * seq_count,
        out_specs=[in_vmem] * (seq_count + 1),
        scratch_shapes=[
            pltpu.VMEM((length, LANES), BF16),
            pltpu.VMEM((blocks, block, LANES), F32),
            pltpu.VMEM((blocks, block, LANES), F32),
            pltpu.VMEM((2 * block, blocks * LANES), BF16),
            pltpu.VMEM((length, LANES), BF16),
            pltpu.SemaphoreType.DMA((quarter, pieces)),
        ],
        compiler_params=limit,
    )(group_order, real, imag, edge, head, inverse, far(out_weight), *spread)
    if pieces > 1:
        backs = swap(convolved)
    else:
        in_order = lax.all_to_all(jnp.stack([piece[:, :width] for piece in convolved]), "seq", 0, 0, tiled=True)
        backs = [in_order.transpose(1, 0, 2).reshape(rows, chan_width)]

    def exchange(terms, bit):
        return lax.ppermute(terms, "chan", [(d, d ^ bit) for d in range(chan_count)])

    far_away, mixed = pl.pallas_call(
        mix_kernel,
        out_shape=(
            jax.ShapeDtypeStruct((quarter, rows, out_width), BF16),
            jax.ShapeDtypeStruct((rows, chan_width), BF16),
        ),
        in_specs=[in_vmem] * (3 + 2 * pieces),
        out_specs=[in_vmem] * 2,
        compiler_params=limit,
    )(query_near, gain_near, weights_first, *backs, *signal)
    far_terms = exchange(far_away, 1)

    def products(first, weights, dtype):
        return pl.pallas_call(
            functools.partial(project_kernel, first),
            out_shape=jax.ShapeDtypeStruct((quarter, rows, out_width), dtype),
            in_specs=[in_vmem] * 2,
            out_specs=in_vmem,
            compiler_params=limit,
        )(mixed, weights)

    far_kept, near_away = products(quarter, weights_first, F32), products(0, weights_next, BF16)
    cuts = [0, rows // 2, rows]
    spans = list(zip(cuts, cuts[1:]))
    send = [(far_kept[:, a:b] + far_terms[:, a:b].astype(F32)).astype(BF16) for a, b in spans]
    send, near_away, mixed = lax.optimization_barrier((send, near_away, mixed))
    sent = [exchange(piece, 2) for piece in send]
    near_terms = exchange(near_away, 1)
    near_kept = pl.pallas_call(
        functools.partial(last_kernel, blocks_last, pieces),
        out_shape=jax.ShapeDtypeStruct((quarter, rows, out_width), F32),
        in_specs=[in_vmem, in_hbm],
        out_specs=in_vmem,
        scratch_shapes=[
            pltpu.VMEM((quarter, chan_width, out_width), BF16),
            pltpu.SemaphoreType.DMA((quarter, pieces)),
        ],
        compiler_params=limit,
    )(mixed, far(out_weight))
    terms = [near_kept, near_terms]
    bit = 4
    while bit < chan_count:
        total = terms[0] + terms[1].astype(F32) + jnp.concatenate(sent, 1).astype(F32)
        sent, spans = [exchange(total[1::2].astype(BF16), bit)], [(0, rows)]
        terms = [total[0::2], jnp.zeros_like(total[0::2])]
        bit *= 2
    result = None
    for i in range(rows // GROUP):
        held = [j for j, (a, b) in enumerate(spans) if a < (i + 1) * GROUP and b > i * GROUP]
        operands = [term[0] for term in terms] + [sent[j][0] for j in held]
        extra = [] if result is None else [result]
        result = pl.pallas_call(
            functools.partial(finish_kernel, i, [spans[j] for j in held], len(terms)),
            out_shape=jax.ShapeDtypeStruct((out_width, rows), F32),
            in_specs=[in_vmem] * len(operands) + [in_hbm] * len(extra),
            out_specs=in_hbm,
            scratch_shapes=[pltpu.VMEM((out_width, GROUP), F32), pltpu.SemaphoreType.DMA((1,))],
            input_output_aliases={len(operands): 0} if extra else {},
            compiler_params=limit,
        )(*operands, *extra)
    return result


def solution(mesh):
    return jax.shard_map(
        local,
        mesh=mesh,
        in_specs=(
            P("seq", "chan"), P("seq", "chan"), P("seq", "chan"), P(), P(), P(), P(), P(), P(None, "chan"), P("chan"),
            P("chan"), P("chan", None),
        ),
        out_specs=P("chan", "seq"),
        check_vma=False,
    )
```

```python
import functools
import math

import jax
import jax.numpy as jnp
import numpy as np
from jax import lax
from jax.experimental import pallas as pl
from jax.experimental.pallas import tpu as pltpu
from jax.sharding import PartitionSpec as P

GROUP = 128
LANES = 128
SINE_FREQ = 2.0
F32 = jnp.float32
BF16 = jnp.bfloat16


def packed_tables(block):
    period = 2 * block
    row = np.arange(block)
    freq = np.arange(block)

    def forward(shift):
        angle = 2.0 * np.pi * (freq[:, None] * (row[None, :] + shift) % period) / period
        real, imag = np.cos(angle), -np.sin(angle)
        imag[0] = np.where((row + shift) % 2 == 0, 1.0, -1.0)
        return np.concatenate([real, imag], 0)

    head, tail = forward(0), forward(block)
    tail[:, 0] = 0.0
    weight = np.where(freq == 0, 1.0, 2.0) / period
    angle = 2.0 * np.pi * (row[:, None] * freq[None, :] % period) / period
    real, imag = np.cos(angle) * weight, -np.sin(angle) * weight
    imag[:, 0] = np.where(row % 2 == 0, 1.0, -1.0) / period
    inverse = np.concatenate([real, imag], 1)
    to_bf16 = lambda table: jnp.asarray(table.astype(np.float32)).astype(BF16)
    return to_bf16(head), to_bf16(np.concatenate([head, tail], 1)), to_bf16(inverse)


def feature_table(length, bands, rows):
    lag = np.arange(length)
    angle = 2.0 * np.pi * (np.arange(1, bands + 1)[:, None] * lag[None, :] % length) / length
    table = np.zeros((rows, length), np.float32)
    table[0] = lag / length
    table[1 : bands + 1] = np.cos(angle)
    table[bands + 1 : 2 * bands + 1] = np.sin(angle)
    table[2 * bands + 1] = 1.0
    return jnp.asarray(table)


def sine(x):
    n = jnp.round(x * (1.0 / math.pi))
    r = x - n * 3.140625
    r = r - n * 9.67502593994140625e-4
    r = r - n * 1.509957990978376432e-7
    square = r * r
    series = jnp.full_like(r, -2.5052108e-8)
    for term in (2.7557319e-6, -1.9841270e-4, 8.3333333e-3, -1.6666667e-1):
        series = series * square + term
    odd = n * 0.5 - jnp.floor(n * 0.5)
    return (r + r * square * series) * (1.0 - 4.0 * odd)


def contract_first(lhs, rhs):
    return lax.dot_general(
        lhs, rhs, (((0,), (0,)), ((), ())), precision=lax.Precision.HIGHEST, preferred_element_type=F32
    )


def first_piece(pieces):
    return lax.axis_index("seq") if pieces > 1 else 0


def weight_copies(blocks, weight_hbm, weight_out, sem):
    width = weight_out.shape[2]
    copies = []
    for i, j in enumerate(blocks):
        cols = pl.ds(pl.multiple_of((lax.axis_index("chan") ^ j) * width, LANES), width)
        copies.append(pltpu.make_async_copy(weight_hbm.at[:, cols], weight_out.at[i], sem.at[i]))
    return copies


def one_minus_exp(y):
    series = jnp.full_like(y, -1.0 / 40320)
    for term in (5040, -720, 120, -24, 6, -2, 1):
        series = series * y + 1.0 / term
    return jnp.where(y < 0.5, y * series, 1.0 - jnp.exp(-y))


def filter_kernel(block, blocks_first, relative, out_w_ref, *refs):
    smalls, (weight_hbm, query_hbm), refs = refs[:7], refs[7:9], refs[9:]
    (real_ref, imag_ref, edge_ref, weight_out, query_out), refs = refs[:5], refs[5:]
    near, (w1, w2, hid, filt, near_sem, weight_sem, query_sem) = refs[:7], refs[7:]
    feat_ref, emb_w_ref, emb_b_ref, mid_w_ref, mid_b_ref, decay_all, table_ref = near
    fetches = [pltpu.make_async_copy(s, t, near_sem.at[i]) for i, (s, t) in enumerate(zip(smalls, near))]
    for fetch in fetches:
        fetch.start()
    for fetch in fetches[:-1]:
        fetch.wait()
    copies = weight_copies(blocks_first, weight_hbm, weight_out, weight_sem)
    copies.append(pltpu.make_async_copy(query_hbm, query_out, query_sem.at[0]))
    for copy in copies:
        copy.start()
    emb, order = emb_w_ref.shape
    length = feat_ref.shape[1]
    blocks = length // block
    w1[...] = jnp.zeros_like(w1)
    w1[0:emb, :] = emb_w_ref[...]
    w1[emb : emb + 1, :] = emb_b_ref[...]
    w2[...] = jnp.zeros_like(w2)
    w2[0:order, :] = mid_w_ref[...]
    w2[order : order + 1, :] = mid_b_ref[...]
    hid[order:, :] = jnp.ones_like(hid[order:, :])
    hid[0:order, :] = sine(SINE_FREQ * contract_first(w1[...], feat_ref[...]))
    hidden = sine(SINE_FREQ * contract_first(w2[...], hid[...]))
    raw = contract_first(out_w_ref[...], hidden).T
    decay = decay_all[pl.ds(lax.axis_index("seq") if relative else 0, 1), :]
    within = jnp.exp(-decay * lax.broadcasted_iota(jnp.int32, (block, LANES), 0).astype(F32))
    within = within * jnp.sqrt(one_minus_exp(2.0 * decay))
    filt[0:block, :] = jnp.zeros((block, LANES), BF16)
    for m in range(blocks):
        start = jnp.exp(-decay * float(m * block))
        filt[(m + 1) * block : (m + 2) * block, :] = (raw[m * block : (m + 1) * block] * (within * start)).astype(BF16)
    first_row = lax.broadcasted_iota(jnp.int32, (16, LANES), 0) == 0
    fetches[-1].wait()
    group = 2
    for m0 in range(0, blocks, group):
        stacked = jnp.concatenate(
            [
                jnp.concatenate(
                    [filt[(m + 1) * block : (m + 2) * block, :], filt[m * block : (m + 1) * block, :]], 0
                )
                for m in range(m0, m0 + group)
            ],
            1,
        )
        spectrum = jnp.dot(table_ref[...], stacked, preferred_element_type=F32)
        for i in range(group):
            m = m0 + i
            real = spectrum[:block, i * LANES : (i + 1) * LANES]
            imag = spectrum[block:, i * LANES : (i + 1) * LANES]
            real_ref[m] = real
            imag_ref[m] = imag
            edge_ref[m] = jnp.where(first_row, imag[:16], real[:16])
            imag_ref[m, 0:16, :] = jnp.where(first_row, 0.0, imag[:16])
    for copy in copies:
        copy.wait()


def conv_kernel(
    block, blocks_next, relative, order_ref, real_ref, imag_ref, edge_ref, table_ref, inverse_ref, weight_hbm, *refs
):
    *refs, weight_out, sig, sre, sim, spec, conv, weight_sem = refs
    count = len(refs) // 2
    x_refs, out_refs = refs[:count], refs[count:]
    first = first_piece(count if relative else 1)
    copies = weight_copies(blocks_next, weight_hbm, weight_out, weight_sem)
    for copy in copies:
        copy.start()
    groups = x_refs[0].shape[0] // GROUP
    length = sig.shape[0]
    blocks = length // block

    def place(k, i):
        return pl.multiple_of(order_ref[(first ^ k) * groups + i] * GROUP, GROUP)

    for k, x_ref in enumerate(x_refs):
        for i in range(groups):
            sig[pl.ds(place(k, i), GROUP), :] = x_ref[i * GROUP : (i + 1) * GROUP, :]
    group = 2
    for b0 in range(0, blocks, group):
        stacked = jnp.concatenate([sig[b * block : (b + 1) * block, :] for b in range(b0, b0 + group)], 1)
        spectrum = jnp.dot(table_ref[...], stacked, preferred_element_type=F32)
        for i in range(group):
            sre[b0 + i] = spectrum[:block, i * LANES : (i + 1) * LANES]
            sim[b0 + i] = spectrum[block:, i * LANES : (i + 1) * LANES]

    def tile(start, first):
        rows = pl.ds(start, 16)
        mirror = pl.ds(block + start, 16)
        s_real = [sre[q, rows, :] for q in range(blocks)]
        s_imag = [sim[q, rows, :] for q in range(blocks)]
        for g in range(blocks):
            acc_real = acc_imag = None
            for q in range(g + 1):
                fr, fi = real_ref[g - q, rows, :], imag_ref[g - q, rows, :]
                fe = edge_ref[g - q] if first else fr
                re = fr * s_real[q] - fi * s_imag[q]
                im = fe * s_imag[q] + fi * s_real[q]
                acc_real = re if q == 0 else acc_real + re
                acc_imag = im if q == 0 else acc_imag + im
            spec[rows, g * LANES : (g + 1) * LANES] = acc_real.astype(BF16)
            spec[mirror, g * LANES : (g + 1) * LANES] = acc_imag.astype(BF16)

    tile(0, True)

    @pl.loop(1, block // 16)
    def _(t):
        tile(pl.multiple_of(t * 16, 16), False)

    result = jnp.dot(inverse_ref[...], spec[...], preferred_element_type=F32)
    for g in range(blocks):
        conv[g * block : (g + 1) * block, :] = result[:, g * LANES : (g + 1) * LANES].astype(BF16)
    for k, out_ref in enumerate(out_refs):
        for i in range(groups):
            out_ref[i * GROUP : (i + 1) * GROUP, :] = conv[pl.ds(place(k, i), GROUP), :]
    for copy in copies:
        copy.wait()


def mix_kernel(query_ref, gain_ref, weight_ref, *refs):
    *refs, out_ref, mixed_ref = refs
    pieces = len(refs) // 2
    unit = refs[0].shape[1]
    for k, (back_ref, sig_ref) in enumerate(zip(refs[:pieces], refs[pieces:])):
        cols = pl.ds(pl.multiple_of((first_piece(pieces) ^ k) * unit, LANES), unit)
        inner = back_ref[...].astype(F32) + gain_ref[:, cols] * sig_ref[...].astype(F32)
        mixed_ref[:, cols] = (query_ref[:, cols].astype(F32) * inner).astype(BF16)
    project_kernel(0, mixed_ref, weight_ref, out_ref)


def project_kernel(first, mixed_ref, weight_ref, out_ref):
    mixed = mixed_ref[...]
    for i in range(out_ref.shape[0]):
        out_ref[i] = jnp.dot(mixed, weight_ref[first + i], preferred_element_type=F32).astype(out_ref.dtype)


def last_kernel(blocks_last, mixed_ref, weight_hbm, out_ref, weight_near, sem):
    copies = weight_copies(blocks_last, weight_hbm, weight_near, sem)
    for copy in copies:
        copy.start()
    for copy in copies:
        copy.wait()
    project_kernel(0, mixed_ref, weight_near, out_ref)


def finish_kernel(span, count, *refs):
    (*held, arrived), (out_hbm, turned, sem) = refs[: count + 1], refs[-3:]
    first, last = span
    total = arrived[...].astype(F32)
    for ref in held:
        total = total + ref[:, first:last].astype(F32)
    turned[...] = total.T
    copy = pltpu.make_async_copy(turned, out_hbm.at[first:last], sem.at[0])
    copy.start()
    copy.wait()


def gated_kernel(key_hbm, value_hbm, *refs):
    *out_refs, key_ref, value_ref, sem = refs
    pieces = len(out_refs)
    unit = out_refs[0].shape[1]
    copies = []
    for k in range(pieces):
        cols = pl.ds(pl.multiple_of((first_piece(pieces) ^ k) * unit, LANES), unit)
        copies.append(pltpu.make_async_copy(key_hbm.at[:, cols], key_ref.at[k], sem.at[0, k]))
        copies.append(pltpu.make_async_copy(value_hbm.at[:, cols], value_ref.at[k], sem.at[1, k]))
    for copy in copies:
        copy.start()
    for k, out_ref in enumerate(out_refs):
        copies[2 * k].wait()
        copies[2 * k + 1].wait()
        out_ref[...] = (key_ref[k].astype(F32) * value_ref[k].astype(F32)).astype(BF16)


def local(
    query, key_gate, value, group_order, emb_weight, emb_bias, mid_weight, mid_bias, out_filter, decay_rate, skip_gain,
    out_weight,
):
    rows, chan_width = query.shape
    seq_count, chan_count = lax.axis_size("seq"), lax.axis_size("chan")
    seq_index, chan_index = lax.axis_index("seq"), lax.axis_index("chan")
    length = rows * seq_count
    slots = length // GROUP
    width = chan_width // seq_count
    block = max(2 * GROUP, length // 16)
    blocks = length // block
    emb, order = emb_weight.shape
    head, head_tail, inverse = packed_tables(block)
    feat_rows = -(-(emb + 1) // 8) * 8
    features = feature_table(length, (emb - 1) // 2, feat_rows)

    limit = pltpu.CompilerParams(vmem_limit_bytes=20 << 20)
    in_vmem = pl.BlockSpec(memory_space=pltpu.VMEM)
    in_smem = pl.BlockSpec(memory_space=pltpu.SMEM)
    in_hbm = pl.BlockSpec(memory_space=pltpu.HBM)
    far = lambda operand: pltpu.with_memory_space_constraint(operand, pltpu.HBM)
    unit = width if width % LANES == 0 else chan_width
    pieces = chan_width // unit

    def swap(arrays):
        return [arrays[0]] + [
            lax.ppermute(arrays[k], "seq", [(d, d ^ k) for d in range(seq_count)]) for k in range(1, seq_count)
        ]

    signal = pl.pallas_call(
        gated_kernel,
        out_shape=[jax.ShapeDtypeStruct((rows, unit), BF16)] * pieces,
        in_specs=[in_hbm] * 2,
        out_specs=[in_vmem] * pieces,
        scratch_shapes=[
            pltpu.VMEM((pieces, rows, unit), BF16),
            pltpu.VMEM((pieces, rows, unit), BF16),
            pltpu.SemaphoreType.DMA((2, pieces)),
        ],
        compiler_params=limit,
    )(far(key_gate), far(value))
    if pieces > 1:
        spread = swap(signal)
    else:
        in_order = signal[0].reshape(rows, seq_count, width).transpose(1, 0, 2)
        in_order = lax.all_to_all(in_order, "seq", 0, 0, tiled=True)
        spread = list(jnp.pad(in_order, [(0, 0), (0, 0), (0, LANES - width)]))

    my_filter = lax.dynamic_slice_in_dim(out_filter, seq_index * width, width, 1)
    decay = decay_rate.reshape(seq_count, width)
    if pieces == 1:
        pad = [(0, 0), (0, LANES - width)]
        my_filter = jnp.pad(my_filter, pad)
        decay = jnp.pad(lax.dynamic_slice_in_dim(decay, seq_index, 1), pad)
    out_width = out_weight.shape[1] // chan_count
    quarter = chan_count // 4
    odd = range(1, chan_count, 2)
    far_odd, near_odd = [j for j in odd if j & 2], [j for j in odd if not j & 2]
    blocks_first, blocks_next, blocks_last = far_odd + [j ^ 1 for j in far_odd], near_odd, [j ^ 1 for j in near_odd]
    smalls = (
        features, emb_weight, emb_bias[None, :], mid_weight, mid_bias[None, :], decay, head_tail,
    )
    real, imag, edge, weights_first, query_near = pl.pallas_call(
        functools.partial(filter_kernel, block, blocks_first, pieces > 1),
        out_shape=(
            jax.ShapeDtypeStruct((blocks, block, LANES), F32),
            jax.ShapeDtypeStruct((blocks, block, LANES), F32),
            jax.ShapeDtypeStruct((blocks, 16, LANES), F32),
            jax.ShapeDtypeStruct((2 * quarter, chan_width, out_width), BF16),
            jax.ShapeDtypeStruct(query.shape, BF16),
        ),
        in_specs=[in_vmem] + [in_hbm] * 9,
        out_specs=[in_vmem] * 5,
        scratch_shapes=[
            *[pltpu.VMEM(small.shape, small.dtype) for small in smalls],
            pltpu.VMEM((feat_rows, order), F32),
            pltpu.VMEM((order + 8, order), F32),
            pltpu.VMEM((order + 8, length), F32),
            pltpu.VMEM((length + block, LANES), BF16),
            pltpu.SemaphoreType.DMA((len(smalls),)),
            pltpu.SemaphoreType.DMA((2 * quarter,)),
            pltpu.SemaphoreType.DMA((1,)),
        ],
        compiler_params=limit,
    )(my_filter, *map(far, (*smalls, out_weight, query)))

    *convolved, weights_next = pl.pallas_call(
        functools.partial(conv_kernel, block, blocks_next, pieces > 1),
        out_shape=[
            *[jax.ShapeDtypeStruct((rows, LANES), BF16)] * seq_count,
            jax.ShapeDtypeStruct((quarter, chan_width, out_width), BF16),
        ],
        in_specs=[in_smem] + [in_vmem] * 5 + [in_hbm] + [in_vmem] * seq_count,
        out_specs=[in_vmem] * (seq_count + 1),
        scratch_shapes=[
            pltpu.VMEM((length, LANES), BF16),
            pltpu.VMEM((blocks, block, LANES), F32),
            pltpu.VMEM((blocks, block, LANES), F32),
            pltpu.VMEM((2 * block, blocks * LANES), BF16),
            pltpu.VMEM((length, LANES), BF16),
            pltpu.SemaphoreType.DMA((quarter,)),
        ],
        compiler_params=limit,
    )(group_order, real, imag, edge, head, inverse, far(out_weight), *spread)
    if pieces > 1:
        backs = swap(convolved)
    else:
        in_order = lax.all_to_all(jnp.stack([piece[:, :width] for piece in convolved]), "seq", 0, 0, tiled=True)
        backs = [in_order.transpose(1, 0, 2).reshape(rows, chan_width)]

    def exchange(terms, bit):
        return lax.ppermute(terms, "chan", [(d, d ^ bit) for d in range(chan_count)])

    far_away, mixed = pl.pallas_call(
        mix_kernel,
        out_shape=(
            jax.ShapeDtypeStruct((quarter, rows, out_width), BF16),
            jax.ShapeDtypeStruct((rows, chan_width), BF16),
        ),
        in_specs=[in_vmem] * (3 + 2 * pieces),
        out_specs=[in_vmem] * 2,
        compiler_params=limit,
    )(query_near, skip_gain[None, :], weights_first, *backs, *signal)
    far_terms = exchange(far_away, 1)

    def products(first, weights, dtype):
        return pl.pallas_call(
            functools.partial(project_kernel, first),
            out_shape=jax.ShapeDtypeStruct((quarter, rows, out_width), dtype),
            in_specs=[in_vmem] * 2,
            out_specs=in_vmem,
            compiler_params=limit,
        )(mixed, weights)

    far_kept, near_away = products(quarter, weights_first, F32), products(0, weights_next, BF16)
    cuts = sorted({0, out_width // 2, max(out_width // 2, out_width * 7 // 8 // LANES * LANES), out_width})
    spans = list(zip(cuts, cuts[1:]))
    send = [(far_kept[:, :, a:b] + far_terms[:, :, a:b].astype(F32)).astype(BF16) for a, b in spans]
    send, near_away, mixed = lax.optimization_barrier((send, near_away, mixed))
    sent = [exchange(piece, 2) for piece in send]
    near_terms = exchange(near_away, 1)
    near_kept = pl.pallas_call(
        functools.partial(last_kernel, blocks_last),
        out_shape=jax.ShapeDtypeStruct((quarter, rows, out_width), F32),
        in_specs=[in_vmem, in_hbm],
        out_specs=in_vmem,
        scratch_shapes=[
            pltpu.VMEM((quarter, chan_width, out_width), BF16),
            pltpu.SemaphoreType.DMA((quarter,)),
        ],
        compiler_params=limit,
    )(mixed, far(out_weight))
    terms = [near_kept, near_terms]
    bit = 4
    while bit < chan_count:
        total = sum(term.astype(F32) for term in (*terms, jnp.concatenate(sent, 2)))
        terms, sent, spans = [total[0::2]], [exchange(total[1::2].astype(BF16), bit)], [(0, out_width)]
        bit *= 2
    result = []
    for span, piece in zip(spans, sent):
        operands = [*[term[0] for term in terms], piece[0]]
        result = [
            pl.pallas_call(
                functools.partial(finish_kernel, span, len(terms)),
                out_shape=jax.ShapeDtypeStruct((out_width, rows), F32),
                in_specs=[in_vmem] * len(operands) + [in_hbm] * len(result),
                out_specs=in_hbm,
                scratch_shapes=[pltpu.VMEM((span[1] - span[0], rows), F32), pltpu.SemaphoreType.DMA((1,))],
                input_output_aliases={len(operands): 0} if result else {},
                compiler_params=limit,
            )(*operands, *result)
        ]
    return result[0]


def solution(mesh):
    return jax.shard_map(
        local,
        mesh=mesh,
        in_specs=(
            P("seq", "chan"), P("seq", "chan"), P("seq", "chan"), P(), P(), P(), P(), P(), P(None, "chan"), P("chan"),
            P("chan"), P("chan", None),
        ),
        out_specs=P("chan", "seq"),
        check_vma=False,
    )
```

```python
import functools
import math

import jax
import jax.numpy as jnp
import numpy as np
from jax import lax
from jax.experimental import pallas as pl
from jax.experimental.pallas import tpu as pltpu
from jax.sharding import PartitionSpec as P

GROUP = 128
LANES = 128
SINE_FREQ = 2.0
F32 = jnp.float32
BF16 = jnp.bfloat16


def packed_tables(block):
    period = 2 * block
    row = np.arange(block)
    freq = np.arange(block)

    def forward(shift):
        angle = 2.0 * np.pi * (freq[:, None] * (row[None, :] + shift) % period) / period
        real, imag = np.cos(angle), -np.sin(angle)
        imag[0] = np.where((row + shift) % 2 == 0, 1.0, -1.0)
        return np.concatenate([real, imag], 0)

    head, tail = forward(0), forward(block)
    tail[:, 0] = 0.0
    weight = np.where(freq == 0, 1.0, 2.0) / period
    angle = 2.0 * np.pi * (row[:, None] * freq[None, :] % period) / period
    real, imag = np.cos(angle) * weight, -np.sin(angle) * weight
    imag[:, 0] = np.where(row % 2 == 0, 1.0, -1.0) / period
    inverse = np.concatenate([real, imag], 1)
    to_bf16 = lambda table: jnp.asarray(table.astype(np.float32)).astype(BF16)
    return to_bf16(head), to_bf16(np.concatenate([head, tail], 1)), to_bf16(inverse)


def feature_table(length, bands, rows):
    lag = np.arange(length)
    angle = 2.0 * np.pi * (np.arange(1, bands + 1)[:, None] * lag[None, :] % length) / length
    table = np.zeros((rows, length), np.float32)
    table[0] = lag / length
    table[1 : bands + 1] = np.cos(angle)
    table[bands + 1 : 2 * bands + 1] = np.sin(angle)
    table[2 * bands + 1] = 1.0
    return jnp.asarray(table)


def sine(x):
    n = jnp.round(x * (1.0 / math.pi))
    r = x - n * 3.140625
    r = r - n * 9.67502593994140625e-4
    r = r - n * 1.509957990978376432e-7
    square = r * r
    series = jnp.full_like(r, -2.5052108e-8)
    for term in (2.7557319e-6, -1.9841270e-4, 8.3333333e-3, -1.6666667e-1):
        series = series * square + term
    odd = n * 0.5 - jnp.floor(n * 0.5)
    return (r + r * square * series) * (1.0 - 4.0 * odd)


def contract_first(lhs, rhs):
    return lax.dot_general(
        lhs, rhs, (((0,), (0,)), ((), ())), precision=lax.Precision.HIGHEST, preferred_element_type=F32
    )


def first_piece(pieces):
    return lax.axis_index("seq") if pieces > 1 else 0


def weight_copies(blocks, weight_hbm, weight_out, sem):
    width = weight_out.shape[2]
    copies = []
    for i, j in enumerate(blocks):
        cols = pl.ds(pl.multiple_of((lax.axis_index("chan") ^ j) * width, LANES), width)
        copies.append(pltpu.make_async_copy(weight_hbm.at[:, cols], weight_out.at[i], sem.at[i]))
    return copies


def one_minus_exp(y):
    series = jnp.full_like(y, -1.0 / 40320)
    for term in (5040, -720, 120, -24, 6, -2, 1):
        series = series * y + 1.0 / term
    return jnp.where(y < 0.5, y * series, 1.0 - jnp.exp(-y))


def filter_kernel(block, blocks_first, relative, out_w_ref, *refs):
    smalls, (weight_hbm, query_hbm), refs = refs[:7], refs[7:9], refs[9:]
    (real_ref, imag_ref, edge_ref, weight_out, query_out), refs = refs[:5], refs[5:]
    near, (w1, w2, hid, filt, near_sem, weight_sem, query_sem) = refs[:7], refs[7:]
    feat_ref, emb_w_ref, emb_b_ref, mid_w_ref, mid_b_ref, decay_all, table_ref = near
    fetches = [pltpu.make_async_copy(s, t, near_sem.at[i]) for i, (s, t) in enumerate(zip(smalls, near))]
    for fetch in fetches:
        fetch.start()
    for fetch in fetches[:-1]:
        fetch.wait()
    copies = weight_copies(blocks_first, weight_hbm, weight_out, weight_sem)
    copies.append(pltpu.make_async_copy(query_hbm, query_out, query_sem.at[0]))
    for copy in copies:
        copy.start()
    emb, order = emb_w_ref.shape
    length = feat_ref.shape[1]
    blocks = length // block
    w1[...] = jnp.zeros_like(w1)
    w1[0:emb, :] = emb_w_ref[...]
    w1[emb : emb + 1, :] = emb_b_ref[...]
    w2[...] = jnp.zeros_like(w2)
    w2[0:order, :] = mid_w_ref[...]
    w2[order : order + 1, :] = mid_b_ref[...]
    hid[order:, :] = jnp.ones_like(hid[order:, :])
    hid[0:order, :] = sine(SINE_FREQ * contract_first(w1[...], feat_ref[...]))
    hidden = sine(SINE_FREQ * contract_first(w2[...], hid[...]))
    raw = contract_first(out_w_ref[...], hidden).T
    decay = decay_all[pl.ds(lax.axis_index("seq") if relative else 0, 1), :]
    within = jnp.exp(-decay * lax.broadcasted_iota(jnp.int32, (block, LANES), 0).astype(F32))
    within = within * jnp.sqrt(one_minus_exp(2.0 * decay))
    filt[0:block, :] = jnp.zeros((block, LANES), BF16)
    for m in range(blocks):
        start = jnp.exp(-decay * float(m * block))
        filt[(m + 1) * block : (m + 2) * block, :] = (raw[m * block : (m + 1) * block] * (within * start)).astype(BF16)
    first_row = lax.broadcasted_iota(jnp.int32, (16, LANES), 0) == 0
    fetches[-1].wait()
    group = 2
    for m0 in range(0, blocks, group):
        stacked = jnp.concatenate(
            [
                jnp.concatenate(
                    [filt[(m + 1) * block : (m + 2) * block, :], filt[m * block : (m + 1) * block, :]], 0
                )
                for m in range(m0, m0 + group)
            ],
            1,
        )
        spectrum = jnp.dot(table_ref[...], stacked, preferred_element_type=F32)
        for i in range(group):
            m = m0 + i
            real = spectrum[:block, i * LANES : (i + 1) * LANES]
            imag = spectrum[block:, i * LANES : (i + 1) * LANES]
            real_ref[m] = real
            imag_ref[m] = imag
            edge_ref[m] = jnp.where(first_row, imag[:16], real[:16])
            imag_ref[m, 0:16, :] = jnp.where(first_row, 0.0, imag[:16])
    for copy in copies:
        copy.wait()


def conv_kernel(
    block, blocks_next, relative, order_ref, real_ref, imag_ref, edge_ref, table_ref, inverse_ref, weight_hbm, *refs
):
    *refs, weight_out, sig, sre, sim, spec, conv, weight_sem = refs
    count = len(refs) // 2
    x_refs, out_refs = refs[:count], refs[count:]
    first = first_piece(count if relative else 1)
    copies = weight_copies(blocks_next, weight_hbm, weight_out, weight_sem)
    for copy in copies:
        copy.start()
    groups = x_refs[0].shape[0] // GROUP
    length = sig.shape[0]
    blocks = length // block

    def place(k, i):
        return pl.multiple_of(order_ref[(first ^ k) * groups + i] * GROUP, GROUP)

    for k, x_ref in enumerate(x_refs):
        for i in range(groups):
            sig[pl.ds(place(k, i), GROUP), :] = x_ref[i * GROUP : (i + 1) * GROUP, :]
    group = 2
    for b0 in range(0, blocks, group):
        stacked = jnp.concatenate([sig[b * block : (b + 1) * block, :] for b in range(b0, b0 + group)], 1)
        spectrum = jnp.dot(table_ref[...], stacked, preferred_element_type=F32)
        for i in range(group):
            sre[b0 + i] = spectrum[:block, i * LANES : (i + 1) * LANES]
            sim[b0 + i] = spectrum[block:, i * LANES : (i + 1) * LANES]

    def tile(start, first):
        rows = pl.ds(start, 16)
        mirror = pl.ds(block + start, 16)
        s_real = [sre[q, rows, :] for q in range(blocks)]
        s_imag = [sim[q, rows, :] for q in range(blocks)]
        for g in range(blocks):
            acc_real = acc_imag = None
            for q in range(g + 1):
                fr, fi = real_ref[g - q, rows, :], imag_ref[g - q, rows, :]
                fe = edge_ref[g - q] if first else fr
                re = fr * s_real[q] - fi * s_imag[q]
                im = fe * s_imag[q] + fi * s_real[q]
                acc_real = re if q == 0 else acc_real + re
                acc_imag = im if q == 0 else acc_imag + im
            spec[rows, g * LANES : (g + 1) * LANES] = acc_real.astype(BF16)
            spec[mirror, g * LANES : (g + 1) * LANES] = acc_imag.astype(BF16)

    tile(0, True)

    @pl.loop(1, block // 16)
    def _(t):
        tile(pl.multiple_of(t * 16, 16), False)

    result = jnp.dot(inverse_ref[...], spec[...], preferred_element_type=F32)
    for g in range(blocks):
        conv[g * block : (g + 1) * block, :] = result[:, g * LANES : (g + 1) * LANES].astype(BF16)
    for k, out_ref in enumerate(out_refs):
        for i in range(groups):
            out_ref[i * GROUP : (i + 1) * GROUP, :] = conv[pl.ds(place(k, i), GROUP), :]
    for copy in copies:
        copy.wait()


def mix_kernel(span, query_ref, gain_ref, weight_ref, *refs):
    *refs, out_ref, mixed_ref = refs
    pieces = len(refs) // 2
    unit = refs[0].shape[1]
    for k, (back_ref, sig_ref) in enumerate(zip(refs[:pieces], refs[pieces:])):
        cols = pl.ds(pl.multiple_of((first_piece(pieces) ^ k) * unit, LANES), unit)
        inner = back_ref[...].astype(F32) + gain_ref[:, cols] * sig_ref[...].astype(F32)
        mixed_ref[:, cols] = (query_ref[:, cols].astype(F32) * inner).astype(BF16)
    project_kernel(0, span, mixed_ref, weight_ref, out_ref)


def project_kernel(first, span, mixed_ref, weight_ref, out_ref):
    mixed = mixed_ref[...]
    for i in range(out_ref.shape[0]):
        weight = weight_ref[first + i, :, slice(*span)]
        out_ref[i] = jnp.dot(mixed, weight, preferred_element_type=F32).astype(out_ref.dtype)


def last_kernel(blocks_last, mixed_ref, weight_hbm, out_ref, weight_near, sem):
    copies = weight_copies(blocks_last, weight_hbm, weight_near, sem)
    for copy in copies:
        copy.start()
    for copy in copies:
        copy.wait()
    project_kernel(0, (0, out_ref.shape[2]), mixed_ref, weight_near, out_ref)


def finish_kernel(span, count, *refs):
    (*held, arrived), (out_hbm, turned, sem) = refs[: count + 1], refs[-3:]
    first, last = span
    total = arrived[...].astype(F32)
    for ref in held:
        total = total + ref[:, first:last].astype(F32)
    turned[...] = total.T
    copy = pltpu.make_async_copy(turned, out_hbm.at[first:last], sem.at[0])
    copy.start()
    copy.wait()


def gated_kernel(key_hbm, value_hbm, *refs):
    *out_refs, key_ref, value_ref, sem = refs
    pieces = len(out_refs)
    unit = out_refs[0].shape[1]
    copies = []
    for k in range(pieces):
        cols = pl.ds(pl.multiple_of((first_piece(pieces) ^ k) * unit, LANES), unit)
        copies.append(pltpu.make_async_copy(key_hbm.at[:, cols], key_ref.at[k], sem.at[0, k]))
        copies.append(pltpu.make_async_copy(value_hbm.at[:, cols], value_ref.at[k], sem.at[1, k]))
    for copy in copies:
        copy.start()
    for k, out_ref in enumerate(out_refs):
        copies[2 * k].wait()
        copies[2 * k + 1].wait()
        out_ref[...] = (key_ref[k].astype(F32) * value_ref[k].astype(F32)).astype(BF16)


def local(
    query, key_gate, value, group_order, emb_weight, emb_bias, mid_weight, mid_bias, out_filter, decay_rate, skip_gain,
    out_weight,
):
    rows, chan_width = query.shape
    seq_count, chan_count = lax.axis_size("seq"), lax.axis_size("chan")
    seq_index, chan_index = lax.axis_index("seq"), lax.axis_index("chan")
    length = rows * seq_count
    slots = length // GROUP
    width = chan_width // seq_count
    block = max(2 * GROUP, length // 16)
    blocks = length // block
    emb, order = emb_weight.shape
    head, head_tail, inverse = packed_tables(block)
    feat_rows = -(-(emb + 1) // 8) * 8
    features = feature_table(length, (emb - 1) // 2, feat_rows)

    limit = pltpu.CompilerParams(vmem_limit_bytes=20 << 20)
    in_vmem = pl.BlockSpec(memory_space=pltpu.VMEM)
    in_smem = pl.BlockSpec(memory_space=pltpu.SMEM)
    in_hbm = pl.BlockSpec(memory_space=pltpu.HBM)
    far = lambda operand: pltpu.with_memory_space_constraint(operand, pltpu.HBM)
    unit = width if width % LANES == 0 else chan_width
    pieces = chan_width // unit

    def swap(arrays):
        swapped = list(arrays)
        for k in sorted(range(1, seq_count), key=lambda k: (k & 1, k)):
            swapped[k] = lax.ppermute(arrays[k], "seq", [(d, d ^ k) for d in range(seq_count)])
        return swapped

    signal = pl.pallas_call(
        gated_kernel,
        out_shape=[jax.ShapeDtypeStruct((rows, unit), BF16)] * pieces,
        in_specs=[in_hbm] * 2,
        out_specs=[in_vmem] * pieces,
        scratch_shapes=[
            pltpu.VMEM((pieces, rows, unit), BF16),
            pltpu.VMEM((pieces, rows, unit), BF16),
            pltpu.SemaphoreType.DMA((2, pieces)),
        ],
        compiler_params=limit,
    )(far(key_gate), far(value))
    if pieces > 1:
        spread = swap(signal)
    else:
        in_order = signal[0].reshape(rows, seq_count, width).transpose(1, 0, 2)
        in_order = lax.all_to_all(in_order, "seq", 0, 0, tiled=True)
        spread = list(jnp.pad(in_order, [(0, 0), (0, 0), (0, LANES - width)]))

    my_filter = lax.dynamic_slice_in_dim(out_filter, seq_index * width, width, 1)
    decay = decay_rate.reshape(seq_count, width)
    if pieces == 1:
        pad = [(0, 0), (0, LANES - width)]
        my_filter = jnp.pad(my_filter, pad)
        decay = jnp.pad(lax.dynamic_slice_in_dim(decay, seq_index, 1), pad)
    out_width = out_weight.shape[1] // chan_count
    quarter = chan_count // 4
    odd = range(1, chan_count, 2)
    far_odd, near_odd = [j for j in odd if j & 2], [j for j in odd if not j & 2]
    blocks_first, blocks_next, blocks_last = far_odd + [j ^ 1 for j in far_odd], near_odd, [j ^ 1 for j in near_odd]
    smalls = (
        features, emb_weight, emb_bias[None, :], mid_weight, mid_bias[None, :], decay, head_tail,
    )
    real, imag, edge, weights_first, query_near = pl.pallas_call(
        functools.partial(filter_kernel, block, blocks_first, pieces > 1),
        out_shape=(
            jax.ShapeDtypeStruct((blocks, block, LANES), F32),
            jax.ShapeDtypeStruct((blocks, block, LANES), F32),
            jax.ShapeDtypeStruct((blocks, 16, LANES), F32),
            jax.ShapeDtypeStruct((2 * quarter, chan_width, out_width), BF16),
            jax.ShapeDtypeStruct(query.shape, BF16),
        ),
        in_specs=[in_vmem] + [in_hbm] * 9,
        out_specs=[in_vmem] * 5,
        scratch_shapes=[
            *[pltpu.VMEM(small.shape, small.dtype) for small in smalls],
            pltpu.VMEM((feat_rows, order), F32),
            pltpu.VMEM((order + 8, order), F32),
            pltpu.VMEM((order + 8, length), F32),
            pltpu.VMEM((length + block, LANES), BF16),
            pltpu.SemaphoreType.DMA((len(smalls),)),
            pltpu.SemaphoreType.DMA((2 * quarter,)),
            pltpu.SemaphoreType.DMA((1,)),
        ],
        compiler_params=limit,
    )(my_filter, *map(far, (*smalls, out_weight, query)))

    *convolved, weights_next = pl.pallas_call(
        functools.partial(conv_kernel, block, blocks_next, pieces > 1),
        out_shape=[
            *[jax.ShapeDtypeStruct((rows, LANES), BF16)] * seq_count,
            jax.ShapeDtypeStruct((quarter, chan_width, out_width), BF16),
        ],
        in_specs=[in_smem] + [in_vmem] * 5 + [in_hbm] + [in_vmem] * seq_count,
        out_specs=[in_vmem] * (seq_count + 1),
        scratch_shapes=[
            pltpu.VMEM((length, LANES), BF16),
            pltpu.VMEM((blocks, block, LANES), F32),
            pltpu.VMEM((blocks, block, LANES), F32),
            pltpu.VMEM((2 * block, blocks * LANES), BF16),
            pltpu.VMEM((length, LANES), BF16),
            pltpu.SemaphoreType.DMA((quarter,)),
        ],
        compiler_params=limit,
    )(group_order, real, imag, edge, head, inverse, far(out_weight), *spread)
    if pieces > 1:
        backs = swap(convolved)
    else:
        in_order = lax.all_to_all(jnp.stack([piece[:, :width] for piece in convolved]), "seq", 0, 0, tiled=True)
        backs = [in_order.transpose(1, 0, 2).reshape(rows, chan_width)]

    def exchange(terms, bit):
        return lax.ppermute(terms, "chan", [(d, d ^ bit) for d in range(chan_count)])

    def products(mixed, first, span, weights, dtype):
        return pl.pallas_call(
            functools.partial(project_kernel, first, span),
            out_shape=jax.ShapeDtypeStruct((quarter, rows, span[1] - span[0]), dtype),
            in_specs=[in_vmem] * 2,
            out_specs=in_vmem,
            compiler_params=limit,
        )(mixed, weights)

    spans = [(0, out_width // 2), (out_width // 2, out_width)]
    far_away, mixed = pl.pallas_call(
        functools.partial(mix_kernel, spans[0]),
        out_shape=(
            jax.ShapeDtypeStruct((quarter, rows, spans[0][1]), BF16),
            jax.ShapeDtypeStruct((rows, chan_width), BF16),
        ),
        in_specs=[in_vmem] * (3 + 2 * pieces),
        out_specs=[in_vmem] * 2,
        compiler_params=limit,
    )(query_near, skip_gain[None, :], weights_first, *backs, *signal)
    far_terms = [exchange(far_away, 1), exchange(products(mixed, 0, spans[1], weights_first, BF16), 1)]
    sent = []
    for span, terms in zip(spans, far_terms):
        far_kept = products(mixed, quarter, span, weights_first, F32)
        send = (far_kept + terms.astype(F32)).astype(BF16)
        sent.append(exchange(send, 2))
    near_away = products(mixed, 0, (0, out_width), weights_next, BF16)
    near_terms = exchange(near_away, 1)
    sent[0], mixed = lax.optimization_barrier((sent[0], mixed))
    near_kept = pl.pallas_call(
        functools.partial(last_kernel, blocks_last),
        out_shape=jax.ShapeDtypeStruct((quarter, rows, out_width), F32),
        in_specs=[in_vmem, in_hbm],
        out_specs=in_vmem,
        scratch_shapes=[
            pltpu.VMEM((quarter, chan_width, out_width), BF16),
            pltpu.SemaphoreType.DMA((quarter,)),
        ],
        compiler_params=limit,
    )(mixed, far(out_weight))
    terms = [near_kept, near_terms]
    bit = 4
    while bit < chan_count:
        total = sum(term.astype(F32) for term in (*terms, jnp.concatenate(sent, 2)))
        terms, sent, spans = [total[0::2]], [exchange(total[1::2].astype(BF16), bit)], [(0, out_width)]
        bit *= 2
    result = []
    for span, piece in zip(spans, sent):
        operands = [*[term[0] for term in terms], piece[0]]
        result = [
            pl.pallas_call(
                functools.partial(finish_kernel, span, len(terms)),
                out_shape=jax.ShapeDtypeStruct((out_width, rows), F32),
                in_specs=[in_vmem] * len(operands) + [in_hbm] * len(result),
                out_specs=in_hbm,
                scratch_shapes=[pltpu.VMEM((span[1] - span[0], rows), F32), pltpu.SemaphoreType.DMA((1,))],
                input_output_aliases={len(operands): 0} if result else {},
                compiler_params=limit,
            )(*operands, *result)
        ]
    return result[0]


def solution(mesh):
    return jax.shard_map(
        local,
        mesh=mesh,
        in_specs=(
            P("seq", "chan"), P("seq", "chan"), P("seq", "chan"), P(), P(), P(), P(), P(), P(None, "chan"), P("chan"),
            P("chan"), P("chan", None),
        ),
        out_specs=P("chan", "seq"),
        check_vma=False,
    )
```

```python
import functools
import math

import jax
import jax.numpy as jnp
import numpy as np
from jax import lax
from jax.experimental import pallas as pl
from jax.experimental.pallas import tpu as pltpu
from jax.sharding import PartitionSpec as P

GROUP = 128
LANES = 128
SINE_FREQ = 2.0
F32 = jnp.float32
BF16 = jnp.bfloat16


def packed_tables(block):
    period = 2 * block
    row = np.arange(block)
    freq = np.arange(block)

    def forward(shift):
        angle = 2.0 * np.pi * (freq[:, None] * (row[None, :] + shift) % period) / period
        real, imag = np.cos(angle), -np.sin(angle)
        imag[0] = np.where((row + shift) % 2 == 0, 1.0, -1.0)
        return np.concatenate([real, imag], 0)

    head, tail = forward(0), forward(block)
    tail[:, 0] = 0.0
    weight = np.where(freq == 0, 1.0, 2.0) / period
    angle = 2.0 * np.pi * (row[:, None] * freq[None, :] % period) / period
    real, imag = np.cos(angle) * weight, -np.sin(angle) * weight
    imag[:, 0] = np.where(row % 2 == 0, 1.0, -1.0) / period
    inverse = np.concatenate([real, imag], 1)
    to_bf16 = lambda table: jnp.asarray(table.astype(np.float32)).astype(BF16)
    return to_bf16(head), to_bf16(np.concatenate([head, tail], 1)), to_bf16(inverse)


def feature_table(length, bands, rows):
    lag = np.arange(length)
    angle = 2.0 * np.pi * (np.arange(1, bands + 1)[:, None] * lag[None, :] % length) / length
    table = np.zeros((rows, length), np.float32)
    table[0] = lag / length
    table[1 : bands + 1] = np.cos(angle)
    table[bands + 1 : 2 * bands + 1] = np.sin(angle)
    table[2 * bands + 1] = 1.0
    return jnp.asarray(table)


def sine(x):
    n = jnp.round(x * (1.0 / math.pi))
    r = x - n * 3.140625
    r = r - n * 9.67502593994140625e-4
    r = r - n * 1.509957990978376432e-7
    square = r * r
    series = jnp.full_like(r, -2.5052108e-8)
    for term in (2.7557319e-6, -1.9841270e-4, 8.3333333e-3, -1.6666667e-1):
        series = series * square + term
    odd = n * 0.5 - jnp.floor(n * 0.5)
    return (r + r * square * series) * (1.0 - 4.0 * odd)


def contract_first(lhs, rhs):
    return lax.dot_general(
        lhs, rhs, (((0,), (0,)), ((), ())), precision=lax.Precision.HIGHEST, preferred_element_type=F32
    )


def first_piece(pieces):
    return lax.axis_index("seq") if pieces > 1 else 0


def weight_copies(blocks, weight_hbm, weight_out, sem):
    width = weight_out.shape[2]
    copies = []
    for i, j in enumerate(blocks):
        cols = pl.ds(pl.multiple_of((lax.axis_index("chan") ^ j) * width, LANES), width)
        copies.append(pltpu.make_async_copy(weight_hbm.at[:, cols], weight_out.at[i], sem.at[i]))
    return copies


def one_minus_exp(y):
    series = jnp.full_like(y, -1.0 / 40320)
    for term in (5040, -720, 120, -24, 6, -2, 1):
        series = series * y + 1.0 / term
    return jnp.where(y < 0.5, y * series, 1.0 - jnp.exp(-y))


def filter_kernel(block, blocks_first, relative, out_w_ref, *refs):
    smalls, (weight_hbm, query_hbm), refs = refs[:7], refs[7:9], refs[9:]
    (real_ref, imag_ref, edge_ref, weight_out, query_out), refs = refs[:5], refs[5:]
    near, (w1, w2, hid, filt, near_sem, weight_sem, query_sem) = refs[:7], refs[7:]
    feat_ref, emb_w_ref, emb_b_ref, mid_w_ref, mid_b_ref, decay_all, table_ref = near
    fetches = [pltpu.make_async_copy(s, t, near_sem.at[i]) for i, (s, t) in enumerate(zip(smalls, near))]
    for fetch in fetches:
        fetch.start()
    for fetch in fetches[:-1]:
        fetch.wait()
    copies = weight_copies(blocks_first, weight_hbm, weight_out, weight_sem)
    copies.append(pltpu.make_async_copy(query_hbm, query_out, query_sem.at[0]))
    for copy in copies:
        copy.start()
    emb, order = emb_w_ref.shape
    length = feat_ref.shape[1]
    blocks = length // block
    w1[...] = jnp.zeros_like(w1)
    w1[0:emb, :] = emb_w_ref[...]
    w1[emb : emb + 1, :] = emb_b_ref[...]
    w2[...] = jnp.zeros_like(w2)
    w2[0:order, :] = mid_w_ref[...]
    w2[order : order + 1, :] = mid_b_ref[...]
    hid[order:, :] = jnp.ones_like(hid[order:, :])
    hid[0:order, :] = sine(SINE_FREQ * contract_first(w1[...], feat_ref[...]))
    hidden = sine(SINE_FREQ * contract_first(w2[...], hid[...]))
    raw = contract_first(out_w_ref[...], hidden).T
    decay = decay_all[pl.ds(lax.axis_index("seq") if relative else 0, 1), :]
    within = jnp.exp(-decay * lax.broadcasted_iota(jnp.int32, (block, LANES), 0).astype(F32))
    within = within * jnp.sqrt(one_minus_exp(2.0 * decay))
    filt[0:block, :] = jnp.zeros((block, LANES), BF16)
    for m in range(blocks):
        start = jnp.exp(-decay * float(m * block))
        filt[(m + 1) * block : (m + 2) * block, :] = (raw[m * block : (m + 1) * block] * (within * start)).astype(BF16)
    first_row = lax.broadcasted_iota(jnp.int32, (16, LANES), 0) == 0
    fetches[-1].wait()
    group = 2
    for m0 in range(0, blocks, group):
        stacked = jnp.concatenate(
            [
                jnp.concatenate(
                    [filt[(m + 1) * block : (m + 2) * block, :], filt[m * block : (m + 1) * block, :]], 0
                )
                for m in range(m0, m0 + group)
            ],
            1,
        )
        spectrum = jnp.dot(table_ref[...], stacked, preferred_element_type=F32)
        for i in range(group):
            m = m0 + i
            real = spectrum[:block, i * LANES : (i + 1) * LANES]
            imag = spectrum[block:, i * LANES : (i + 1) * LANES]
            real_ref[m] = real
            imag_ref[m] = imag
            edge_ref[m] = jnp.where(first_row, imag[:16], real[:16])
            imag_ref[m, 0:16, :] = jnp.where(first_row, 0.0, imag[:16])
    for copy in copies:
        copy.wait()


def conv_kernel(
    block, blocks_next, arrival, relative, order_ref, real_ref, imag_ref, edge_ref, table_ref, inverse_ref, weight_hbm, *refs
):
    *refs, weight_out, sig, sre, sim, spec, conv, weight_sem = refs
    count = len(refs) // 2
    x_refs, out_refs = refs[:count], refs[count:]
    first = first_piece(count if relative else 1)
    copies = weight_copies(blocks_next, weight_hbm, weight_out, weight_sem)
    for copy in copies:
        copy.start()
    groups = x_refs[0].shape[0] // GROUP
    length = sig.shape[0]
    blocks = length // block

    def place(k, i):
        return pl.multiple_of(order_ref[(first ^ k) * groups + i] * GROUP, GROUP)

    for k, x_ref in zip(arrival, x_refs):
        for i in range(groups):
            sig[pl.ds(place(k, i), GROUP), :] = x_ref[i * GROUP : (i + 1) * GROUP, :]
    group = 2
    for b0 in range(0, blocks, group):
        stacked = jnp.concatenate([sig[b * block : (b + 1) * block, :] for b in range(b0, b0 + group)], 1)
        spectrum = jnp.dot(table_ref[...], stacked, preferred_element_type=F32)
        for i in range(group):
            sre[b0 + i] = spectrum[:block, i * LANES : (i + 1) * LANES]
            sim[b0 + i] = spectrum[block:, i * LANES : (i + 1) * LANES]

    def tile(start, first):
        rows = pl.ds(start, 16)
        mirror = pl.ds(block + start, 16)
        s_real = [sre[q, rows, :] for q in range(blocks)]
        s_imag = [sim[q, rows, :] for q in range(blocks)]
        for g in range(blocks):
            acc_real = acc_imag = None
            for q in range(g + 1):
                fr, fi = real_ref[g - q, rows, :], imag_ref[g - q, rows, :]
                fe = edge_ref[g - q] if first else fr
                re = fr * s_real[q] - fi * s_imag[q]
                im = fe * s_imag[q] + fi * s_real[q]
                acc_real = re if q == 0 else acc_real + re
                acc_imag = im if q == 0 else acc_imag + im
            spec[rows, g * LANES : (g + 1) * LANES] = acc_real.astype(BF16)
            spec[mirror, g * LANES : (g + 1) * LANES] = acc_imag.astype(BF16)

    tile(0, True)

    @pl.loop(1, block // 16)
    def _(t):
        tile(pl.multiple_of(t * 16, 16), False)

    result = jnp.dot(inverse_ref[...], spec[...], preferred_element_type=F32)
    for g in range(blocks):
        conv[g * block : (g + 1) * block, :] = result[:, g * LANES : (g + 1) * LANES].astype(BF16)
    for k, out_ref in enumerate(out_refs):
        for i in range(groups):
            out_ref[i * GROUP : (i + 1) * GROUP, :] = conv[pl.ds(place(k, i), GROUP), :]
    for copy in copies:
        copy.wait()


def mix_kernel(arrival, query_ref, gain_ref, weight_ref, *refs):
    *refs, out_ref, mixed_ref = refs
    pieces = len(refs) // 2
    unit = refs[0].shape[1]
    for k, back_ref, sig_ref in zip(arrival, refs[:pieces], refs[pieces:]):
        cols = pl.ds(pl.multiple_of((first_piece(pieces) ^ k) * unit, LANES), unit)
        inner = back_ref[...].astype(F32) + gain_ref[:, cols] * sig_ref[...].astype(F32)
        mixed_ref[:, cols] = (query_ref[:, cols].astype(F32) * inner).astype(BF16)
    project_kernel(0, mixed_ref, weight_ref, out_ref)


def project_kernel(first, mixed_ref, weight_ref, out_ref):
    mixed = mixed_ref[...]
    for i in range(out_ref.shape[0]):
        out_ref[i] = jnp.dot(mixed, weight_ref[first + i], preferred_element_type=F32).astype(out_ref.dtype)


def last_kernel(blocks_last, mixed_ref, weight_hbm, out_ref, weight_near, sem):
    copies = weight_copies(blocks_last, weight_hbm, weight_near, sem)
    for copy in copies:
        copy.start()
    for copy in copies:
        copy.wait()
    project_kernel(0, mixed_ref, weight_near, out_ref)


def finish_kernel(span, count, *refs):
    (*held, arrived), (out_hbm, turned, sem) = refs[: count + 1], refs[-3:]
    first, last = span
    step = min(LANES, last - first)
    copies = []
    for i, start in enumerate(range(0, last - first, step)):
        cols = slice(start, start + step)
        total = arrived[:, cols].astype(F32)
        for ref in held:
            total = total + ref[:, first + start : first + start + step].astype(F32)
        turned[cols] = total.T
        copies.append(pltpu.make_async_copy(turned.at[cols], out_hbm.at[first + start : first + start + step], sem.at[i]))
        copies[-1].start()
    for copy in copies:
        copy.wait()


def gated_kernel(key_hbm, value_hbm, *refs):
    *out_refs, key_ref, value_ref, sem = refs
    pieces = len(out_refs)
    unit = out_refs[0].shape[1]
    copies = []
    for k in range(pieces):
        cols = pl.ds(pl.multiple_of((first_piece(pieces) ^ k) * unit, LANES), unit)
        copies.append(pltpu.make_async_copy(key_hbm.at[:, cols], key_ref.at[k], sem.at[0, k]))
        copies.append(pltpu.make_async_copy(value_hbm.at[:, cols], value_ref.at[k], sem.at[1, k]))
    for copy in copies:
        copy.start()
    for k, out_ref in enumerate(out_refs):
        copies[2 * k].wait()
        copies[2 * k + 1].wait()
        out_ref[...] = (key_ref[k].astype(F32) * value_ref[k].astype(F32)).astype(BF16)


def local(
    query, key_gate, value, group_order, emb_weight, emb_bias, mid_weight, mid_bias, out_filter, decay_rate, skip_gain,
    out_weight,
):
    rows, chan_width = query.shape
    seq_count, chan_count = lax.axis_size("seq"), lax.axis_size("chan")
    seq_index, chan_index = lax.axis_index("seq"), lax.axis_index("chan")
    length = rows * seq_count
    slots = length // GROUP
    width = chan_width // seq_count
    block = max(2 * GROUP, length // 16)
    blocks = length // block
    emb, order = emb_weight.shape
    head, head_tail, inverse = packed_tables(block)
    feat_rows = -(-(emb + 1) // 8) * 8
    features = feature_table(length, (emb - 1) // 2, feat_rows)

    limit = pltpu.CompilerParams(vmem_limit_bytes=20 << 20)
    in_vmem = pl.BlockSpec(memory_space=pltpu.VMEM)
    in_smem = pl.BlockSpec(memory_space=pltpu.SMEM)
    in_hbm = pl.BlockSpec(memory_space=pltpu.HBM)
    far = lambda operand: pltpu.with_memory_space_constraint(operand, pltpu.HBM)
    unit = width if width % LANES == 0 else chan_width
    pieces = chan_width // unit

    arrival = sorted(range(seq_count), key=lambda k: (k & 1, k))

    def swap(arrays):
        return [arrays[0]] + [
            lax.ppermute(arrays[k], "seq", [(d, d ^ k) for d in range(seq_count)]) for k in range(1, seq_count)
        ]

    signal = pl.pallas_call(
        gated_kernel,
        out_shape=[jax.ShapeDtypeStruct((rows, unit), BF16)] * pieces,
        in_specs=[in_hbm] * 2,
        out_specs=[in_vmem] * pieces,
        scratch_shapes=[
            pltpu.VMEM((pieces, rows, unit), BF16),
            pltpu.VMEM((pieces, rows, unit), BF16),
            pltpu.SemaphoreType.DMA((2, pieces)),
        ],
        compiler_params=limit,
    )(far(key_gate), far(value))
    if pieces > 1:
        spread = swap(signal)
    else:
        in_order = signal[0].reshape(rows, seq_count, width).transpose(1, 0, 2)
        in_order = lax.all_to_all(in_order, "seq", 0, 0, tiled=True)
        spread = list(jnp.pad(in_order, [(0, 0), (0, 0), (0, LANES - width)]))

    my_filter = lax.dynamic_slice_in_dim(out_filter, seq_index * width, width, 1)
    decay = decay_rate.reshape(seq_count, width)
    if pieces == 1:
        pad = [(0, 0), (0, LANES - width)]
        my_filter = jnp.pad(my_filter, pad)
        decay = jnp.pad(lax.dynamic_slice_in_dim(decay, seq_index, 1), pad)
    out_width = out_weight.shape[1] // chan_count
    quarter = chan_count // 4
    odd = range(1, chan_count, 2)
    far_odd, near_odd = [j for j in odd if j & 2], [j for j in odd if not j & 2]
    blocks_first, blocks_next, blocks_last = far_odd + [j ^ 1 for j in far_odd], near_odd, [j ^ 1 for j in near_odd]
    smalls = (
        features, emb_weight, emb_bias[None, :], mid_weight, mid_bias[None, :], decay, head_tail,
    )
    real, imag, edge, weights_first, query_near = pl.pallas_call(
        functools.partial(filter_kernel, block, blocks_first, pieces > 1),
        out_shape=(
            jax.ShapeDtypeStruct((blocks, block, LANES), F32),
            jax.ShapeDtypeStruct((blocks, block, LANES), F32),
            jax.ShapeDtypeStruct((blocks, 16, LANES), F32),
            jax.ShapeDtypeStruct((2 * quarter, chan_width, out_width), BF16),
            jax.ShapeDtypeStruct(query.shape, BF16),
        ),
        in_specs=[in_vmem] + [in_hbm] * 9,
        out_specs=[in_vmem] * 5,
        scratch_shapes=[
            *[pltpu.VMEM(small.shape, small.dtype) for small in smalls],
            pltpu.VMEM((feat_rows, order), F32),
            pltpu.VMEM((order + 8, order), F32),
            pltpu.VMEM((order + 8, length), F32),
            pltpu.VMEM((length + block, LANES), BF16),
            pltpu.SemaphoreType.DMA((len(smalls),)),
            pltpu.SemaphoreType.DMA((2 * quarter,)),
            pltpu.SemaphoreType.DMA((1,)),
        ],
        compiler_params=limit,
    )(my_filter, *map(far, (*smalls, out_weight, query)))

    *convolved, weights_next = pl.pallas_call(
        functools.partial(conv_kernel, block, blocks_next, arrival, pieces > 1),
        out_shape=[
            *[jax.ShapeDtypeStruct((rows, LANES), BF16)] * seq_count,
            jax.ShapeDtypeStruct((quarter, chan_width, out_width), BF16),
        ],
        in_specs=[in_smem] + [in_vmem] * 5 + [in_hbm] + [in_vmem] * seq_count,
        out_specs=[in_vmem] * (seq_count + 1),
        scratch_shapes=[
            pltpu.VMEM((length, LANES), BF16),
            pltpu.VMEM((blocks, block, LANES), F32),
            pltpu.VMEM((blocks, block, LANES), F32),
            pltpu.VMEM((2 * block, blocks * LANES), BF16),
            pltpu.VMEM((length, LANES), BF16),
            pltpu.SemaphoreType.DMA((quarter,)),
        ],
        compiler_params=limit,
    )(group_order, real, imag, edge, head, inverse, far(out_weight), *[spread[k] for k in arrival])
    if pieces > 1:
        backs = swap(convolved)
    else:
        in_order = lax.all_to_all(jnp.stack([piece[:, :width] for piece in convolved]), "seq", 0, 0, tiled=True)
        backs = [in_order.transpose(1, 0, 2).reshape(rows, chan_width)]

    def exchange(terms, bit):
        return lax.ppermute(terms, "chan", [(d, d ^ bit) for d in range(chan_count)])

    far_away, mixed = pl.pallas_call(
        functools.partial(mix_kernel, arrival if pieces > 1 else [0]),
        out_shape=(
            jax.ShapeDtypeStruct((quarter, rows, out_width), BF16),
            jax.ShapeDtypeStruct((rows, chan_width), BF16),
        ),
        in_specs=[in_vmem] * (3 + 2 * pieces),
        out_specs=[in_vmem] * 2,
        compiler_params=limit,
    )(query_near, skip_gain[None, :], weights_first, *[array[k] for array in (backs, signal) for k in (arrival if pieces > 1 else [0])])
    far_terms = exchange(far_away, 1)

    def products(first, weights, dtype):
        return pl.pallas_call(
            functools.partial(project_kernel, first),
            out_shape=jax.ShapeDtypeStruct((quarter, rows, out_width), dtype),
            in_specs=[in_vmem] * 2,
            out_specs=in_vmem,
            compiler_params=limit,
        )(mixed, weights)

    far_kept, near_away = products(quarter, weights_first, F32), products(0, weights_next, BF16)
    spans = [(0, out_width // 2), (out_width // 2, out_width)]
    send = [(far_kept[:, :, a:b] + far_terms[:, :, a:b].astype(F32)).astype(BF16) for a, b in spans]
    send, near_away, mixed = lax.optimization_barrier((send, near_away, mixed))
    sent = [exchange(piece, 2) for piece in send]
    near_terms = exchange(near_away, 1)
    near_kept = pl.pallas_call(
        functools.partial(last_kernel, blocks_last),
        out_shape=jax.ShapeDtypeStruct((quarter, rows, out_width), F32),
        in_specs=[in_vmem, in_hbm],
        out_specs=in_vmem,
        scratch_shapes=[
            pltpu.VMEM((quarter, chan_width, out_width), BF16),
            pltpu.SemaphoreType.DMA((quarter,)),
        ],
        compiler_params=limit,
    )(mixed, far(out_weight))
    terms = [near_kept, near_terms]
    bit = 4
    while bit < chan_count:
        total = sum(term.astype(F32) for term in (*terms, jnp.concatenate(sent, 2)))
        terms, sent, spans = [total[0::2]], [exchange(total[1::2].astype(BF16), bit)], [(0, out_width)]
        bit *= 2
    result = []
    for span, piece in zip(spans, sent):
        operands = [*[term[0] for term in terms], piece[0]]
        result = [
            pl.pallas_call(
                functools.partial(finish_kernel, span, len(terms)),
                out_shape=jax.ShapeDtypeStruct((out_width, rows), F32),
                in_specs=[in_vmem] * len(operands) + [in_hbm] * len(result),
                out_specs=in_hbm,
                scratch_shapes=[
                    pltpu.VMEM((span[1] - span[0], rows), F32),
                    pltpu.SemaphoreType.DMA((max(1, (span[1] - span[0]) // LANES),)),
                ],
                input_output_aliases={len(operands): 0} if result else {},
                compiler_params=limit,
            )(*operands, *result)
        ]
    return result[0]


def solution(mesh):
    return jax.shard_map(
        local,
        mesh=mesh,
        in_specs=(
            P("seq", "chan"), P("seq", "chan"), P("seq", "chan"), P(), P(), P(), P(), P(), P(None, "chan"), P("chan"),
            P("chan"), P("chan", None),
        ),
        out_specs=P("chan", "seq"),
        check_vma=False,
    )
```

```python
import functools
import math

import jax
import jax.numpy as jnp
import numpy as np
from jax import lax
from jax.experimental import pallas as pl
from jax.experimental.pallas import tpu as pltpu
from jax.sharding import PartitionSpec as P

GROUP = 128
LANES = 128
SINE_FREQ = 2.0
F32 = jnp.float32
BF16 = jnp.bfloat16


def packed_tables(block):
    period = 2 * block
    row = np.arange(block)
    freq = np.arange(block)

    def forward(shift):
        angle = 2.0 * np.pi * (freq[:, None] * (row[None, :] + shift) % period) / period
        real, imag = np.cos(angle), -np.sin(angle)
        imag[0] = np.where((row + shift) % 2 == 0, 1.0, -1.0)
        return np.concatenate([real, imag], 0)

    head, tail = forward(0), forward(block)
    tail[:, 0] = 0.0
    weight = np.where(freq == 0, 1.0, 2.0) / period
    angle = 2.0 * np.pi * (row[:, None] * freq[None, :] % period) / period
    real, imag = np.cos(angle) * weight, -np.sin(angle) * weight
    imag[:, 0] = np.where(row % 2 == 0, 1.0, -1.0) / period
    inverse = np.concatenate([real, imag], 1)
    to_bf16 = lambda table: jnp.asarray(table.astype(np.float32)).astype(BF16)
    return to_bf16(head), to_bf16(np.concatenate([head, tail], 1)), to_bf16(inverse)


def feature_table(length, bands, rows):
    lag = np.arange(length)
    angle = 2.0 * np.pi * (np.arange(1, bands + 1)[:, None] * lag[None, :] % length) / length
    table = np.zeros((rows, length), np.float32)
    table[0] = lag / length
    table[1 : bands + 1] = np.cos(angle)
    table[bands + 1 : 2 * bands + 1] = np.sin(angle)
    table[2 * bands + 1] = 1.0
    return jnp.asarray(table)


def sine(x):
    n = jnp.round(x * (1.0 / math.pi))
    r = x - n * 3.140625
    r = r - n * 9.67502593994140625e-4
    r = r - n * 1.509957990978376432e-7
    square = r * r
    series = jnp.full_like(r, -2.5052108e-8)
    for term in (2.7557319e-6, -1.9841270e-4, 8.3333333e-3, -1.6666667e-1):
        series = series * square + term
    odd = n * 0.5 - jnp.floor(n * 0.5)
    return (r + r * square * series) * (1.0 - 4.0 * odd)


def contract_first(lhs, rhs):
    return lax.dot_general(
        lhs, rhs, (((0,), (0,)), ((), ())), precision=lax.Precision.HIGHEST, preferred_element_type=F32
    )


def first_piece(pieces):
    return lax.axis_index("seq") if pieces > 1 else 0


def weight_copies(blocks, weight_hbm, weight_out, sem):
    width = weight_out.shape[2]
    copies = []
    for i, j in enumerate(blocks):
        cols = pl.ds(pl.multiple_of((lax.axis_index("chan") ^ j) * width, LANES), width)
        copies.append(pltpu.make_async_copy(weight_hbm.at[:, cols], weight_out.at[i], sem.at[i]))
    return copies


def one_minus_exp(y):
    series = jnp.full_like(y, -1.0 / 40320)
    for term in (5040, -720, 120, -24, 6, -2, 1):
        series = series * y + 1.0 / term
    return jnp.where(y < 0.5, y * series, 1.0 - jnp.exp(-y))


def filter_kernel(
    block, blocks_first, relative, out_w_ref, feat_ref, emb_w_ref, emb_b_ref, mid_w_ref, mid_b_ref, decay_all, table_ref,
    weight_hbm, query_hbm, real_ref, imag_ref, edge_ref, weight_out, query_out, w1, w2, hid, filt, weight_sem, query_sem,
):
    copies = weight_copies(blocks_first, weight_hbm, weight_out, weight_sem)
    copies.append(pltpu.make_async_copy(query_hbm, query_out, query_sem.at[0]))
    for copy in copies:
        copy.start()
    emb, order = emb_w_ref.shape
    length = feat_ref.shape[1]
    blocks = length // block
    w1[...] = jnp.zeros_like(w1)
    w1[0:emb, :] = emb_w_ref[...]
    w1[emb : emb + 1, :] = emb_b_ref[...]
    w2[...] = jnp.zeros_like(w2)
    w2[0:order, :] = mid_w_ref[...]
    w2[order : order + 1, :] = mid_b_ref[...]
    hid[order:, :] = jnp.ones_like(hid[order:, :])
    hid[0:order, :] = sine(SINE_FREQ * contract_first(w1[...], feat_ref[...]))
    hidden = sine(SINE_FREQ * contract_first(w2[...], hid[...]))
    raw = contract_first(out_w_ref[...], hidden).T
    decay = decay_all[pl.ds(lax.axis_index("seq") if relative else 0, 1), :]
    within = jnp.exp(-decay * lax.broadcasted_iota(jnp.int32, (block, LANES), 0).astype(F32))
    within = within * jnp.sqrt(one_minus_exp(2.0 * decay))
    filt[0:block, :] = jnp.zeros((block, LANES), BF16)
    for m in range(blocks):
        start = jnp.exp(-decay * float(m * block))
        filt[(m + 1) * block : (m + 2) * block, :] = (raw[m * block : (m + 1) * block] * (within * start)).astype(BF16)
    first_row = lax.broadcasted_iota(jnp.int32, (16, LANES), 0) == 0
    group = 2
    for m0 in range(0, blocks, group):
        stacked = jnp.concatenate(
            [
                jnp.concatenate(
                    [filt[(m + 1) * block : (m + 2) * block, :], filt[m * block : (m + 1) * block, :]], 0
                )
                for m in range(m0, m0 + group)
            ],
            1,
        )
        spectrum = jnp.dot(table_ref[...], stacked, preferred_element_type=F32)
        for i in range(group):
            m = m0 + i
            real = spectrum[:block, i * LANES : (i + 1) * LANES]
            imag = spectrum[block:, i * LANES : (i + 1) * LANES]
            real_ref[m] = real
            imag_ref[m] = imag
            edge_ref[m] = jnp.where(first_row, imag[:16], real[:16])
            imag_ref[m, 0:16, :] = jnp.where(first_row, 0.0, imag[:16])
    for copy in copies:
        copy.wait()


def conv_kernel(
    block, blocks_next, arrival, relative, order_ref, real_ref, imag_ref, edge_ref, table_ref, inverse_ref, weight_hbm, *refs
):
    *refs, weight_out, sig, sre, sim, spec, conv, weight_sem = refs
    count = len(refs) // 2
    x_refs, out_refs = refs[:count], refs[count:]
    first = first_piece(count if relative else 1)
    copies = weight_copies(blocks_next, weight_hbm, weight_out, weight_sem)
    for copy in copies:
        copy.start()
    groups = x_refs[0].shape[0] // GROUP
    length = sig.shape[0]
    blocks = length // block

    def place(k, i):
        return pl.multiple_of(order_ref[(first ^ k) * groups + i] * GROUP, GROUP)

    for k, x_ref in zip(arrival, x_refs):
        for i in range(groups):
            sig[pl.ds(place(k, i), GROUP), :] = x_ref[i * GROUP : (i + 1) * GROUP, :]
    group = 2
    for b0 in range(0, blocks, group):
        stacked = jnp.concatenate([sig[b * block : (b + 1) * block, :] for b in range(b0, b0 + group)], 1)
        spectrum = jnp.dot(table_ref[...], stacked, preferred_element_type=F32)
        for i in range(group):
            sre[b0 + i] = spectrum[:block, i * LANES : (i + 1) * LANES]
            sim[b0 + i] = spectrum[block:, i * LANES : (i + 1) * LANES]

    def tile(start, first):
        rows = pl.ds(start, 16)
        mirror = pl.ds(block + start, 16)
        s_real = [sre[q, rows, :] for q in range(blocks)]
        s_imag = [sim[q, rows, :] for q in range(blocks)]
        for g in range(blocks):
            acc_real = acc_imag = None
            for q in range(g + 1):
                fr, fi = real_ref[g - q, rows, :], imag_ref[g - q, rows, :]
                fe = edge_ref[g - q] if first else fr
                re = fr * s_real[q] - fi * s_imag[q]
                im = fe * s_imag[q] + fi * s_real[q]
                acc_real = re if q == 0 else acc_real + re
                acc_imag = im if q == 0 else acc_imag + im
            spec[rows, g * LANES : (g + 1) * LANES] = acc_real.astype(BF16)
            spec[mirror, g * LANES : (g + 1) * LANES] = acc_imag.astype(BF16)

    tile(0, True)

    @pl.loop(1, block // 16)
    def _(t):
        tile(pl.multiple_of(t * 16, 16), False)

    result = jnp.dot(inverse_ref[...], spec[...], preferred_element_type=F32)
    for g in range(blocks):
        conv[g * block : (g + 1) * block, :] = result[:, g * LANES : (g + 1) * LANES].astype(BF16)
    for k, out_ref in enumerate(out_refs):
        for i in range(groups):
            out_ref[i * GROUP : (i + 1) * GROUP, :] = conv[pl.ds(place(k, i), GROUP), :]
    for copy in copies:
        copy.wait()


def mix_kernel(arrival, query_ref, gain_ref, weight_ref, *refs):
    *refs, out_ref, mixed_ref = refs
    pieces = len(refs) // 2
    unit = refs[0].shape[1]
    for k, back_ref, sig_ref in zip(arrival, refs[:pieces], refs[pieces:]):
        cols = pl.ds(pl.multiple_of((first_piece(pieces) ^ k) * unit, LANES), unit)
        inner = back_ref[...].astype(F32) + gain_ref[:, cols] * sig_ref[...].astype(F32)
        mixed_ref[:, cols] = (query_ref[:, cols].astype(F32) * inner).astype(BF16)
    project_kernel(0, mixed_ref, weight_ref, out_ref)


def project_kernel(first, mixed_ref, weight_ref, out_ref):
    mixed = mixed_ref[...]
    for i in range(out_ref.shape[0]):
        out_ref[i] = jnp.dot(mixed, weight_ref[first + i], preferred_element_type=F32).astype(out_ref.dtype)


def last_kernel(blocks_last, mixed_ref, weight_hbm, out_ref, weight_near, sem):
    copies = weight_copies(blocks_last, weight_hbm, weight_near, sem)
    for copy in copies:
        copy.start()
    for copy in copies:
        copy.wait()
    project_kernel(0, mixed_ref, weight_near, out_ref)


def finish_kernel(span, count, *refs):
    (*held, arrived), (out_hbm, turned, sem) = refs[: count + 1], refs[-3:]
    first, last = span
    step = min(LANES, last - first)
    copies = []
    for i, start in enumerate(range(0, last - first, step)):
        cols = slice(start, start + step)
        total = arrived[:, cols].astype(F32)
        for ref in held:
            total = total + ref[:, first + start : first + start + step].astype(F32)
        turned[cols] = total.T
        copies.append(pltpu.make_async_copy(turned.at[cols], out_hbm.at[first + start : first + start + step], sem.at[i]))
        copies[-1].start()
    for copy in copies:
        copy.wait()


def gated_kernel(smalls, key_hbm, value_hbm, *refs):
    small_hbms, (*out_refs, key_ref, value_ref, sem, small_sem) = refs[:smalls], refs[smalls:]
    out_refs, small_refs = out_refs[:-smalls], out_refs[-smalls:]
    pieces = len(out_refs)
    unit = out_refs[0].shape[1]
    copies = []
    for k in range(pieces):
        cols = pl.ds(pl.multiple_of((first_piece(pieces) ^ k) * unit, LANES), unit)
        copies.append(pltpu.make_async_copy(key_hbm.at[:, cols], key_ref.at[k], sem.at[0, k]))
        copies.append(pltpu.make_async_copy(value_hbm.at[:, cols], value_ref.at[k], sem.at[1, k]))
    fetches = [pltpu.make_async_copy(s, t, small_sem.at[i]) for i, (s, t) in enumerate(zip(small_hbms, small_refs))]
    for copy in copies + fetches:
        copy.start()
    for k, out_ref in enumerate(out_refs):
        copies[2 * k].wait()
        copies[2 * k + 1].wait()
        out_ref[...] = (key_ref[k].astype(F32) * value_ref[k].astype(F32)).astype(BF16)
    for fetch in fetches:
        fetch.wait()


def local(
    query, key_gate, value, group_order, emb_weight, emb_bias, mid_weight, mid_bias, out_filter, decay_rate, skip_gain,
    out_weight,
):
    rows, chan_width = query.shape
    seq_count, chan_count = lax.axis_size("seq"), lax.axis_size("chan")
    seq_index, chan_index = lax.axis_index("seq"), lax.axis_index("chan")
    length = rows * seq_count
    slots = length // GROUP
    width = chan_width // seq_count
    block = max(2 * GROUP, length // 16)
    blocks = length // block
    emb, order = emb_weight.shape
    head, head_tail, inverse = packed_tables(block)
    feat_rows = -(-(emb + 1) // 8) * 8
    features = feature_table(length, (emb - 1) // 2, feat_rows)

    limit = pltpu.CompilerParams(vmem_limit_bytes=20 << 20)
    in_vmem = pl.BlockSpec(memory_space=pltpu.VMEM)
    in_smem = pl.BlockSpec(memory_space=pltpu.SMEM)
    in_hbm = pl.BlockSpec(memory_space=pltpu.HBM)
    far = lambda operand: pltpu.with_memory_space_constraint(operand, pltpu.HBM)
    unit = width if width % LANES == 0 else chan_width
    pieces = chan_width // unit

    arrival = sorted(range(seq_count), key=lambda k: (k & 1, k))

    def swap(arrays):
        return [arrays[0]] + [
            lax.ppermute(arrays[k], "seq", [(d, d ^ k) for d in range(seq_count)]) for k in range(1, seq_count)
        ]

    decay = decay_rate.reshape(seq_count, width)
    if pieces == 1:
        pad = [(0, 0), (0, LANES - width)]
        decay = jnp.pad(lax.dynamic_slice_in_dim(decay, seq_index, 1), pad)
    smalls = (features, emb_weight, emb_bias[None, :], mid_weight, mid_bias[None, :], decay, head_tail)
    near = pl.pallas_call(
        functools.partial(gated_kernel, len(smalls)),
        out_shape=[
            *[jax.ShapeDtypeStruct((rows, unit), BF16)] * pieces,
            *[jax.ShapeDtypeStruct(small.shape, small.dtype) for small in smalls],
        ],
        in_specs=[in_hbm] * (2 + len(smalls)),
        out_specs=[in_vmem] * (pieces + len(smalls)),
        scratch_shapes=[
            pltpu.VMEM((pieces, rows, unit), BF16),
            pltpu.VMEM((pieces, rows, unit), BF16),
            pltpu.SemaphoreType.DMA((2, pieces)),
            pltpu.SemaphoreType.DMA((len(smalls),)),
        ],
        compiler_params=limit,
    )(*map(far, (key_gate, value, *smalls)))
    signal, smalls = near[:pieces], near[pieces:]
    if pieces > 1:
        spread = swap(signal)
    else:
        in_order = signal[0].reshape(rows, seq_count, width).transpose(1, 0, 2)
        in_order = lax.all_to_all(in_order, "seq", 0, 0, tiled=True)
        spread = list(jnp.pad(in_order, [(0, 0), (0, 0), (0, LANES - width)]))

    my_filter = lax.dynamic_slice_in_dim(out_filter, seq_index * width, width, 1)
    if pieces == 1:
        my_filter = jnp.pad(my_filter, pad)
    out_width = out_weight.shape[1] // chan_count
    quarter = chan_count // 4
    odd = range(1, chan_count, 2)
    far_odd, near_odd = [j for j in odd if j & 2], [j for j in odd if not j & 2]
    blocks_first, blocks_next, blocks_last = far_odd + [j ^ 1 for j in far_odd], near_odd, [j ^ 1 for j in near_odd]
    real, imag, edge, weights_first, query_near = pl.pallas_call(
        functools.partial(filter_kernel, block, blocks_first, pieces > 1),
        out_shape=(
            jax.ShapeDtypeStruct((blocks, block, LANES), F32),
            jax.ShapeDtypeStruct((blocks, block, LANES), F32),
            jax.ShapeDtypeStruct((blocks, 16, LANES), F32),
            jax.ShapeDtypeStruct((2 * quarter, chan_width, out_width), BF16),
            jax.ShapeDtypeStruct(query.shape, BF16),
        ),
        in_specs=[in_vmem] * 8 + [in_hbm] * 2,
        out_specs=[in_vmem] * 5,
        scratch_shapes=[
            pltpu.VMEM((feat_rows, order), F32),
            pltpu.VMEM((order + 8, order), F32),
            pltpu.VMEM((order + 8, length), F32),
            pltpu.VMEM((length + block, LANES), BF16),
            pltpu.SemaphoreType.DMA((2 * quarter,)),
            pltpu.SemaphoreType.DMA((1,)),
        ],
        compiler_params=limit,
    )(my_filter, *smalls, far(out_weight), far(query))

    *convolved, weights_next = pl.pallas_call(
        functools.partial(conv_kernel, block, blocks_next, arrival, pieces > 1),
        out_shape=[
            *[jax.ShapeDtypeStruct((rows, LANES), BF16)] * seq_count,
            jax.ShapeDtypeStruct((quarter, chan_width, out_width), BF16),
        ],
        in_specs=[in_smem] + [in_vmem] * 5 + [in_hbm] + [in_vmem] * seq_count,
        out_specs=[in_vmem] * (seq_count + 1),
        scratch_shapes=[
            pltpu.VMEM((length, LANES), BF16),
            pltpu.VMEM((blocks, block, LANES), F32),
            pltpu.VMEM((blocks, block, LANES), F32),
            pltpu.VMEM((2 * block, blocks * LANES), BF16),
            pltpu.VMEM((length, LANES), BF16),
            pltpu.SemaphoreType.DMA((quarter,)),
        ],
        compiler_params=limit,
    )(group_order, real, imag, edge, head, inverse, far(out_weight), *[spread[k] for k in arrival])
    if pieces > 1:
        backs = swap(convolved)
    else:
        in_order = lax.all_to_all(jnp.stack([piece[:, :width] for piece in convolved]), "seq", 0, 0, tiled=True)
        backs = [in_order.transpose(1, 0, 2).reshape(rows, chan_width)]

    def exchange(terms, bit):
        return lax.ppermute(terms, "chan", [(d, d ^ bit) for d in range(chan_count)])

    far_away, mixed = pl.pallas_call(
        functools.partial(mix_kernel, arrival if pieces > 1 else [0]),
        out_shape=(
            jax.ShapeDtypeStruct((quarter, rows, out_width), BF16),
            jax.ShapeDtypeStruct((rows, chan_width), BF16),
        ),
        in_specs=[in_vmem] * (3 + 2 * pieces),
        out_specs=[in_vmem] * 2,
        compiler_params=limit,
    )(query_near, skip_gain[None, :], weights_first, *[array[k] for array in (backs, signal) for k in (arrival if pieces > 1 else [0])])
    far_terms = exchange(far_away, 1)

    def products(first, weights, dtype):
        return pl.pallas_call(
            functools.partial(project_kernel, first),
            out_shape=jax.ShapeDtypeStruct((quarter, rows, out_width), dtype),
            in_specs=[in_vmem] * 2,
            out_specs=in_vmem,
            compiler_params=limit,
        )(mixed, weights)

    far_kept, near_away = products(quarter, weights_first, F32), products(0, weights_next, BF16)
    spans = [(0, out_width // 2), (out_width // 2, out_width)]
    send = [(far_kept[:, :, a:b] + far_terms[:, :, a:b].astype(F32)).astype(BF16) for a, b in spans]
    send, near_away, mixed = lax.optimization_barrier((send, near_away, mixed))
    sent = [exchange(piece, 2) for piece in send]
    near_terms = exchange(near_away, 1)
    near_kept = pl.pallas_call(
        functools.partial(last_kernel, blocks_last),
        out_shape=jax.ShapeDtypeStruct((quarter, rows, out_width), F32),
        in_specs=[in_vmem, in_hbm],
        out_specs=in_vmem,
        scratch_shapes=[
            pltpu.VMEM((quarter, chan_width, out_width), BF16),
            pltpu.SemaphoreType.DMA((quarter,)),
        ],
        compiler_params=limit,
    )(mixed, far(out_weight))
    terms = [near_kept, near_terms]
    bit = 4
    while bit < chan_count:
        total = sum(term.astype(F32) for term in (*terms, jnp.concatenate(sent, 2)))
        terms, sent, spans = [total[0::2]], [exchange(total[1::2].astype(BF16), bit)], [(0, out_width)]
        bit *= 2
    result = []
    for span, piece in zip(spans, sent):
        operands = [*[term[0] for term in terms], piece[0]]
        result = [
            pl.pallas_call(
                functools.partial(finish_kernel, span, len(terms)),
                out_shape=jax.ShapeDtypeStruct((out_width, rows), F32),
                in_specs=[in_vmem] * len(operands) + [in_hbm] * len(result),
                out_specs=in_hbm,
                scratch_shapes=[
                    pltpu.VMEM((span[1] - span[0], rows), F32),
                    pltpu.SemaphoreType.DMA((max(1, (span[1] - span[0]) // LANES),)),
                ],
                input_output_aliases={len(operands): 0} if result else {},
                compiler_params=limit,
            )(*operands, *result)
        ]
    return result[0]


def solution(mesh):
    return jax.shard_map(
        local,
        mesh=mesh,
        in_specs=(
            P("seq", "chan"), P("seq", "chan"), P("seq", "chan"), P(), P(), P(), P(), P(), P(None, "chan"), P("chan"),
            P("chan"), P("chan", None),
        ),
        out_specs=P("chan", "seq"),
        check_vma=False,
    )
```

```python
import functools
import math

import jax
import jax.numpy as jnp
import numpy as np
from jax import lax
from jax.experimental import pallas as pl
from jax.experimental.pallas import tpu as pltpu
from jax.sharding import PartitionSpec as P

GROUP = 128
LANES = 128
SINE_FREQ = 2.0
F32 = jnp.float32
BF16 = jnp.bfloat16


def packed_tables(block):
    period = 2 * block
    row = np.arange(block)
    freq = np.arange(block)

    def forward(shift):
        angle = 2.0 * np.pi * (freq[:, None] * (row[None, :] + shift) % period) / period
        real, imag = np.cos(angle), -np.sin(angle)
        imag[0] = np.where((row + shift) % 2 == 0, 1.0, -1.0)
        return np.concatenate([real, imag], 0)

    head, tail = forward(0), forward(block)
    tail[:, 0] = 0.0
    weight = np.where(freq == 0, 1.0, 2.0) / period
    angle = 2.0 * np.pi * (row[:, None] * freq[None, :] % period) / period
    real, imag = np.cos(angle) * weight, -np.sin(angle) * weight
    imag[:, 0] = np.where(row % 2 == 0, 1.0, -1.0) / period
    inverse = np.concatenate([real, imag], 1)
    to_bf16 = lambda table: jnp.asarray(table.astype(np.float32)).astype(BF16)
    return to_bf16(head), to_bf16(np.concatenate([head, tail], 1)), to_bf16(inverse)


def feature_table(length, bands, rows):
    lag = np.arange(length)
    angle = 2.0 * np.pi * (np.arange(1, bands + 1)[:, None] * lag[None, :] % length) / length
    table = np.zeros((rows, length), np.float32)
    table[0] = lag / length
    table[1 : bands + 1] = np.cos(angle)
    table[bands + 1 : 2 * bands + 1] = np.sin(angle)
    table[2 * bands + 1] = 1.0
    return jnp.asarray(table)


def sine(x):
    n = jnp.round(x * (1.0 / math.pi))
    r = x - n * 3.140625
    r = r - n * 9.67502593994140625e-4
    r = r - n * 1.509957990978376432e-7
    square = r * r
    series = jnp.full_like(r, -2.5052108e-8)
    for term in (2.7557319e-6, -1.9841270e-4, 8.3333333e-3, -1.6666667e-1):
        series = series * square + term
    odd = n * 0.5 - jnp.floor(n * 0.5)
    return (r + r * square * series) * (1.0 - 4.0 * odd)


def contract_first(lhs, rhs):
    return lax.dot_general(
        lhs, rhs, (((0,), (0,)), ((), ())), precision=lax.Precision.HIGHEST, preferred_element_type=F32
    )


def first_piece(pieces):
    return lax.axis_index("seq") if pieces > 1 else 0


def weight_copies(blocks, weight_hbm, weight_out, sem):
    width = weight_out.shape[2]
    copies = []
    for i, j in enumerate(blocks):
        cols = pl.ds(pl.multiple_of((lax.axis_index("chan") ^ j) * width, LANES), width)
        copies.append(pltpu.make_async_copy(weight_hbm.at[:, cols], weight_out.at[i], sem.at[i]))
    return copies


def one_minus_exp(y):
    series = jnp.full_like(y, -1.0 / 40320)
    for term in (5040, -720, 120, -24, 6, -2, 1):
        series = series * y + 1.0 / term
    return jnp.where(y < 0.5, y * series, 1.0 - jnp.exp(-y))


def filter_kernel(block, blocks_first, relative, out_w_ref, *refs):
    smalls, weight_hbm, refs = refs[:7], refs[7], refs[8:]
    (real_ref, imag_ref, edge_ref, weight_out), refs = refs[:4], refs[4:]
    near, (w1, w2, hid, filt, near_sem, weight_sem) = refs[:7], refs[7:]
    feat_ref, emb_w_ref, emb_b_ref, mid_w_ref, mid_b_ref, decay_all, table_ref = near
    fetches = [pltpu.make_async_copy(s, t, near_sem.at[i]) for i, (s, t) in enumerate(zip(smalls, near))]
    for fetch in fetches:
        fetch.start()
    for fetch in fetches[:-1]:
        fetch.wait()
    copies = weight_copies(blocks_first, weight_hbm, weight_out, weight_sem)
    for copy in copies:
        copy.start()
    emb, order = emb_w_ref.shape
    length = feat_ref.shape[1]
    blocks = length // block
    w1[...] = jnp.zeros_like(w1)
    w1[0:emb, :] = emb_w_ref[...]
    w1[emb : emb + 1, :] = emb_b_ref[...]
    w2[...] = jnp.zeros_like(w2)
    w2[0:order, :] = mid_w_ref[...]
    w2[order : order + 1, :] = mid_b_ref[...]
    hid[order:, :] = jnp.ones_like(hid[order:, :])
    hid[0:order, :] = sine(SINE_FREQ * contract_first(w1[...], feat_ref[...]))
    hidden = sine(SINE_FREQ * contract_first(w2[...], hid[...]))
    raw = contract_first(out_w_ref[...], hidden).T
    decay = decay_all[pl.ds(lax.axis_index("seq") if relative else 0, 1), :]
    within = jnp.exp(-decay * lax.broadcasted_iota(jnp.int32, (block, LANES), 0).astype(F32))
    within = within * jnp.sqrt(one_minus_exp(2.0 * decay))
    filt[0:block, :] = jnp.zeros((block, LANES), BF16)
    for m in range(blocks):
        start = jnp.exp(-decay * float(m * block))
        filt[(m + 1) * block : (m + 2) * block, :] = (raw[m * block : (m + 1) * block] * (within * start)).astype(BF16)
    first_row = lax.broadcasted_iota(jnp.int32, (16, LANES), 0) == 0
    fetches[-1].wait()
    group = 2
    for m0 in range(0, blocks, group):
        stacked = jnp.concatenate(
            [
                jnp.concatenate(
                    [filt[(m + 1) * block : (m + 2) * block, :], filt[m * block : (m + 1) * block, :]], 0
                )
                for m in range(m0, m0 + group)
            ],
            1,
        )
        spectrum = jnp.dot(table_ref[...], stacked, preferred_element_type=F32)
        for i in range(group):
            m = m0 + i
            real = spectrum[:block, i * LANES : (i + 1) * LANES]
            imag = spectrum[block:, i * LANES : (i + 1) * LANES]
            real_ref[m] = real
            imag_ref[m] = imag
            edge_ref[m] = jnp.where(first_row, imag[:16], real[:16])
            imag_ref[m, 0:16, :] = jnp.where(first_row, 0.0, imag[:16])
    for copy in copies:
        copy.wait()


def conv_kernel(
    block, blocks_next, arrival, relative, order_ref, real_ref, imag_ref, edge_ref, table_ref, inverse_ref, weight_hbm, *refs
):
    *refs, weight_out, sig, sre, sim, spec, conv, weight_sem = refs
    count = len(refs) // 2
    x_refs, out_refs = refs[:count], refs[count:]
    first = first_piece(count if relative else 1)
    copies = weight_copies(blocks_next, weight_hbm, weight_out, weight_sem)
    for copy in copies:
        copy.start()
    groups = x_refs[0].shape[0] // GROUP
    length = sig.shape[0]
    blocks = length // block

    def place(k, i):
        return pl.multiple_of(order_ref[(first ^ k) * groups + i] * GROUP, GROUP)

    for k, x_ref in zip(arrival, x_refs):
        for i in range(groups):
            sig[pl.ds(place(k, i), GROUP), :] = x_ref[i * GROUP : (i + 1) * GROUP, :]
    group = 2
    for b0 in range(0, blocks, group):
        stacked = jnp.concatenate([sig[b * block : (b + 1) * block, :] for b in range(b0, b0 + group)], 1)
        spectrum = jnp.dot(table_ref[...], stacked, preferred_element_type=F32)
        for i in range(group):
            sre[b0 + i] = spectrum[:block, i * LANES : (i + 1) * LANES]
            sim[b0 + i] = spectrum[block:, i * LANES : (i + 1) * LANES]

    def tile(start, first):
        rows = pl.ds(start, 16)
        mirror = pl.ds(block + start, 16)
        s_real = [sre[q, rows, :] for q in range(blocks)]
        s_imag = [sim[q, rows, :] for q in range(blocks)]
        for g in range(blocks):
            acc_real = acc_imag = None
            for q in range(g + 1):
                fr, fi = real_ref[g - q, rows, :], imag_ref[g - q, rows, :]
                fe = edge_ref[g - q] if first else fr
                re = fr * s_real[q] - fi * s_imag[q]
                im = fe * s_imag[q] + fi * s_real[q]
                acc_real = re if q == 0 else acc_real + re
                acc_imag = im if q == 0 else acc_imag + im
            spec[rows, g * LANES : (g + 1) * LANES] = acc_real.astype(BF16)
            spec[mirror, g * LANES : (g + 1) * LANES] = acc_imag.astype(BF16)

    tile(0, True)

    @pl.loop(1, block // 16)
    def _(t):
        tile(pl.multiple_of(t * 16, 16), False)

    result = jnp.dot(inverse_ref[...], spec[...], preferred_element_type=F32)
    for g in range(blocks):
        conv[g * block : (g + 1) * block, :] = result[:, g * LANES : (g + 1) * LANES].astype(BF16)
    for k, out_ref in enumerate(out_refs):
        for i in range(groups):
            out_ref[i * GROUP : (i + 1) * GROUP, :] = conv[pl.ds(place(k, i), GROUP), :]
    for copy in copies:
        copy.wait()


def copy_kernel(blocks_next, after_ref, weight_hbm, query_hbm, weight_out, query_out, weight_sem, query_sem):
    copies = weight_copies(blocks_next, weight_hbm, weight_out, weight_sem)
    copies.append(pltpu.make_async_copy(query_hbm, query_out, query_sem.at[0]))
    for copy in copies:
        copy.start()
    for copy in copies:
        copy.wait()


def mix_kernel(arrival, query_ref, gain_ref, weight_ref, *refs):
    *refs, out_ref, mixed_ref = refs
    pieces = len(refs) // 2
    unit = refs[0].shape[1]
    for k, back_ref, sig_ref in zip(arrival, refs[:pieces], refs[pieces:]):
        cols = pl.ds(pl.multiple_of((first_piece(pieces) ^ k) * unit, LANES), unit)
        inner = back_ref[...].astype(F32) + gain_ref[:, cols] * sig_ref[...].astype(F32)
        mixed_ref[:, cols] = (query_ref[:, cols].astype(F32) * inner).astype(BF16)
    project_kernel(0, mixed_ref, weight_ref, out_ref)


def project_kernel(first, mixed_ref, weight_ref, out_ref):
    mixed = mixed_ref[...]
    for i in range(out_ref.shape[0]):
        out_ref[i] = jnp.dot(mixed, weight_ref[first + i], preferred_element_type=F32).astype(out_ref.dtype)


def last_kernel(blocks_last, mixed_ref, weight_hbm, out_ref, weight_near, sem):
    copies = weight_copies(blocks_last, weight_hbm, weight_near, sem)
    for copy in copies:
        copy.start()
    for copy in copies:
        copy.wait()
    project_kernel(0, mixed_ref, weight_near, out_ref)


def finish_kernel(span, count, *refs):
    (*held, arrived), (out_hbm, turned, sem) = refs[: count + 1], refs[-3:]
    first, last = span
    step = min(LANES, last - first)
    copies = []
    for i, start in enumerate(range(0, last - first, step)):
        cols = slice(start, start + step)
        total = arrived[:, cols].astype(F32)
        for ref in held:
            total = total + ref[:, first + start : first + start + step].astype(F32)
        turned[cols] = total.T
        copies.append(pltpu.make_async_copy(turned.at[cols], out_hbm.at[first + start : first + start + step], sem.at[i]))
        copies[-1].start()
    for copy in copies:
        copy.wait()


def gated_kernel(key_hbm, value_hbm, *refs):
    *out_refs, key_ref, value_ref, sem = refs
    pieces = len(out_refs)
    unit = out_refs[0].shape[1]
    copies = []
    for k in range(pieces):
        cols = pl.ds(pl.multiple_of((first_piece(pieces) ^ k) * unit, LANES), unit)
        copies.append(pltpu.make_async_copy(key_hbm.at[:, cols], key_ref.at[k], sem.at[0, k]))
        copies.append(pltpu.make_async_copy(value_hbm.at[:, cols], value_ref.at[k], sem.at[1, k]))
    for copy in copies:
        copy.start()
    for k, out_ref in enumerate(out_refs):
        copies[2 * k].wait()
        copies[2 * k + 1].wait()
        out_ref[...] = (key_ref[k].astype(F32) * value_ref[k].astype(F32)).astype(BF16)


def local(
    query, key_gate, value, group_order, emb_weight, emb_bias, mid_weight, mid_bias, out_filter, decay_rate, skip_gain,
    out_weight,
):
    rows, chan_width = query.shape
    seq_count, chan_count = lax.axis_size("seq"), lax.axis_size("chan")
    seq_index, chan_index = lax.axis_index("seq"), lax.axis_index("chan")
    length = rows * seq_count
    slots = length // GROUP
    width = chan_width // seq_count
    block = max(2 * GROUP, length // 16)
    blocks = length // block
    emb, order = emb_weight.shape
    head, head_tail, inverse = packed_tables(block)
    feat_rows = -(-(emb + 1) // 8) * 8
    features = feature_table(length, (emb - 1) // 2, feat_rows)

    limit = pltpu.CompilerParams(vmem_limit_bytes=20 << 20)
    in_vmem = pl.BlockSpec(memory_space=pltpu.VMEM)
    in_smem = pl.BlockSpec(memory_space=pltpu.SMEM)
    in_hbm = pl.BlockSpec(memory_space=pltpu.HBM)
    far = lambda operand: pltpu.with_memory_space_constraint(operand, pltpu.HBM)
    unit = width if width % LANES == 0 else chan_width
    pieces = chan_width // unit

    arrival = sorted(range(seq_count), key=lambda k: (k & 1, k))

    def swap(arrays):
        return [arrays[0]] + [
            lax.ppermute(arrays[k], "seq", [(d, d ^ k) for d in range(seq_count)]) for k in range(1, seq_count)
        ]

    signal = pl.pallas_call(
        gated_kernel,
        out_shape=[jax.ShapeDtypeStruct((rows, unit), BF16)] * pieces,
        in_specs=[in_hbm] * 2,
        out_specs=[in_vmem] * pieces,
        scratch_shapes=[
            pltpu.VMEM((pieces, rows, unit), BF16),
            pltpu.VMEM((pieces, rows, unit), BF16),
            pltpu.SemaphoreType.DMA((2, pieces)),
        ],
        compiler_params=limit,
    )(far(key_gate), far(value))
    if pieces > 1:
        spread = swap(signal)
    else:
        in_order = signal[0].reshape(rows, seq_count, width).transpose(1, 0, 2)
        in_order = lax.all_to_all(in_order, "seq", 0, 0, tiled=True)
        spread = list(jnp.pad(in_order, [(0, 0), (0, 0), (0, LANES - width)]))

    my_filter = lax.dynamic_slice_in_dim(out_filter, seq_index * width, width, 1)
    decay = decay_rate.reshape(seq_count, width)
    if pieces == 1:
        pad = [(0, 0), (0, LANES - width)]
        my_filter = jnp.pad(my_filter, pad)
        decay = jnp.pad(lax.dynamic_slice_in_dim(decay, seq_index, 1), pad)
    out_width = out_weight.shape[1] // chan_count
    quarter = chan_count // 4
    odd = range(1, chan_count, 2)
    far_odd, near_odd = [j for j in odd if j & 2], [j for j in odd if not j & 2]
    blocks_kept, blocks_last = [j ^ 1 for j in far_odd], [j ^ 1 for j in near_odd]
    smalls = (
        features, emb_weight, emb_bias[None, :], mid_weight, mid_bias[None, :], decay, head_tail,
    )
    real, imag, edge, weights_away = pl.pallas_call(
        functools.partial(filter_kernel, block, far_odd, pieces > 1),
        out_shape=(
            jax.ShapeDtypeStruct((blocks, block, LANES), F32),
            jax.ShapeDtypeStruct((blocks, block, LANES), F32),
            jax.ShapeDtypeStruct((blocks, 16, LANES), F32),
            jax.ShapeDtypeStruct((quarter, chan_width, out_width), BF16),
        ),
        in_specs=[in_vmem] + [in_hbm] * 8,
        out_specs=[in_vmem] * 4,
        scratch_shapes=[
            *[pltpu.VMEM(small.shape, small.dtype) for small in smalls],
            pltpu.VMEM((feat_rows, order), F32),
            pltpu.VMEM((order + 8, order), F32),
            pltpu.VMEM((order + 8, length), F32),
            pltpu.VMEM((length + block, LANES), BF16),
            pltpu.SemaphoreType.DMA((len(smalls),)),
            pltpu.SemaphoreType.DMA((quarter,)),
        ],
        compiler_params=limit,
    )(my_filter, *map(far, (*smalls, out_weight)))

    *convolved, weights_kept = pl.pallas_call(
        functools.partial(conv_kernel, block, blocks_kept, arrival, pieces > 1),
        out_shape=[
            *[jax.ShapeDtypeStruct((rows, LANES), BF16)] * seq_count,
            jax.ShapeDtypeStruct((quarter, chan_width, out_width), BF16),
        ],
        in_specs=[in_smem] + [in_vmem] * 5 + [in_hbm] + [in_vmem] * seq_count,
        out_specs=[in_vmem] * (seq_count + 1),
        scratch_shapes=[
            pltpu.VMEM((length, LANES), BF16),
            pltpu.VMEM((blocks, block, LANES), F32),
            pltpu.VMEM((blocks, block, LANES), F32),
            pltpu.VMEM((2 * block, blocks * LANES), BF16),
            pltpu.VMEM((length, LANES), BF16),
            pltpu.SemaphoreType.DMA((quarter,)),
        ],
        compiler_params=limit,
    )(group_order, real, imag, edge, head, inverse, far(out_weight), *[spread[k] for k in arrival])
    weights_next, query_near = pl.pallas_call(
        functools.partial(copy_kernel, near_odd),
        out_shape=(
            jax.ShapeDtypeStruct((quarter, chan_width, out_width), BF16),
            jax.ShapeDtypeStruct(query.shape, BF16),
        ),
        in_specs=[in_vmem] + [in_hbm] * 2,
        out_specs=[in_vmem] * 2,
        scratch_shapes=[pltpu.SemaphoreType.DMA((quarter,)), pltpu.SemaphoreType.DMA((1,))],
        compiler_params=limit,
    )(convolved[0], far(out_weight), far(query))
    if pieces > 1:
        backs = swap(convolved)
    else:
        in_order = lax.all_to_all(jnp.stack([piece[:, :width] for piece in convolved]), "seq", 0, 0, tiled=True)
        backs = [in_order.transpose(1, 0, 2).reshape(rows, chan_width)]

    def exchange(terms, bit):
        return lax.ppermute(terms, "chan", [(d, d ^ bit) for d in range(chan_count)])

    far_away, mixed = pl.pallas_call(
        functools.partial(mix_kernel, arrival if pieces > 1 else [0]),
        out_shape=(
            jax.ShapeDtypeStruct((quarter, rows, out_width), BF16),
            jax.ShapeDtypeStruct((rows, chan_width), BF16),
        ),
        in_specs=[in_vmem] * (3 + 2 * pieces),
        out_specs=[in_vmem] * 2,
        compiler_params=limit,
    )(query_near, skip_gain[None, :], weights_away, *[array[k] for array in (backs, signal) for k in (arrival if pieces > 1 else [0])])
    far_terms = exchange(far_away, 1)

    def products(first, weights, dtype):
        return pl.pallas_call(
            functools.partial(project_kernel, first),
            out_shape=jax.ShapeDtypeStruct((quarter, rows, out_width), dtype),
            in_specs=[in_vmem] * 2,
            out_specs=in_vmem,
            compiler_params=limit,
        )(mixed, weights)

    far_kept, near_away = products(0, weights_kept, F32), products(0, weights_next, BF16)
    spans = [(0, out_width // 2), (out_width // 2, out_width)]
    send = [(far_kept[:, :, a:b] + far_terms[:, :, a:b].astype(F32)).astype(BF16) for a, b in spans]
    send, near_away, mixed = lax.optimization_barrier((send, near_away, mixed))
    sent = [exchange(piece, 2) for piece in send]
    near_terms = exchange(near_away, 1)
    near_kept = pl.pallas_call(
        functools.partial(last_kernel, blocks_last),
        out_shape=jax.ShapeDtypeStruct((quarter, rows, out_width), F32),
        in_specs=[in_vmem, in_hbm],
        out_specs=in_vmem,
        scratch_shapes=[
            pltpu.VMEM((quarter, chan_width, out_width), BF16),
            pltpu.SemaphoreType.DMA((quarter,)),
        ],
        compiler_params=limit,
    )(mixed, far(out_weight))
    terms = [near_kept, near_terms]
    bit = 4
    while bit < chan_count:
        total = sum(term.astype(F32) for term in (*terms, jnp.concatenate(sent, 2)))
        terms, sent, spans = [total[0::2]], [exchange(total[1::2].astype(BF16), bit)], [(0, out_width)]
        bit *= 2
    result = []
    for span, piece in zip(spans, sent):
        operands = [*[term[0] for term in terms], piece[0]]
        result = [
            pl.pallas_call(
                functools.partial(finish_kernel, span, len(terms)),
                out_shape=jax.ShapeDtypeStruct((out_width, rows), F32),
                in_specs=[in_vmem] * len(operands) + [in_hbm] * len(result),
                out_specs=in_hbm,
                scratch_shapes=[
                    pltpu.VMEM((span[1] - span[0], rows), F32),
                    pltpu.SemaphoreType.DMA((max(1, (span[1] - span[0]) // LANES),)),
                ],
                input_output_aliases={len(operands): 0} if result else {},
                compiler_params=limit,
            )(*operands, *result)
        ]
    return result[0]


def solution(mesh):
    return jax.shard_map(
        local,
        mesh=mesh,
        in_specs=(
            P("seq", "chan"), P("seq", "chan"), P("seq", "chan"), P(), P(), P(), P(), P(), P(None, "chan"), P("chan"),
            P("chan"), P("chan", None),
        ),
        out_specs=P("chan", "seq"),
        check_vma=False,
    )
```

```python
import functools
import math

import jax
import jax.numpy as jnp
import numpy as np
from jax import lax
from jax.experimental import pallas as pl
from jax.experimental.pallas import tpu as pltpu
from jax.sharding import PartitionSpec as P

GROUP = 128
LANES = 128
SINE_FREQ = 2.0
F32 = jnp.float32
BF16 = jnp.bfloat16


def packed_tables(block):
    period = 2 * block
    row = np.arange(block)
    freq = np.arange(block)

    def forward(shift):
        angle = 2.0 * np.pi * (freq[:, None] * (row[None, :] + shift) % period) / period
        real, imag = np.cos(angle), -np.sin(angle)
        imag[0] = np.where((row + shift) % 2 == 0, 1.0, -1.0)
        return np.concatenate([real, imag], 0)

    head, tail = forward(0), forward(block)
    tail[:, 0] = 0.0
    weight = np.where(freq == 0, 1.0, 2.0) / period
    angle = 2.0 * np.pi * (row[:, None] * freq[None, :] % period) / period
    real, imag = np.cos(angle) * weight, -np.sin(angle) * weight
    imag[:, 0] = np.where(row % 2 == 0, 1.0, -1.0) / period
    inverse = np.concatenate([real, imag], 1)
    to_bf16 = lambda table: jnp.asarray(table.astype(np.float32)).astype(BF16)
    return to_bf16(head), to_bf16(np.concatenate([head, tail], 1)), to_bf16(inverse)


def feature_table(length, bands, rows):
    lag = np.arange(length)
    angle = 2.0 * np.pi * (np.arange(1, bands + 1)[:, None] * lag[None, :] % length) / length
    table = np.zeros((rows, length), np.float32)
    table[0] = lag / length
    table[1 : bands + 1] = np.cos(angle)
    table[bands + 1 : 2 * bands + 1] = np.sin(angle)
    table[2 * bands + 1] = 1.0
    return jnp.asarray(table)


def sine(x):
    n = jnp.round(x * (1.0 / math.pi))
    r = x - n * 3.140625
    r = r - n * 9.67502593994140625e-4
    r = r - n * 1.509957990978376432e-7
    square = r * r
    series = jnp.full_like(r, -2.5052108e-8)
    for term in (2.7557319e-6, -1.9841270e-4, 8.3333333e-3, -1.6666667e-1):
        series = series * square + term
    odd = n * 0.5 - jnp.floor(n * 0.5)
    return (r + r * square * series) * (1.0 - 4.0 * odd)


def contract_first(lhs, rhs):
    return lax.dot_general(
        lhs, rhs, (((0,), (0,)), ((), ())), precision=lax.Precision.HIGHEST, preferred_element_type=F32
    )


def first_piece(pieces):
    return lax.axis_index("seq") if pieces > 1 else 0


def weight_copies(blocks, weight_hbm, weight_out, sem):
    width = weight_out.shape[2]
    copies = []
    for i, j in enumerate(blocks):
        cols = pl.ds(pl.multiple_of((lax.axis_index("chan") ^ j) * width, LANES), width)
        copies.append(pltpu.make_async_copy(weight_hbm.at[:, cols], weight_out.at[i], sem.at[i]))
    return copies


def one_minus_exp(y):
    series = jnp.full_like(y, -1.0 / 40320)
    for term in (5040, -720, 120, -24, 6, -2, 1):
        series = series * y + 1.0 / term
    return jnp.where(y < 0.5, y * series, 1.0 - jnp.exp(-y))


def filter_kernel(block, blocks_first, relative, out_w_ref, *refs):
    smalls, weight_hbm, refs = refs[:7], refs[7], refs[8:]
    (real_ref, imag_ref, edge_ref, weight_out), refs = refs[:4], refs[4:]
    near, (w1, w2, hid, filt, near_sem, weight_sem) = refs[:7], refs[7:]
    feat_ref, emb_w_ref, emb_b_ref, mid_w_ref, mid_b_ref, decay_all, table_ref = near
    fetches = [pltpu.make_async_copy(s, t, near_sem.at[i]) for i, (s, t) in enumerate(zip(smalls, near))]
    for fetch in fetches:
        fetch.start()
    for fetch in fetches[:-1]:
        fetch.wait()
    copies = weight_copies(blocks_first, weight_hbm, weight_out, weight_sem)
    for copy in copies:
        copy.start()
    emb, order = emb_w_ref.shape
    length = feat_ref.shape[1]
    blocks = length // block
    w1[...] = jnp.zeros_like(w1)
    w1[0:emb, :] = emb_w_ref[...]
    w1[emb : emb + 1, :] = emb_b_ref[...]
    w2[...] = jnp.zeros_like(w2)
    w2[0:order, :] = mid_w_ref[...]
    w2[order : order + 1, :] = mid_b_ref[...]
    hid[order:, :] = jnp.ones_like(hid[order:, :])
    hid[0:order, :] = sine(SINE_FREQ * contract_first(w1[...], feat_ref[...]))
    hidden = sine(SINE_FREQ * contract_first(w2[...], hid[...]))
    raw = contract_first(out_w_ref[...], hidden).T
    decay = decay_all[pl.ds(lax.axis_index("seq") if relative else 0, 1), :]
    within = jnp.exp(-decay * lax.broadcasted_iota(jnp.int32, (block, LANES), 0).astype(F32))
    within = within * jnp.sqrt(one_minus_exp(2.0 * decay))
    filt[0:block, :] = jnp.zeros((block, LANES), BF16)
    for m in range(blocks):
        start = jnp.exp(-decay * float(m * block))
        filt[(m + 1) * block : (m + 2) * block, :] = (raw[m * block : (m + 1) * block] * (within * start)).astype(BF16)
    first_row = lax.broadcasted_iota(jnp.int32, (16, LANES), 0) == 0
    fetches[-1].wait()
    group = 2
    for m0 in range(0, blocks, group):
        stacked = jnp.concatenate(
            [
                jnp.concatenate(
                    [filt[(m + 1) * block : (m + 2) * block, :], filt[m * block : (m + 1) * block, :]], 0
                )
                for m in range(m0, m0 + group)
            ],
            1,
        )
        spectrum = jnp.dot(table_ref[...], stacked, preferred_element_type=F32)
        for i in range(group):
            m = m0 + i
            real = spectrum[:block, i * LANES : (i + 1) * LANES]
            imag = spectrum[block:, i * LANES : (i + 1) * LANES]
            real_ref[m] = real
            imag_ref[m] = imag
            edge_ref[m] = jnp.where(first_row, imag[:16], real[:16])
            imag_ref[m, 0:16, :] = jnp.where(first_row, 0.0, imag[:16])
    for copy in copies:
        copy.wait()


def conv_kernel(
    block, blocks_next, arrival, relative, order_ref, real_ref, imag_ref, edge_ref, table_ref, inverse_ref, weight_hbm, *refs
):
    *refs, weight_out, sig, sre, sim, spec, conv, weight_sem = refs
    count = len(refs) // 2
    x_refs, out_refs = refs[:count], refs[count:]
    first = first_piece(count if relative else 1)
    copies = weight_copies(blocks_next, weight_hbm, weight_out, weight_sem)
    for copy in copies:
        copy.start()
    groups = x_refs[0].shape[0] // GROUP
    length = sig.shape[0]
    blocks = length // block

    def place(k, i):
        return pl.multiple_of(order_ref[(first ^ k) * groups + i] * GROUP, GROUP)

    for k, x_ref in zip(arrival, x_refs):
        for i in range(groups):
            sig[pl.ds(place(k, i), GROUP), :] = x_ref[i * GROUP : (i + 1) * GROUP, :]
    group = 2
    for b0 in range(0, blocks, group):
        stacked = jnp.concatenate([sig[b * block : (b + 1) * block, :] for b in range(b0, b0 + group)], 1)
        spectrum = jnp.dot(table_ref[...], stacked, preferred_element_type=F32)
        for i in range(group):
            sre[b0 + i] = spectrum[:block, i * LANES : (i + 1) * LANES]
            sim[b0 + i] = spectrum[block:, i * LANES : (i + 1) * LANES]

    def tile(start, first):
        rows = pl.ds(start, 16)
        mirror = pl.ds(block + start, 16)
        s_real = [sre[q, rows, :] for q in range(blocks)]
        s_imag = [sim[q, rows, :] for q in range(blocks)]
        for g in range(blocks):
            acc_real = acc_imag = None
            for q in range(g + 1):
                fr, fi = real_ref[g - q, rows, :], imag_ref[g - q, rows, :]
                fe = edge_ref[g - q] if first else fr
                re = fr * s_real[q] - fi * s_imag[q]
                im = fe * s_imag[q] + fi * s_real[q]
                acc_real = re if q == 0 else acc_real + re
                acc_imag = im if q == 0 else acc_imag + im
            spec[rows, g * LANES : (g + 1) * LANES] = acc_real.astype(BF16)
            spec[mirror, g * LANES : (g + 1) * LANES] = acc_imag.astype(BF16)

    tile(0, True)

    @pl.loop(1, block // 16)
    def _(t):
        tile(pl.multiple_of(t * 16, 16), False)

    result = jnp.dot(inverse_ref[...], spec[...], preferred_element_type=F32)
    for g in range(blocks):
        conv[g * block : (g + 1) * block, :] = result[:, g * LANES : (g + 1) * LANES].astype(BF16)
    for k, out_ref in enumerate(out_refs):
        for i in range(groups):
            out_ref[i * GROUP : (i + 1) * GROUP, :] = conv[pl.ds(place(k, i), GROUP), :]
    for copy in copies:
        copy.wait()


def copy_kernel(blocks_next, after_ref, gain_ref, weight_hbm, query_hbm, *refs):
    *sig_refs, weight_out, query_out, skip_out, weight_sem, query_sem = refs
    pieces = len(sig_refs)
    unit = sig_refs[0].shape[1]
    columns = [pl.ds(pl.multiple_of((first_piece(pieces) ^ k) * unit, LANES), unit) for k in range(pieces)]
    copies = [
        pltpu.make_async_copy(query_hbm.at[:, cols], query_out.at[k], query_sem.at[k]) for k, cols in enumerate(columns)
    ]
    copies += weight_copies(blocks_next, weight_hbm, weight_out, weight_sem)
    for copy in copies:
        copy.start()
    for k, (cols, sig_ref) in enumerate(zip(columns, sig_refs)):
        skip_out[k] = gain_ref[:, cols] * sig_ref[...].astype(F32)
    for copy in copies:
        copy.wait()


def mix_kernel(arrival, query_ref, skip_ref, weight_ref, *refs):
    *back_refs, out_ref, mixed_ref = refs
    pieces, _, unit = query_ref.shape
    for k, back_ref in zip(arrival, back_refs):
        cols = pl.ds(pl.multiple_of((first_piece(pieces) ^ k) * unit, LANES), unit)
        mixed_ref[:, cols] = (query_ref[k].astype(F32) * (back_ref[...].astype(F32) + skip_ref[k])).astype(BF16)
    project_kernel(0, mixed_ref, weight_ref, out_ref)


def project_kernel(first, mixed_ref, weight_ref, out_ref):
    mixed = mixed_ref[...]
    for i in range(out_ref.shape[0]):
        out_ref[i] = jnp.dot(mixed, weight_ref[first + i], preferred_element_type=F32).astype(out_ref.dtype)


def last_kernel(blocks_last, mixed_ref, weight_hbm, out_ref, weight_near, sem):
    copies = weight_copies(blocks_last, weight_hbm, weight_near, sem)
    for copy in copies:
        copy.start()
    for copy in copies:
        copy.wait()
    project_kernel(0, mixed_ref, weight_near, out_ref)


def finish_kernel(span, count, *refs):
    (*held, arrived), (out_hbm, turned, sem) = refs[: count + 1], refs[-3:]
    first, last = span
    step = min(LANES, last - first)
    copies = []
    for i, start in enumerate(range(0, last - first, step)):
        cols = slice(start, start + step)
        total = arrived[:, cols].astype(F32)
        for ref in held:
            total = total + ref[:, first + start : first + start + step].astype(F32)
        turned[cols] = total.T
        copies.append(pltpu.make_async_copy(turned.at[cols], out_hbm.at[first + start : first + start + step], sem.at[i]))
        copies[-1].start()
    for copy in copies:
        copy.wait()


def gated_kernel(key_hbm, value_hbm, *refs):
    *out_refs, key_ref, value_ref, sem = refs
    pieces = len(out_refs)
    unit = out_refs[0].shape[1]
    copies = []
    for k in range(pieces):
        cols = pl.ds(pl.multiple_of((first_piece(pieces) ^ k) * unit, LANES), unit)
        copies.append(pltpu.make_async_copy(key_hbm.at[:, cols], key_ref.at[k], sem.at[0, k]))
        copies.append(pltpu.make_async_copy(value_hbm.at[:, cols], value_ref.at[k], sem.at[1, k]))
    for copy in copies:
        copy.start()
    for k, out_ref in enumerate(out_refs):
        copies[2 * k].wait()
        copies[2 * k + 1].wait()
        out_ref[...] = (key_ref[k].astype(F32) * value_ref[k].astype(F32)).astype(BF16)


def local(
    query, key_gate, value, group_order, emb_weight, emb_bias, mid_weight, mid_bias, out_filter, decay_rate, skip_gain,
    out_weight,
):
    rows, chan_width = query.shape
    seq_count, chan_count = lax.axis_size("seq"), lax.axis_size("chan")
    seq_index, chan_index = lax.axis_index("seq"), lax.axis_index("chan")
    length = rows * seq_count
    slots = length // GROUP
    width = chan_width // seq_count
    block = max(2 * GROUP, length // 16)
    blocks = length // block
    emb, order = emb_weight.shape
    head, head_tail, inverse = packed_tables(block)
    feat_rows = -(-(emb + 1) // 8) * 8
    features = feature_table(length, (emb - 1) // 2, feat_rows)

    limit = pltpu.CompilerParams(vmem_limit_bytes=20 << 20)
    in_vmem = pl.BlockSpec(memory_space=pltpu.VMEM)
    in_smem = pl.BlockSpec(memory_space=pltpu.SMEM)
    in_hbm = pl.BlockSpec(memory_space=pltpu.HBM)
    far = lambda operand: pltpu.with_memory_space_constraint(operand, pltpu.HBM)
    unit = width if width % LANES == 0 else chan_width
    pieces = chan_width // unit

    arrival = sorted(range(seq_count), key=lambda k: (k & 1, k))

    def swap(arrays):
        return [arrays[0]] + [
            lax.ppermute(arrays[k], "seq", [(d, d ^ k) for d in range(seq_count)]) for k in range(1, seq_count)
        ]

    signal = pl.pallas_call(
        gated_kernel,
        out_shape=[jax.ShapeDtypeStruct((rows, unit), BF16)] * pieces,
        in_specs=[in_hbm] * 2,
        out_specs=[in_vmem] * pieces,
        scratch_shapes=[
            pltpu.VMEM((pieces, rows, unit), BF16),
            pltpu.VMEM((pieces, rows, unit), BF16),
            pltpu.SemaphoreType.DMA((2, pieces)),
        ],
        compiler_params=limit,
    )(far(key_gate), far(value))
    if pieces > 1:
        spread = swap(signal)
    else:
        in_order = signal[0].reshape(rows, seq_count, width).transpose(1, 0, 2)
        in_order = lax.all_to_all(in_order, "seq", 0, 0, tiled=True)
        spread = list(jnp.pad(in_order, [(0, 0), (0, 0), (0, LANES - width)]))

    my_filter = lax.dynamic_slice_in_dim(out_filter, seq_index * width, width, 1)
    decay = decay_rate.reshape(seq_count, width)
    if pieces == 1:
        pad = [(0, 0), (0, LANES - width)]
        my_filter = jnp.pad(my_filter, pad)
        decay = jnp.pad(lax.dynamic_slice_in_dim(decay, seq_index, 1), pad)
    out_width = out_weight.shape[1] // chan_count
    quarter = chan_count // 4
    odd = range(1, chan_count, 2)
    far_odd, near_odd = [j for j in odd if j & 2], [j for j in odd if not j & 2]
    blocks_kept, blocks_last = [j ^ 1 for j in far_odd], [j ^ 1 for j in near_odd]
    smalls = (
        features, emb_weight, emb_bias[None, :], mid_weight, mid_bias[None, :], decay, head_tail,
    )
    real, imag, edge, weights_away = pl.pallas_call(
        functools.partial(filter_kernel, block, far_odd, pieces > 1),
        out_shape=(
            jax.ShapeDtypeStruct((blocks, block, LANES), F32),
            jax.ShapeDtypeStruct((blocks, block, LANES), F32),
            jax.ShapeDtypeStruct((blocks, 16, LANES), F32),
            jax.ShapeDtypeStruct((quarter, chan_width, out_width), BF16),
        ),
        in_specs=[in_vmem] + [in_hbm] * 8,
        out_specs=[in_vmem] * 4,
        scratch_shapes=[
            *[pltpu.VMEM(small.shape, small.dtype) for small in smalls],
            pltpu.VMEM((feat_rows, order), F32),
            pltpu.VMEM((order + 8, order), F32),
            pltpu.VMEM((order + 8, length), F32),
            pltpu.VMEM((length + block, LANES), BF16),
            pltpu.SemaphoreType.DMA((len(smalls),)),
            pltpu.SemaphoreType.DMA((quarter,)),
        ],
        compiler_params=limit,
    )(my_filter, *map(far, (*smalls, out_weight)))

    *convolved, weights_kept = pl.pallas_call(
        functools.partial(conv_kernel, block, blocks_kept, arrival, pieces > 1),
        out_shape=[
            *[jax.ShapeDtypeStruct((rows, LANES), BF16)] * seq_count,
            jax.ShapeDtypeStruct((quarter, chan_width, out_width), BF16),
        ],
        in_specs=[in_smem] + [in_vmem] * 5 + [in_hbm] + [in_vmem] * seq_count,
        out_specs=[in_vmem] * (seq_count + 1),
        scratch_shapes=[
            pltpu.VMEM((length, LANES), BF16),
            pltpu.VMEM((blocks, block, LANES), F32),
            pltpu.VMEM((blocks, block, LANES), F32),
            pltpu.VMEM((2 * block, blocks * LANES), BF16),
            pltpu.VMEM((length, LANES), BF16),
            pltpu.SemaphoreType.DMA((quarter,)),
        ],
        compiler_params=limit,
    )(group_order, real, imag, edge, head, inverse, far(out_weight), *[spread[k] for k in arrival])
    weights_next, query_near, skip = pl.pallas_call(
        functools.partial(copy_kernel, near_odd),
        out_shape=(
            jax.ShapeDtypeStruct((quarter, chan_width, out_width), BF16),
            jax.ShapeDtypeStruct((pieces, rows, unit), BF16),
            jax.ShapeDtypeStruct((pieces, rows, unit), F32),
        ),
        in_specs=[in_vmem] * 2 + [in_hbm] * 2 + [in_vmem] * pieces,
        out_specs=[in_vmem] * 3,
        scratch_shapes=[pltpu.SemaphoreType.DMA((quarter,)), pltpu.SemaphoreType.DMA((pieces,))],
        compiler_params=limit,
    )(convolved[0], skip_gain[None, :], far(out_weight), far(query), *signal)
    if pieces > 1:
        backs = swap(convolved)
    else:
        in_order = lax.all_to_all(jnp.stack([piece[:, :width] for piece in convolved]), "seq", 0, 0, tiled=True)
        backs = [in_order.transpose(1, 0, 2).reshape(rows, chan_width)]

    def exchange(terms, bit):
        return lax.ppermute(terms, "chan", [(d, d ^ bit) for d in range(chan_count)])

    far_away, mixed = pl.pallas_call(
        functools.partial(mix_kernel, arrival if pieces > 1 else [0]),
        out_shape=(
            jax.ShapeDtypeStruct((quarter, rows, out_width), BF16),
            jax.ShapeDtypeStruct((rows, chan_width), BF16),
        ),
        in_specs=[in_vmem] * (3 + pieces),
        out_specs=[in_vmem] * 2,
        compiler_params=limit,
    )(query_near, skip, weights_away, *[backs[k] for k in (arrival if pieces > 1 else [0])])
    far_terms = exchange(far_away, 1)

    def products(first, weights, dtype):
        return pl.pallas_call(
            functools.partial(project_kernel, first),
            out_shape=jax.ShapeDtypeStruct((quarter, rows, out_width), dtype),
            in_specs=[in_vmem] * 2,
            out_specs=in_vmem,
            compiler_params=limit,
        )(mixed, weights)

    far_kept, near_away = products(0, weights_kept, F32), products(0, weights_next, BF16)
    spans = [(0, out_width // 2), (out_width // 2, out_width)]
    send = [(far_kept[:, :, a:b] + far_terms[:, :, a:b].astype(F32)).astype(BF16) for a, b in spans]
    send, near_away, mixed = lax.optimization_barrier((send, near_away, mixed))
    sent = [exchange(piece, 2) for piece in send]
    near_terms = exchange(near_away, 1)
    near_kept = pl.pallas_call(
        functools.partial(last_kernel, blocks_last),
        out_shape=jax.ShapeDtypeStruct((quarter, rows, out_width), F32),
        in_specs=[in_vmem, in_hbm],
        out_specs=in_vmem,
        scratch_shapes=[
            pltpu.VMEM((quarter, chan_width, out_width), BF16),
            pltpu.SemaphoreType.DMA((quarter,)),
        ],
        compiler_params=limit,
    )(mixed, far(out_weight))
    terms = [near_kept, near_terms]
    bit = 4
    while bit < chan_count:
        total = sum(term.astype(F32) for term in (*terms, jnp.concatenate(sent, 2)))
        terms, sent, spans = [total[0::2]], [exchange(total[1::2].astype(BF16), bit)], [(0, out_width)]
        bit *= 2
    result = []
    for span, piece in zip(spans, sent):
        operands = [*[term[0] for term in terms], piece[0]]
        result = [
            pl.pallas_call(
                functools.partial(finish_kernel, span, len(terms)),
                out_shape=jax.ShapeDtypeStruct((out_width, rows), F32),
                in_specs=[in_vmem] * len(operands) + [in_hbm] * len(result),
                out_specs=in_hbm,
                scratch_shapes=[
                    pltpu.VMEM((span[1] - span[0], rows), F32),
                    pltpu.SemaphoreType.DMA((max(1, (span[1] - span[0]) // LANES),)),
                ],
                input_output_aliases={len(operands): 0} if result else {},
                compiler_params=limit,
            )(*operands, *result)
        ]
    return result[0]


def solution(mesh):
    return jax.shard_map(
        local,
        mesh=mesh,
        in_specs=(
            P("seq", "chan"), P("seq", "chan"), P("seq", "chan"), P(), P(), P(), P(), P(), P(None, "chan"), P("chan"),
            P("chan"), P("chan", None),
        ),
        out_specs=P("chan", "seq"),
        check_vma=False,
    )
```

```python
import functools
import math

import jax
import jax.numpy as jnp
import numpy as np
from jax import lax
from jax.experimental import pallas as pl
from jax.experimental.pallas import tpu as pltpu
from jax.sharding import PartitionSpec as P

GROUP = 128
LANES = 128
SINE_FREQ = 2.0
F32 = jnp.float32
BF16 = jnp.bfloat16


def packed_tables(block):
    period = 2 * block
    row = np.arange(block)
    freq = np.arange(block)

    def forward(shift):
        angle = 2.0 * np.pi * (freq[:, None] * (row[None, :] + shift) % period) / period
        real, imag = np.cos(angle), -np.sin(angle)
        imag[0] = np.where((row + shift) % 2 == 0, 1.0, -1.0)
        return np.concatenate([real, imag], 0)

    head, tail = forward(0), forward(block)
    tail[:, 0] = 0.0
    weight = np.where(freq == 0, 1.0, 2.0) / period
    angle = 2.0 * np.pi * (row[:, None] * freq[None, :] % period) / period
    real, imag = np.cos(angle) * weight, -np.sin(angle) * weight
    imag[:, 0] = np.where(row % 2 == 0, 1.0, -1.0) / period
    inverse = np.concatenate([real, imag], 1)
    to_bf16 = lambda table: jnp.asarray(table.astype(np.float32)).astype(BF16)
    return to_bf16(head), to_bf16(np.concatenate([head, tail], 1)), to_bf16(inverse)


def feature_table(length, bands, rows):
    lag = np.arange(length)
    angle = 2.0 * np.pi * (np.arange(1, bands + 1)[:, None] * lag[None, :] % length) / length
    table = np.zeros((rows, length), np.float32)
    table[0] = lag / length
    table[1 : bands + 1] = np.cos(angle)
    table[bands + 1 : 2 * bands + 1] = np.sin(angle)
    table[2 * bands + 1] = 1.0
    return jnp.asarray(table)


def sine(x):
    n = jnp.round(x * (1.0 / math.pi))
    r = x - n * 3.140625
    r = r - n * 9.67502593994140625e-4
    r = r - n * 1.509957990978376432e-7
    square = r * r
    series = jnp.full_like(r, -2.5052108e-8)
    for term in (2.7557319e-6, -1.9841270e-4, 8.3333333e-3, -1.6666667e-1):
        series = series * square + term
    odd = n * 0.5 - jnp.floor(n * 0.5)
    return (r + r * square * series) * (1.0 - 4.0 * odd)


def contract_first(lhs, rhs):
    return lax.dot_general(
        lhs, rhs, (((0,), (0,)), ((), ())), precision=lax.Precision.HIGHEST, preferred_element_type=F32
    )


def first_piece(pieces):
    return lax.axis_index("seq") if pieces > 1 else 0


def weight_copies(blocks, weight_hbm, weight_out, sem):
    width = weight_out.shape[2]
    copies = []
    for i, j in enumerate(blocks):
        cols = pl.ds(pl.multiple_of((lax.axis_index("chan") ^ j) * width, LANES), width)
        copies.append(pltpu.make_async_copy(weight_hbm.at[:, cols], weight_out.at[i], sem.at[i]))
    return copies


def one_minus_exp(y):
    series = jnp.full_like(y, -1.0 / 40320)
    for term in (5040, -720, 120, -24, 6, -2, 1):
        series = series * y + 1.0 / term
    return jnp.where(y < 0.5, y * series, 1.0 - jnp.exp(-y))


def filter_kernel(block, blocks_first, relative, out_w_ref, *refs):
    smalls, weight_hbm, refs = refs[:7], refs[7], refs[8:]
    (real_ref, imag_ref, edge_ref, weight_out), refs = refs[:4], refs[4:]
    near, (w1, w2, hid, filt, near_sem, weight_sem) = refs[:7], refs[7:]
    feat_ref, emb_w_ref, emb_b_ref, mid_w_ref, mid_b_ref, decay_all, table_ref = near
    fetches = [pltpu.make_async_copy(s, t, near_sem.at[i]) for i, (s, t) in enumerate(zip(smalls, near))]
    for fetch in fetches:
        fetch.start()
    for fetch in fetches[:-1]:
        fetch.wait()
    copies = weight_copies(blocks_first, weight_hbm, weight_out, weight_sem)
    for copy in copies:
        copy.start()
    emb, order = emb_w_ref.shape
    length = feat_ref.shape[1]
    blocks = length // block
    w1[...] = jnp.zeros_like(w1)
    w1[0:emb, :] = emb_w_ref[...]
    w1[emb : emb + 1, :] = emb_b_ref[...]
    w2[...] = jnp.zeros_like(w2)
    w2[0:order, :] = mid_w_ref[...]
    w2[order : order + 1, :] = mid_b_ref[...]
    hid[order:, :] = jnp.ones_like(hid[order:, :])
    hid[0:order, :] = sine(SINE_FREQ * contract_first(w1[...], feat_ref[...]))
    hidden = sine(SINE_FREQ * contract_first(w2[...], hid[...]))
    raw = contract_first(out_w_ref[...], hidden).T
    decay = decay_all[pl.ds(lax.axis_index("seq") if relative else 0, 1), :]
    within = jnp.exp(-decay * lax.broadcasted_iota(jnp.int32, (block, LANES), 0).astype(F32))
    within = within * jnp.sqrt(one_minus_exp(2.0 * decay))
    filt[0:block, :] = jnp.zeros((block, LANES), BF16)
    for m in range(blocks):
        start = jnp.exp(-decay * float(m * block))
        filt[(m + 1) * block : (m + 2) * block, :] = (raw[m * block : (m + 1) * block] * (within * start)).astype(BF16)
    first_row = lax.broadcasted_iota(jnp.int32, (16, LANES), 0) == 0
    fetches[-1].wait()
    group = 2
    for m0 in range(0, blocks, group):
        stacked = jnp.concatenate(
            [
                jnp.concatenate(
                    [filt[(m + 1) * block : (m + 2) * block, :], filt[m * block : (m + 1) * block, :]], 0
                )
                for m in range(m0, m0 + group)
            ],
            1,
        )
        spectrum = jnp.dot(table_ref[...], stacked, preferred_element_type=F32)
        for i in range(group):
            m = m0 + i
            real = spectrum[:block, i * LANES : (i + 1) * LANES]
            imag = spectrum[block:, i * LANES : (i + 1) * LANES]
            real_ref[m] = real
            imag_ref[m] = imag
            edge_ref[m] = jnp.where(first_row, imag[:16], real[:16])
            imag_ref[m, 0:16, :] = jnp.where(first_row, 0.0, imag[:16])
    for copy in copies:
        copy.wait()


def conv_kernel(
    block, blocks_next, arrival, relative, order_ref, real_ref, imag_ref, edge_ref, table_ref, inverse_ref, weight_hbm, *refs
):
    *refs, weight_out, sig, sre, sim, spec, conv, weight_sem = refs
    count = len(refs) // 2
    x_refs, out_refs = refs[:count], refs[count:]
    first = first_piece(count if relative else 1)
    copies = weight_copies(blocks_next, weight_hbm, weight_out, weight_sem)
    for copy in copies:
        copy.start()
    groups = x_refs[0].shape[0] // GROUP
    length = sig.shape[0]
    blocks = length // block

    def place(k, i):
        return pl.multiple_of(order_ref[(first ^ k) * groups + i] * GROUP, GROUP)

    for k, x_ref in zip(arrival, x_refs):
        for i in range(groups):
            sig[pl.ds(place(k, i), GROUP), :] = x_ref[i * GROUP : (i + 1) * GROUP, :]
    group = 2
    for b0 in range(0, blocks, group):
        stacked = jnp.concatenate([sig[b * block : (b + 1) * block, :] for b in range(b0, b0 + group)], 1)
        spectrum = jnp.dot(table_ref[...], stacked, preferred_element_type=F32)
        for i in range(group):
            sre[b0 + i] = spectrum[:block, i * LANES : (i + 1) * LANES]
            sim[b0 + i] = spectrum[block:, i * LANES : (i + 1) * LANES]

    def tile(start, first):
        rows = pl.ds(start, 16)
        mirror = pl.ds(block + start, 16)
        s_real = [sre[q, rows, :] for q in range(blocks)]
        s_imag = [sim[q, rows, :] for q in range(blocks)]
        for g in range(blocks):
            acc_real = acc_imag = None
            for q in range(g + 1):
                fr, fi = real_ref[g - q, rows, :], imag_ref[g - q, rows, :]
                fe = edge_ref[g - q] if first else fr
                re = fr * s_real[q] - fi * s_imag[q]
                im = fe * s_imag[q] + fi * s_real[q]
                acc_real = re if q == 0 else acc_real + re
                acc_imag = im if q == 0 else acc_imag + im
            spec[rows, g * LANES : (g + 1) * LANES] = acc_real.astype(BF16)
            spec[mirror, g * LANES : (g + 1) * LANES] = acc_imag.astype(BF16)

    tile(0, True)

    @pl.loop(1, block // 16)
    def _(t):
        tile(pl.multiple_of(t * 16, 16), False)

    result = jnp.dot(inverse_ref[...], spec[...], preferred_element_type=F32)
    for g in range(blocks):
        conv[g * block : (g + 1) * block, :] = result[:, g * LANES : (g + 1) * LANES].astype(BF16)
    for k, out_ref in enumerate(out_refs):
        for i in range(groups):
            out_ref[i * GROUP : (i + 1) * GROUP, :] = conv[pl.ds(place(k, i), GROUP), :]
    for copy in copies:
        copy.wait()


def copy_kernel(blocks_next, after_ref, gain_ref, weight_hbm, query_hbm, *refs):
    *sig_refs, weight_out, query_out, skip_out, weight_sem, query_sem = refs
    pieces = len(sig_refs)
    unit = sig_refs[0].shape[1]
    columns = [pl.ds(pl.multiple_of((first_piece(pieces) ^ k) * unit, LANES), unit) for k in range(pieces)]
    copies = [
        pltpu.make_async_copy(query_hbm.at[:, cols], query_out.at[k], query_sem.at[k]) for k, cols in enumerate(columns)
    ]
    copies += weight_copies(blocks_next, weight_hbm, weight_out, weight_sem)
    for copy in copies:
        copy.start()
    for k, (cols, sig_ref) in enumerate(zip(columns, sig_refs)):
        skip_out[k] = gain_ref[:, cols] * sig_ref[...].astype(F32)
    for copy in copies:
        copy.wait()


def mix_kernel(arrival, query_ref, skip_ref, weight_ref, *refs):
    *back_refs, out_ref, mixed_ref = refs
    pieces, _, unit = query_ref.shape
    for k, back_ref in zip(arrival, back_refs):
        cols = pl.ds(pl.multiple_of((first_piece(pieces) ^ k) * unit, LANES), unit)
        mixed_ref[:, cols] = (query_ref[k].astype(F32) * (back_ref[...].astype(F32) + skip_ref[k])).astype(BF16)
    project_kernel(0, mixed_ref, weight_ref, out_ref)


def project_kernel(first, mixed_ref, weight_ref, out_ref):
    mixed = mixed_ref[...]
    for i in range(out_ref.shape[0]):
        out_ref[i] = jnp.dot(mixed, weight_ref[first + i], preferred_element_type=F32).astype(out_ref.dtype)


def last_kernel(blocks_last, mixed_ref, weight_hbm, out_ref, weight_near, sem):
    copies = weight_copies(blocks_last, weight_hbm, weight_near, sem)
    for copy in copies:
        copy.start()
    for copy in copies:
        copy.wait()
    project_kernel(0, mixed_ref, weight_near, out_ref)


def finish_kernel(span, count, *refs):
    (*held, arrived), (out_hbm, turned, sem) = refs[: count + 1], refs[-3:]
    first, last = span
    step = min(LANES, last - first)
    copies = []
    for i, start in enumerate(range(0, last - first, step)):
        cols = slice(start, start + step)
        total = arrived[:, cols].astype(F32)
        for ref in held:
            total = total + ref[:, first + start : first + start + step].astype(F32)
        turned[cols] = total.T
        copies.append(pltpu.make_async_copy(turned.at[cols], out_hbm.at[first + start : first + start + step], sem.at[i]))
        copies[-1].start()
    for copy in copies:
        copy.wait()


def gated_kernel(key_hbm, value_hbm, *refs):
    *out_refs, key_ref, value_ref, sem = refs
    pieces = len(out_refs)
    unit = out_refs[0].shape[1]
    copies = []
    for k in range(pieces):
        cols = pl.ds(pl.multiple_of((first_piece(pieces) ^ k) * unit, LANES), unit)
        copies.append(pltpu.make_async_copy(key_hbm.at[:, cols], key_ref.at[k], sem.at[0, k]))
        copies.append(pltpu.make_async_copy(value_hbm.at[:, cols], value_ref.at[k], sem.at[1, k]))
    for copy in copies:
        copy.start()
    for k, out_ref in enumerate(out_refs):
        copies[2 * k].wait()
        copies[2 * k + 1].wait()
        out_ref[...] = (key_ref[k].astype(F32) * value_ref[k].astype(F32)).astype(BF16)


def local(
    query, key_gate, value, group_order, emb_weight, emb_bias, mid_weight, mid_bias, out_filter, decay_rate, skip_gain,
    out_weight,
):
    rows, chan_width = query.shape
    seq_count, chan_count = lax.axis_size("seq"), lax.axis_size("chan")
    seq_index, chan_index = lax.axis_index("seq"), lax.axis_index("chan")
    length = rows * seq_count
    slots = length // GROUP
    width = chan_width // seq_count
    block = max(2 * GROUP, length // 16)
    blocks = length // block
    emb, order = emb_weight.shape
    head, head_tail, inverse = packed_tables(block)
    feat_rows = -(-(emb + 1) // 8) * 8
    features = feature_table(length, (emb - 1) // 2, feat_rows)

    limit = pltpu.CompilerParams(vmem_limit_bytes=20 << 20)
    in_vmem = pl.BlockSpec(memory_space=pltpu.VMEM)
    in_smem = pl.BlockSpec(memory_space=pltpu.SMEM)
    in_hbm = pl.BlockSpec(memory_space=pltpu.HBM)
    far = lambda operand: pltpu.with_memory_space_constraint(operand, pltpu.HBM)
    unit = width if width % LANES == 0 else chan_width
    pieces = chan_width // unit

    middle = seq_count // 2
    arrival = [k for near in range(middle) for k in (near, near + middle)]

    def swap(arrays):
        return [arrays[0]] + [
            lax.ppermute(arrays[k], "seq", [(d, d ^ k) for d in range(seq_count)]) for k in range(1, seq_count)
        ]

    signal = pl.pallas_call(
        gated_kernel,
        out_shape=[jax.ShapeDtypeStruct((rows, unit), BF16)] * pieces,
        in_specs=[in_hbm] * 2,
        out_specs=[in_vmem] * pieces,
        scratch_shapes=[
            pltpu.VMEM((pieces, rows, unit), BF16),
            pltpu.VMEM((pieces, rows, unit), BF16),
            pltpu.SemaphoreType.DMA((2, pieces)),
        ],
        compiler_params=limit,
    )(far(key_gate), far(value))
    if pieces > 1:
        spread = swap(signal)
    else:
        in_order = signal[0].reshape(rows, seq_count, width).transpose(1, 0, 2)
        in_order = lax.all_to_all(in_order, "seq", 0, 0, tiled=True)
        spread = list(jnp.pad(in_order, [(0, 0), (0, 0), (0, LANES - width)]))

    my_filter = lax.dynamic_slice_in_dim(out_filter, seq_index * width, width, 1)
    decay = decay_rate.reshape(seq_count, width)
    if pieces == 1:
        pad = [(0, 0), (0, LANES - width)]
        my_filter = jnp.pad(my_filter, pad)
        decay = jnp.pad(lax.dynamic_slice_in_dim(decay, seq_index, 1), pad)
    out_width = out_weight.shape[1] // chan_count
    quarter = chan_count // 4
    odd = range(1, chan_count, 2)
    far_odd, near_odd = [j for j in odd if j & 2], [j for j in odd if not j & 2]
    blocks_kept, blocks_last = [j ^ 1 for j in far_odd], [j ^ 1 for j in near_odd]
    smalls = (
        features, emb_weight, emb_bias[None, :], mid_weight, mid_bias[None, :], decay, head_tail,
    )
    real, imag, edge, weights_away = pl.pallas_call(
        functools.partial(filter_kernel, block, far_odd, pieces > 1),
        out_shape=(
            jax.ShapeDtypeStruct((blocks, block, LANES), F32),
            jax.ShapeDtypeStruct((blocks, block, LANES), F32),
            jax.ShapeDtypeStruct((blocks, 16, LANES), F32),
            jax.ShapeDtypeStruct((quarter, chan_width, out_width), BF16),
        ),
        in_specs=[in_vmem] + [in_hbm] * 8,
        out_specs=[in_vmem] * 4,
        scratch_shapes=[
            *[pltpu.VMEM(small.shape, small.dtype) for small in smalls],
            pltpu.VMEM((feat_rows, order), F32),
            pltpu.VMEM((order + 8, order), F32),
            pltpu.VMEM((order + 8, length), F32),
            pltpu.VMEM((length + block, LANES), BF16),
            pltpu.SemaphoreType.DMA((len(smalls),)),
            pltpu.SemaphoreType.DMA((quarter,)),
        ],
        compiler_params=limit,
    )(my_filter, *map(far, (*smalls, out_weight)))

    *convolved, weights_kept = pl.pallas_call(
        functools.partial(conv_kernel, block, blocks_kept, arrival, pieces > 1),
        out_shape=[
            *[jax.ShapeDtypeStruct((rows, LANES), BF16)] * seq_count,
            jax.ShapeDtypeStruct((quarter, chan_width, out_width), BF16),
        ],
        in_specs=[in_smem] + [in_vmem] * 5 + [in_hbm] + [in_vmem] * seq_count,
        out_specs=[in_vmem] * (seq_count + 1),
        scratch_shapes=[
            pltpu.VMEM((length, LANES), BF16),
            pltpu.VMEM((blocks, block, LANES), F32),
            pltpu.VMEM((blocks, block, LANES), F32),
            pltpu.VMEM((2 * block, blocks * LANES), BF16),
            pltpu.VMEM((length, LANES), BF16),
            pltpu.SemaphoreType.DMA((quarter,)),
        ],
        compiler_params=limit,
    )(group_order, real, imag, edge, head, inverse, far(out_weight), *[spread[k] for k in arrival])
    weights_next, query_near, skip = pl.pallas_call(
        functools.partial(copy_kernel, near_odd),
        out_shape=(
            jax.ShapeDtypeStruct((quarter, chan_width, out_width), BF16),
            jax.ShapeDtypeStruct((pieces, rows, unit), BF16),
            jax.ShapeDtypeStruct((pieces, rows, unit), F32),
        ),
        in_specs=[in_vmem] * 2 + [in_hbm] * 2 + [in_vmem] * pieces,
        out_specs=[in_vmem] * 3,
        scratch_shapes=[pltpu.SemaphoreType.DMA((quarter,)), pltpu.SemaphoreType.DMA((pieces,))],
        compiler_params=limit,
    )(convolved[0], skip_gain[None, :], far(out_weight), far(query), *signal)
    if pieces > 1:
        backs = swap(convolved)
    else:
        in_order = lax.all_to_all(jnp.stack([piece[:, :width] for piece in convolved]), "seq", 0, 0, tiled=True)
        backs = [in_order.transpose(1, 0, 2).reshape(rows, chan_width)]

    def exchange(terms, bit):
        return lax.ppermute(terms, "chan", [(d, d ^ bit) for d in range(chan_count)])

    far_away, mixed = pl.pallas_call(
        functools.partial(mix_kernel, arrival if pieces > 1 else [0]),
        out_shape=(
            jax.ShapeDtypeStruct((quarter, rows, out_width), BF16),
            jax.ShapeDtypeStruct((rows, chan_width), BF16),
        ),
        in_specs=[in_vmem] * (3 + pieces),
        out_specs=[in_vmem] * 2,
        compiler_params=limit,
    )(query_near, skip, weights_away, *[backs[k] for k in (arrival if pieces > 1 else [0])])
    far_terms = exchange(far_away, 1)

    def products(first, weights, dtype):
        return pl.pallas_call(
            functools.partial(project_kernel, first),
            out_shape=jax.ShapeDtypeStruct((quarter, rows, out_width), dtype),
            in_specs=[in_vmem] * 2,
            out_specs=in_vmem,
            compiler_params=limit,
        )(mixed, weights)

    far_kept, near_away = products(0, weights_kept, F32), products(0, weights_next, BF16)
    spans = [(0, out_width // 2), (out_width // 2, out_width)]
    send = [(far_kept[:, :, a:b] + far_terms[:, :, a:b].astype(F32)).astype(BF16) for a, b in spans]
    send, near_away, mixed = lax.optimization_barrier((send, near_away, mixed))
    sent = [exchange(piece, 2) for piece in send]
    near_terms = exchange(near_away, 1)
    near_kept = pl.pallas_call(
        functools.partial(last_kernel, blocks_last),
        out_shape=jax.ShapeDtypeStruct((quarter, rows, out_width), F32),
        in_specs=[in_vmem, in_hbm],
        out_specs=in_vmem,
        scratch_shapes=[
            pltpu.VMEM((quarter, chan_width, out_width), BF16),
            pltpu.SemaphoreType.DMA((quarter,)),
        ],
        compiler_params=limit,
    )(mixed, far(out_weight))
    terms = [near_kept, near_terms]
    bit = 4
    while bit < chan_count:
        total = sum(term.astype(F32) for term in (*terms, jnp.concatenate(sent, 2)))
        terms, sent, spans = [total[0::2]], [exchange(total[1::2].astype(BF16), bit)], [(0, out_width)]
        bit *= 2
    result = []
    for span, piece in zip(spans, sent):
        operands = [*[term[0] for term in terms], piece[0]]
        result = [
            pl.pallas_call(
                functools.partial(finish_kernel, span, len(terms)),
                out_shape=jax.ShapeDtypeStruct((out_width, rows), F32),
                in_specs=[in_vmem] * len(operands) + [in_hbm] * len(result),
                out_specs=in_hbm,
                scratch_shapes=[
                    pltpu.VMEM((span[1] - span[0], rows), F32),
                    pltpu.SemaphoreType.DMA((max(1, (span[1] - span[0]) // LANES),)),
                ],
                input_output_aliases={len(operands): 0} if result else {},
                compiler_params=limit,
            )(*operands, *result)
        ]
    return result[0]


def solution(mesh):
    return jax.shard_map(
        local,
        mesh=mesh,
        in_specs=(
            P("seq", "chan"), P("seq", "chan"), P("seq", "chan"), P(), P(), P(), P(), P(), P(None, "chan"), P("chan"),
            P("chan"), P("chan", None),
        ),
        out_specs=P("chan", "seq"),
        check_vma=False,
    )
```

```python
import functools
import math

import jax
import jax.numpy as jnp
import numpy as np
from jax import lax
from jax.experimental import pallas as pl
from jax.experimental.pallas import tpu as pltpu
from jax.sharding import PartitionSpec as P

GROUP = 128
LANES = 128
SINE_FREQ = 2.0
F32 = jnp.float32
BF16 = jnp.bfloat16


def packed_tables(block):
    period = 2 * block
    row = np.arange(block)
    freq = np.arange(block)

    def forward(shift):
        angle = 2.0 * np.pi * (freq[:, None] * (row[None, :] + shift) % period) / period
        real, imag = np.cos(angle), -np.sin(angle)
        imag[0] = np.where((row + shift) % 2 == 0, 1.0, -1.0)
        return np.concatenate([real, imag], 0)

    head, tail = forward(0), forward(block)
    tail[:, 0] = 0.0
    weight = np.where(freq == 0, 1.0, 2.0) / period
    angle = 2.0 * np.pi * (row[:, None] * freq[None, :] % period) / period
    real, imag = np.cos(angle) * weight, -np.sin(angle) * weight
    imag[:, 0] = np.where(row % 2 == 0, 1.0, -1.0) / period
    inverse = np.concatenate([real, imag], 1)
    to_bf16 = lambda table: jnp.asarray(table.astype(np.float32)).astype(BF16)
    return to_bf16(head), to_bf16(np.concatenate([head, tail], 1)), to_bf16(inverse)


def feature_table(length, bands, rows):
    lag = np.arange(length)
    angle = 2.0 * np.pi * (np.arange(1, bands + 1)[:, None] * lag[None, :] % length) / length
    table = np.zeros((rows, length), np.float32)
    table[0] = lag / length
    table[1 : bands + 1] = np.cos(angle)
    table[bands + 1 : 2 * bands + 1] = np.sin(angle)
    table[2 * bands + 1] = 1.0
    return jnp.asarray(table)


def sine(x):
    n = jnp.round(x * (1.0 / math.pi))
    r = x - n * 3.140625
    r = r - n * 9.67502593994140625e-4
    r = r - n * 1.509957990978376432e-7
    square = r * r
    series = jnp.full_like(r, -2.5052108e-8)
    for term in (2.7557319e-6, -1.9841270e-4, 8.3333333e-3, -1.6666667e-1):
        series = series * square + term
    odd = n * 0.5 - jnp.floor(n * 0.5)
    return (r + r * square * series) * (1.0 - 4.0 * odd)


def contract_first(lhs, rhs):
    return lax.dot_general(
        lhs, rhs, (((0,), (0,)), ((), ())), precision=lax.Precision.HIGHEST, preferred_element_type=F32
    )


def first_piece(pieces):
    return lax.axis_index("seq") if pieces > 1 else 0


def weight_copies(blocks, weight_hbm, weight_out, sem):
    width = weight_out.shape[2]
    copies = []
    for i, j in enumerate(blocks):
        cols = pl.ds(pl.multiple_of((lax.axis_index("chan") ^ j) * width, LANES), width)
        copies.append(pltpu.make_async_copy(weight_hbm.at[:, cols], weight_out.at[i], sem.at[i]))
    return copies


def one_minus_exp(y):
    series = jnp.full_like(y, -1.0 / 40320)
    for term in (5040, -720, 120, -24, 6, -2, 1):
        series = series * y + 1.0 / term
    return jnp.where(y < 0.5, y * series, 1.0 - jnp.exp(-y))


def filter_kernel(block, blocks_first, relative, out_w_ref, *refs):
    smalls, weight_hbm, refs = refs[:7], refs[7], refs[8:]
    (real_ref, imag_ref, edge_ref, weight_out), refs = refs[:4], refs[4:]
    near, (w1, w2, hid, filt, near_sem, weight_sem) = refs[:7], refs[7:]
    feat_ref, emb_w_ref, emb_b_ref, mid_w_ref, mid_b_ref, decay_all, table_ref = near
    fetches = [pltpu.make_async_copy(s, t, near_sem.at[i]) for i, (s, t) in enumerate(zip(smalls, near))]
    for fetch in fetches:
        fetch.start()
    for fetch in fetches[:-1]:
        fetch.wait()
    copies = weight_copies(blocks_first, weight_hbm, weight_out, weight_sem)
    for copy in copies:
        copy.start()
    emb, order = emb_w_ref.shape
    length = feat_ref.shape[1]
    blocks = length // block
    w1[...] = jnp.zeros_like(w1)
    w1[0:emb, :] = emb_w_ref[...]
    w1[emb : emb + 1, :] = emb_b_ref[...]
    w2[...] = jnp.zeros_like(w2)
    w2[0:order, :] = mid_w_ref[...]
    w2[order : order + 1, :] = mid_b_ref[...]
    hid[order:, :] = jnp.ones_like(hid[order:, :])
    hid[0:order, :] = sine(SINE_FREQ * contract_first(w1[...], feat_ref[...]))
    hidden = sine(SINE_FREQ * contract_first(w2[...], hid[...]))
    raw = contract_first(out_w_ref[...], hidden).T
    decay = decay_all[pl.ds(lax.axis_index("seq") if relative else 0, 1), :]
    within = jnp.exp(-decay * lax.broadcasted_iota(jnp.int32, (block, LANES), 0).astype(F32))
    within = within * jnp.sqrt(one_minus_exp(2.0 * decay))
    filt[0:block, :] = jnp.zeros((block, LANES), BF16)
    for m in range(blocks):
        start = jnp.exp(-decay * float(m * block))
        filt[(m + 1) * block : (m + 2) * block, :] = (raw[m * block : (m + 1) * block] * (within * start)).astype(BF16)
    first_row = lax.broadcasted_iota(jnp.int32, (16, LANES), 0) == 0
    fetches[-1].wait()
    group = 2
    for m0 in range(0, blocks, group):
        stacked = jnp.concatenate(
            [
                jnp.concatenate(
                    [filt[(m + 1) * block : (m + 2) * block, :], filt[m * block : (m + 1) * block, :]], 0
                )
                for m in range(m0, m0 + group)
            ],
            1,
        )
        spectrum = jnp.dot(table_ref[...], stacked, preferred_element_type=F32)
        for i in range(group):
            m = m0 + i
            real = spectrum[:block, i * LANES : (i + 1) * LANES]
            imag = spectrum[block:, i * LANES : (i + 1) * LANES]
            real_ref[m] = real
            imag_ref[m] = imag
            edge_ref[m] = jnp.where(first_row, imag[:16], real[:16])
            imag_ref[m, 0:16, :] = jnp.where(first_row, 0.0, imag[:16])
    for copy in copies:
        copy.wait()


def conv_kernel(
    block, blocks_next, arrival, relative, order_ref, real_ref, imag_ref, edge_ref, table_ref, inverse_ref, weight_hbm, *refs
):
    *refs, weight_out, sig, sre, sim, spec, conv, weight_sem = refs
    count = len(refs) // 2
    x_refs, out_refs = refs[:count], refs[count:]
    first = first_piece(count if relative else 1)
    copies = weight_copies(blocks_next, weight_hbm, weight_out, weight_sem)
    for copy in copies:
        copy.start()
    groups = x_refs[0].shape[0] // GROUP
    length = sig.shape[0]
    blocks = length // block

    def place(k, i):
        return pl.multiple_of(order_ref[(first ^ k) * groups + i] * GROUP, GROUP)

    for k, x_ref in zip(arrival, x_refs):
        for i in range(groups):
            sig[pl.ds(place(k, i), GROUP), :] = x_ref[i * GROUP : (i + 1) * GROUP, :]
    group = 2
    for b0 in range(0, blocks, group):
        stacked = jnp.concatenate([sig[b * block : (b + 1) * block, :] for b in range(b0, b0 + group)], 1)
        spectrum = jnp.dot(table_ref[...], stacked, preferred_element_type=F32)
        for i in range(group):
            sre[b0 + i] = spectrum[:block, i * LANES : (i + 1) * LANES]
            sim[b0 + i] = spectrum[block:, i * LANES : (i + 1) * LANES]

    def tile(start, first):
        rows = pl.ds(start, 16)
        mirror = pl.ds(block + start, 16)
        s_real = [sre[q, rows, :] for q in range(blocks)]
        s_imag = [sim[q, rows, :] for q in range(blocks)]
        for g in range(blocks):
            acc_real = acc_imag = None
            for q in range(g + 1):
                fr, fi = real_ref[g - q, rows, :], imag_ref[g - q, rows, :]
                fe = edge_ref[g - q] if first else fr
                re = fr * s_real[q] - fi * s_imag[q]
                im = fe * s_imag[q] + fi * s_real[q]
                acc_real = re if q == 0 else acc_real + re
                acc_imag = im if q == 0 else acc_imag + im
            spec[rows, g * LANES : (g + 1) * LANES] = acc_real.astype(BF16)
            spec[mirror, g * LANES : (g + 1) * LANES] = acc_imag.astype(BF16)

    tile(0, True)

    @pl.loop(1, block // 16)
    def _(t):
        tile(pl.multiple_of(t * 16, 16), False)

    result = jnp.dot(inverse_ref[...], spec[...], preferred_element_type=F32)
    for g in range(blocks):
        conv[g * block : (g + 1) * block, :] = result[:, g * LANES : (g + 1) * LANES].astype(BF16)
    for k, out_ref in enumerate(out_refs):
        for i in range(groups):
            out_ref[i * GROUP : (i + 1) * GROUP, :] = conv[pl.ds(place(k, i), GROUP), :]
    for copy in copies:
        copy.wait()


def copy_kernel(blocks_next, after_ref, gain_ref, weight_hbm, query_hbm, *refs):
    *sig_refs, weight_out, query_out, skip_out, weight_sem, query_sem = refs
    pieces = len(sig_refs)
    unit = sig_refs[0].shape[1]
    columns = [pl.ds(pl.multiple_of((first_piece(pieces) ^ k) * unit, LANES), unit) for k in range(pieces)]
    copies = [
        pltpu.make_async_copy(query_hbm.at[:, cols], query_out.at[k], query_sem.at[k]) for k, cols in enumerate(columns)
    ]
    copies += weight_copies(blocks_next, weight_hbm, weight_out, weight_sem)
    for copy in copies:
        copy.start()
    for k, (cols, sig_ref) in enumerate(zip(columns, sig_refs)):
        skip_out[k] = gain_ref[:, cols] * sig_ref[...].astype(F32)
    for copy in copies:
        copy.wait()


def mix_kernel(arrival, query_ref, skip_ref, weight_ref, *refs):
    *back_refs, out_ref, mixed_ref = refs
    pieces, _, unit = query_ref.shape
    for k, back_ref in zip(arrival, back_refs):
        cols = pl.ds(pl.multiple_of((first_piece(pieces) ^ k) * unit, LANES), unit)
        mixed_ref[:, cols] = (query_ref[k].astype(F32) * (back_ref[...].astype(F32) + skip_ref[k])).astype(BF16)
    project_kernel(0, mixed_ref, weight_ref, out_ref)


def project_kernel(first, mixed_ref, weight_ref, out_ref):
    mixed = mixed_ref[...]
    for i in range(out_ref.shape[0]):
        out_ref[i] = jnp.dot(mixed, weight_ref[first + i], preferred_element_type=F32).astype(out_ref.dtype)


def last_kernel(blocks_last, mixed_ref, weight_hbm, out_ref, weight_near, sem):
    copies = weight_copies(blocks_last, weight_hbm, weight_near, sem)
    for copy in copies:
        copy.start()
    for copy in copies:
        copy.wait()
    project_kernel(0, mixed_ref, weight_near, out_ref)


def finish_kernel(span, count, *refs):
    (*held, arrived), (out_hbm, turned, sem) = refs[: count + 1], refs[-3:]
    first, last = span
    step = min(LANES, last - first)
    copies = []
    for i, start in enumerate(range(0, last - first, step)):
        cols = slice(start, start + step)
        total = arrived[:, cols].astype(F32)
        for ref in held:
            total = total + ref[:, first + start : first + start + step].astype(F32)
        turned[cols] = total.T
        copies.append(pltpu.make_async_copy(turned.at[cols], out_hbm.at[first + start : first + start + step], sem.at[i]))
        copies[-1].start()
    for copy in copies:
        copy.wait()


def gated_kernel(key_hbm, value_hbm, *refs):
    *out_refs, key_ref, value_ref, sem = refs
    pieces = len(out_refs)
    unit = out_refs[0].shape[1]
    copies = []
    for k in range(pieces):
        cols = pl.ds(pl.multiple_of((first_piece(pieces) ^ k) * unit, LANES), unit)
        copies.append(pltpu.make_async_copy(key_hbm.at[:, cols], key_ref.at[k], sem.at[0, k]))
        copies.append(pltpu.make_async_copy(value_hbm.at[:, cols], value_ref.at[k], sem.at[1, k]))
    for copy in copies:
        copy.start()
    for k, out_ref in enumerate(out_refs):
        copies[2 * k].wait()
        copies[2 * k + 1].wait()
        out_ref[...] = (key_ref[k].astype(F32) * value_ref[k].astype(F32)).astype(BF16)


def local(
    query, key_gate, value, group_order, emb_weight, emb_bias, mid_weight, mid_bias, out_filter, decay_rate, skip_gain,
    out_weight,
):
    rows, chan_width = query.shape
    seq_count, chan_count = lax.axis_size("seq"), lax.axis_size("chan")
    seq_index, chan_index = lax.axis_index("seq"), lax.axis_index("chan")
    length = rows * seq_count
    slots = length // GROUP
    width = chan_width // seq_count
    block = max(2 * GROUP, length // 16)
    blocks = length // block
    emb, order = emb_weight.shape
    head, head_tail, inverse = packed_tables(block)
    feat_rows = -(-(emb + 1) // 8) * 8
    features = feature_table(length, (emb - 1) // 2, feat_rows)

    limit = pltpu.CompilerParams(vmem_limit_bytes=20 << 20)
    in_vmem = pl.BlockSpec(memory_space=pltpu.VMEM)
    in_smem = pl.BlockSpec(memory_space=pltpu.SMEM)
    in_hbm = pl.BlockSpec(memory_space=pltpu.HBM)
    far = lambda operand: pltpu.with_memory_space_constraint(operand, pltpu.HBM)
    unit = width if width % LANES == 0 else chan_width
    pieces = chan_width // unit

    middle = seq_count // 2
    arrival = [k for near in range(middle) for k in (near, seq_count - 1 - near)]

    def swap(arrays):
        return [arrays[0]] + [
            lax.ppermute(arrays[k], "seq", [(d, d ^ k) for d in range(seq_count)]) for k in range(1, seq_count)
        ]

    signal = pl.pallas_call(
        gated_kernel,
        out_shape=[jax.ShapeDtypeStruct((rows, unit), BF16)] * pieces,
        in_specs=[in_hbm] * 2,
        out_specs=[in_vmem] * pieces,
        scratch_shapes=[
            pltpu.VMEM((pieces, rows, unit), BF16),
            pltpu.VMEM((pieces, rows, unit), BF16),
            pltpu.SemaphoreType.DMA((2, pieces)),
        ],
        compiler_params=limit,
    )(far(key_gate), far(value))
    if pieces > 1:
        spread = swap(signal)
    else:
        in_order = signal[0].reshape(rows, seq_count, width).transpose(1, 0, 2)
        in_order = lax.all_to_all(in_order, "seq", 0, 0, tiled=True)
        spread = list(jnp.pad(in_order, [(0, 0), (0, 0), (0, LANES - width)]))

    my_filter = lax.dynamic_slice_in_dim(out_filter, seq_index * width, width, 1)
    decay = decay_rate.reshape(seq_count, width)
    if pieces == 1:
        pad = [(0, 0), (0, LANES - width)]
        my_filter = jnp.pad(my_filter, pad)
        decay = jnp.pad(lax.dynamic_slice_in_dim(decay, seq_index, 1), pad)
    out_width = out_weight.shape[1] // chan_count
    quarter = chan_count // 4
    odd = range(1, chan_count, 2)
    far_odd, near_odd = [j for j in odd if j & 2], [j for j in odd if not j & 2]
    blocks_kept, blocks_last = [j ^ 1 for j in far_odd], [j ^ 1 for j in near_odd]
    smalls = (
        features, emb_weight, emb_bias[None, :], mid_weight, mid_bias[None, :], decay, head_tail,
    )
    real, imag, edge, weights_away = pl.pallas_call(
        functools.partial(filter_kernel, block, far_odd, pieces > 1),
        out_shape=(
            jax.ShapeDtypeStruct((blocks, block, LANES), F32),
            jax.ShapeDtypeStruct((blocks, block, LANES), F32),
            jax.ShapeDtypeStruct((blocks, 16, LANES), F32),
            jax.ShapeDtypeStruct((quarter, chan_width, out_width), BF16),
        ),
        in_specs=[in_vmem] + [in_hbm] * 8,
        out_specs=[in_vmem] * 4,
        scratch_shapes=[
            *[pltpu.VMEM(small.shape, small.dtype) for small in smalls],
            pltpu.VMEM((feat_rows, order), F32),
            pltpu.VMEM((order + 8, order), F32),
            pltpu.VMEM((order + 8, length), F32),
            pltpu.VMEM((length + block, LANES), BF16),
            pltpu.SemaphoreType.DMA((len(smalls),)),
            pltpu.SemaphoreType.DMA((quarter,)),
        ],
        compiler_params=limit,
    )(my_filter, *map(far, (*smalls, out_weight)))

    *convolved, weights_kept = pl.pallas_call(
        functools.partial(conv_kernel, block, blocks_kept, arrival, pieces > 1),
        out_shape=[
            *[jax.ShapeDtypeStruct((rows, LANES), BF16)] * seq_count,
            jax.ShapeDtypeStruct((quarter, chan_width, out_width), BF16),
        ],
        in_specs=[in_smem] + [in_vmem] * 5 + [in_hbm] + [in_vmem] * seq_count,
        out_specs=[in_vmem] * (seq_count + 1),
        scratch_shapes=[
            pltpu.VMEM((length, LANES), BF16),
            pltpu.VMEM((blocks, block, LANES), F32),
            pltpu.VMEM((blocks, block, LANES), F32),
            pltpu.VMEM((2 * block, blocks * LANES), BF16),
            pltpu.VMEM((length, LANES), BF16),
            pltpu.SemaphoreType.DMA((quarter,)),
        ],
        compiler_params=limit,
    )(group_order, real, imag, edge, head, inverse, far(out_weight), *[spread[k] for k in arrival])
    weights_next, query_near, skip = pl.pallas_call(
        functools.partial(copy_kernel, near_odd),
        out_shape=(
            jax.ShapeDtypeStruct((quarter, chan_width, out_width), BF16),
            jax.ShapeDtypeStruct((pieces, rows, unit), BF16),
            jax.ShapeDtypeStruct((pieces, rows, unit), F32),
        ),
        in_specs=[in_vmem] * 2 + [in_hbm] * 2 + [in_vmem] * pieces,
        out_specs=[in_vmem] * 3,
        scratch_shapes=[pltpu.SemaphoreType.DMA((quarter,)), pltpu.SemaphoreType.DMA((pieces,))],
        compiler_params=limit,
    )(convolved[0], skip_gain[None, :], far(out_weight), far(query), *signal)
    if pieces > 1:
        backs = swap(convolved)
    else:
        in_order = lax.all_to_all(jnp.stack([piece[:, :width] for piece in convolved]), "seq", 0, 0, tiled=True)
        backs = [in_order.transpose(1, 0, 2).reshape(rows, chan_width)]

    def exchange(terms, bit):
        return lax.ppermute(terms, "chan", [(d, d ^ bit) for d in range(chan_count)])

    far_away, mixed = pl.pallas_call(
        functools.partial(mix_kernel, arrival if pieces > 1 else [0]),
        out_shape=(
            jax.ShapeDtypeStruct((quarter, rows, out_width), BF16),
            jax.ShapeDtypeStruct((rows, chan_width), BF16),
        ),
        in_specs=[in_vmem] * (3 + pieces),
        out_specs=[in_vmem] * 2,
        compiler_params=limit,
    )(query_near, skip, weights_away, *[backs[k] for k in (arrival if pieces > 1 else [0])])
    far_terms = exchange(far_away, 1)

    def products(first, weights, dtype):
        return pl.pallas_call(
            functools.partial(project_kernel, first),
            out_shape=jax.ShapeDtypeStruct((quarter, rows, out_width), dtype),
            in_specs=[in_vmem] * 2,
            out_specs=in_vmem,
            compiler_params=limit,
        )(mixed, weights)

    far_kept, near_away = products(0, weights_kept, F32), products(0, weights_next, BF16)
    spans = [(0, out_width // 2), (out_width // 2, out_width)]
    send = [(far_kept[:, :, a:b] + far_terms[:, :, a:b].astype(F32)).astype(BF16) for a, b in spans]
    send, near_away, mixed = lax.optimization_barrier((send, near_away, mixed))
    sent = [exchange(piece, 2) for piece in send]
    near_terms = exchange(near_away, 1)
    near_kept = pl.pallas_call(
        functools.partial(last_kernel, blocks_last),
        out_shape=jax.ShapeDtypeStruct((quarter, rows, out_width), F32),
        in_specs=[in_vmem, in_hbm],
        out_specs=in_vmem,
        scratch_shapes=[
            pltpu.VMEM((quarter, chan_width, out_width), BF16),
            pltpu.SemaphoreType.DMA((quarter,)),
        ],
        compiler_params=limit,
    )(mixed, far(out_weight))
    terms = [near_kept, near_terms]
    bit = 4
    while bit < chan_count:
        total = sum(term.astype(F32) for term in (*terms, jnp.concatenate(sent, 2)))
        terms, sent, spans = [total[0::2]], [exchange(total[1::2].astype(BF16), bit)], [(0, out_width)]
        bit *= 2
    result = []
    for span, piece in zip(spans, sent):
        operands = [*[term[0] for term in terms], piece[0]]
        result = [
            pl.pallas_call(
                functools.partial(finish_kernel, span, len(terms)),
                out_shape=jax.ShapeDtypeStruct((out_width, rows), F32),
                in_specs=[in_vmem] * len(operands) + [in_hbm] * len(result),
                out_specs=in_hbm,
                scratch_shapes=[
                    pltpu.VMEM((span[1] - span[0], rows), F32),
                    pltpu.SemaphoreType.DMA((max(1, (span[1] - span[0]) // LANES),)),
                ],
                input_output_aliases={len(operands): 0} if result else {},
                compiler_params=limit,
            )(*operands, *result)
        ]
    return result[0]


def solution(mesh):
    return jax.shard_map(
        local,
        mesh=mesh,
        in_specs=(
            P("seq", "chan"), P("seq", "chan"), P("seq", "chan"), P(), P(), P(), P(), P(), P(None, "chan"), P("chan"),
            P("chan"), P("chan", None),
        ),
        out_specs=P("chan", "seq"),
        check_vma=False,
    )
```
